32 devices in a mesh: fsdp: 8 (over y, x, core), seq: 4 (over z).
Axes of the slice: x: 2, y: 2, z: 4, core: 2. Of those that a mesh axis runs over, the one named last changes fastest.
Arguments:
- tokens: bfloat16 [16, 2048, 768], P('fsdp', 'seq'), may hold values from -6 to 6
- teacher: bfloat16 [16, 2048, 768], P('fsdp', 'seq'), may hold values from -6 to 6
- segment_ids: int32 [16, 2048], P('fsdp', 'seq'), may hold values from 0 to 3, as said below
- latent_flags: int32 [16, 2048], P('fsdp', 'seq'), may hold values from 0 to 1, as said below
- valid_mask: int32 [16, 2048], P('fsdp', 'seq'), may hold values from 0 to 1, as said below
- attngain: bfloat16 [768], P('fsdp'), may hold values from 0.5 to 1.5
- attnshift: bfloat16 [768], P('fsdp'), may hold values from -4 to 4
- qkvweight: bfloat16 [768, 2304], P('fsdp'), may hold values from -0.3125 to 0.3125
- qvbias: bfloat16 [1536], P('fsdp'), may hold values from -4 to 4
- outweight: bfloat16 [768, 768], P('fsdp'), may hold values from -0.875 to 0.875
- outbias: bfloat16 [768], P('fsdp'), may hold values from -4 to 4
- mlpgain: bfloat16 [768], P('fsdp'), may hold values from 0.5 to 1.5
- mlpshift: bfloat16 [768], P('fsdp'), may hold values from -4 to 4
- fcweight: bfloat16 [768, 3072], P('fsdp'), may hold values from -0.21875 to 0.21875
- fcbias: bfloat16 [3072], P('fsdp'), may hold values from -6 to 6
- projweight: bfloat16 [3072, 768], P('fsdp'), may hold values from -0.109375 to 0.109375
- projbias: bfloat16 [768], P('fsdp'), may hold values from -4 to 4
Outputs:
- distill_loss: float32 [], replicated
- layer_out: bfloat16 [16, 2048, 768], P('fsdp', 'seq')
- grad_tokens: bfloat16 [16, 2048, 768], P('fsdp', 'seq')
- grad_attngain: float32 [768], P('fsdp')
- grad_attnshift: float32 [768], P('fsdp')
- grad_qkvweight: float32 [768, 2304], P('fsdp')
- grad_qvbias: float32 [1536], P('fsdp')
- grad_outweight: float32 [768, 768], P('fsdp')
- grad_outbias: float32 [768], P('fsdp')
- grad_mlpgain: float32 [768], P('fsdp')
- grad_mlpshift: float32 [768], P('fsdp')
- grad_fcweight: float32 [768, 3072], P('fsdp')
- grad_fcbias: float32 [3072], P('fsdp')
- grad_projweight: float32 [3072, 768], P('fsdp')
- grad_projbias: float32 [768], P('fsdp')
The draws below stay inside these ranges and needn't reach their ends.
Inputs may be any that keep to these rules, and one draw needn't show every extreme that they name: `segment_ids`: ids never fall along a sequence, start at 0, and every sequence holds four documents. `latent_flags`: the first token of every sequence is not latent. `valid_mask`: the first token of every sequence is valid.
All inputs are finite; a program needn't handle non-finite values.
Results may differ from the reference program's by a relative error of at most 0.012.
The reference program's roundings to bfloat16 on the way count: a program that leaves them out, or rounds other values in their place, can miss the bound.
Values may be sent and summed in bfloat16 or wider, within the bound.
No kernel may reach another device: no remote copies, remote signals or barrier semaphores. Data moves between devices by JAX's collectives and lax.ppermute only.
A program may use at most 256 MiB of HBM per device.

```python
import math
import jax
import jax.numpy as jnp
from jax import lax

D = 768
H = 12
HD = 64
FF = 3072
LEN = 2048
SEQS = 16
TOKENS = 32768


def draw_segment_ids(key, part):
    base = jax.random.fold_in(key, 11)
    jitter = jax.random.randint(base, (SEQS, 3), -(LEN // 16), LEN // 16 + 1, dtype=jnp.int32)
    bounds = (jnp.arange(1, 4, dtype=jnp.int32) * (LEN // 4))[None, :] + jitter
    place = jnp.arange(LEN, dtype=jnp.int32)
    return jnp.sum((place[None, :, None] >= bounds[:, None, :]).astype(jnp.int32), -1).astype(jnp.int32)


def draw_latent_flags(key, part):
    base = jax.random.fold_in(key, 17)
    drawn = jax.random.randint(base, (SEQS, LEN), 0, 4, dtype=jnp.int32)
    place = jnp.arange(LEN, dtype=jnp.int32)[None, :]
    return jnp.where((drawn == 0) & (place != 0), 1, 0).astype(jnp.int32)


def draw_valid_mask(key, part):
    base = jax.random.fold_in(key, 23)
    order = jnp.arange(SEQS, dtype=jnp.int32)[:, None] * LEN + jnp.arange(LEN, dtype=jnp.int32)[None, :]
    limit = 256 + 512 * order // (SEQS * LEN)
    drawn = jax.random.randint(base, (SEQS, LEN), 0, 1024, dtype=jnp.int32)
    place = jnp.arange(LEN, dtype=jnp.int32)[None, :]
    return jnp.where((place == 0) | (drawn < limit), 1, 0).astype(jnp.int32)


def block_levels(own_key, dims, cuts, smallest, largest):
    level, own = 1.0, jax.random.fold_in(own_key, 6)
    for position, blocks in cuts:
        steps = jnp.exp(jax.random.uniform(jax.random.fold_in(own, position), (blocks,), jnp.float32, smallest / len(cuts), largest / len(cuts)))
        level = level * jnp.repeat(steps, dims[position] // blocks).reshape([-1 if axis == position else 1 for axis in range(len(dims))])
    return level


def scatter_about(own_key, dims, width, most, cuts=(), kind=jnp.bfloat16):
    values = jax.random.normal(own_key, dims, jnp.float32) * width
    if len(cuts) > 0:
        values = block_levels(own_key, dims, cuts, -0.22, 0.18) * values
    return jnp.clip(values, min=-most, max=most).astype(kind)


def setup_inputs(seed: int = 0) -> dict:
    seeds = jax.random.split(jax.random.key(seed), 18)
    return {
        "tokens": scatter_about(seeds[0], (SEQS, LEN, D), 1.0, 6.0, ((0, 8), (1, 4))),
        "teacher": scatter_about(seeds[1], (SEQS, LEN, D), 1.0, 6.0, ((0, 8), (1, 4))),
        "segment_ids": draw_segment_ids(jax.random.fold_in(seeds[17], 71), 0),
        "latent_flags": draw_latent_flags(jax.random.fold_in(seeds[17], 71), 0),
        "valid_mask": draw_valid_mask(jax.random.fold_in(seeds[17], 71), 0),
        "attngain": jnp.clip(1.0 + 0.1 * jax.random.normal(seeds[5], (D,), jnp.float32), 0.5, 1.5).astype(jnp.bfloat16),
        "attnshift": scatter_about(seeds[6], (D,), 0.3, 4.0, ((0, 8),)),
        "qkvweight": scatter_about(seeds[7], (D, 3 * D), (D // 2) ** -0.5, 0.3125, ((0, 8),)),
        "qvbias": scatter_about(seeds[8], (2 * D,), 0.3, 4.0, ((0, 8),)),
        "outweight": scatter_about(seeds[9], (D, D), (D // 16) ** -0.5, 0.875, ((0, 8),)),
        "outbias": scatter_about(seeds[10], (D,), 0.3, 4.0, ((0, 8),)),
        "mlpgain": jnp.clip(1.0 + 0.1 * jax.random.normal(seeds[11], (D,), jnp.float32), 0.5, 1.5).astype(jnp.bfloat16),
        "mlpshift": scatter_about(seeds[12], (D,), 0.3, 4.0, ((0, 8),)),
        "fcweight": scatter_about(seeds[13], (D, FF), D ** -0.5, 0.21875, ((0, 8),)),
        "fcbias": scatter_about(seeds[14], (FF,), 0.5, 6.0, ((0, 8),)),
        "projweight": scatter_about(seeds[15], (FF, D), FF ** -0.5, 0.109375, ((0, 8),)),
        "projbias": scatter_about(seeds[16], (D,), 0.3, 4.0, ((0, 8),)),
    }


EPSILON = 1e-05
PRECISE = lax.Precision.HIGHEST

@jax.custom_vjp
def low(v):
    return lax.optimization_barrier(v.astype(jnp.bfloat16)).astype(jnp.float32)

@jax.custom_vjp
def low_back(v):
    return v

def low_keep(v):
    return (low(v), None)

def low_pass(kept, grad):
    return (grad,)

def back_keep(v):
    return (v, None)

def back_low(kept, grad):
    return (low(grad),)
low.defvjp(low_keep, low_pass)
low_back.defvjp(back_keep, back_low)

def layer_norm(values, gain, shift):
    center = values - lax.optimization_barrier(jnp.mean(values, -1, keepdims=True))
    spread = lax.optimization_barrier(jnp.mean(center * center, -1, keepdims=True))
    return center * lax.rsqrt(spread + EPSILON) * gain + shift

def gelu_tanh(values):
    inner = 0.7978845608028654 * (values + 0.044715 * values * values * values)
    return 0.5 * values * (1.0 + jnp.tanh(inner))

def product(left, right):
    return jnp.dot(left, right, precision=PRECISE, preferred_element_type=jnp.float32)

def attend_one(item):
    joint_seq, segment_seq = item
    query = joint_seq[:, 0]
    keys = joint_seq[:, 1]
    values = joint_seq[:, 2]
    scale = 1.0 / math.sqrt(HD)
    scores = low_back(scale * jnp.einsum('qhd,khd->hqk', query, keys, precision=PRECISE))
    place = jnp.arange(LEN, dtype=jnp.int32)
    allowed = (place[None, :] <= place[:, None]) & (segment_seq[:, None] == segment_seq[None, :])
    masked = jnp.where(allowed[None], scores, -1e+30)
    highest = lax.optimization_barrier(jnp.max(masked, -1, keepdims=True))
    powers = jnp.exp(masked - highest)
    probs = powers / lax.optimization_barrier(jnp.sum(powers, -1, keepdims=True))
    mixed = jnp.einsum('hqk,khd->qhd', low(probs), values, precision=PRECISE)
    return mixed.reshape(LEN, H * HD)

def forward(inputs, params, segment_ids):
    attngain, attnshift, qkvweight, qvbias, outweight, outbias, mlpgain, mlpshift, fcweight, fcbias, projweight, projbias = params
    flat_rows = inputs.reshape(-1, D)
    normed = low(layer_norm(flat_rows, attngain, attnshift))
    bias_full = jnp.concatenate([qvbias[:D], jnp.zeros((D,), jnp.float32), qvbias[D:]])
    joint = low(low_back(product(normed, qkvweight) + bias_full))
    joint = joint.reshape(SEQS, LEN, 3, H, HD)
    attended = lax.map(jax.checkpoint(attend_one), (joint, segment_ids))
    attended = low(low_back(attended)).reshape(-1, D)
    branch = low_back(product(attended, outweight) + outbias)
    resid = flat_rows + branch
    normed_two = low(layer_norm(resid, mlpgain, mlpshift))
    hidden = low_back(product(normed_two, fcweight) + fcbias)
    active = low(gelu_tanh(hidden))
    mlp_out = low_back(product(active, projweight) + projbias)
    return (resid + mlp_out).reshape(SEQS, LEN, D)

def reference(tokens, teacher, segment_ids, latent_flags, valid_mask, attngain, attnshift, qkvweight, qvbias, outweight, outbias, mlpgain, mlpshift, fcweight, fcbias, projweight, projbias):
    params = tuple((p.astype(jnp.float32) for p in (attngain, attnshift, qkvweight, qvbias, outweight, outbias, mlpgain, mlpshift, fcweight, fcbias, projweight, projbias)))
    inputs = tokens.astype(jnp.float32)

    def apply_block(values, weights):
        return forward(values, weights, segment_ids)
    result, pullback = jax.vjp(apply_block, inputs, params)
    weight = (valid_mask * (1 - latent_flags)).astype(jnp.float32)
    error = result - teacher.astype(jnp.float32)
    count = jnp.sum(weight)
    distill_loss = jnp.sum(weight * lax.optimization_barrier(jnp.sum(error * error, -1))) / (D * count)
    factor = TOKENS / count
    cotangent = error * (weight * factor)[..., None]
    grad_inputs, grads = pullback(cotangent)
    return (distill_loss, result.astype(jnp.bfloat16), grad_inputs.astype(jnp.bfloat16), grads[0], grads[1], grads[2], grads[3], grads[4], grads[5], grads[6], grads[7], grads[8], grads[9], grads[10], grads[11])
```

```python
import functools

import jax
import jax.numpy as jnp
from jax import lax
from jax.experimental import pallas as pl
from jax.experimental.pallas import tpu as pltpu
from jax.sharding import PartitionSpec as P

H = 12
HD = 64
PAIR = 2 * HD
EPSILON = 1e-05
KEY_TILE = 128
QUERY_TILE = 256
ROW_TILE = 256
HALO_CHUNK = 128
VMEM_LIMIT = 62 * 1024 * 1024

NT = (((1,), (1,)), ((), ()))
NN = (((1,), (0,)), ((), ()))
TN = (((0,), (0,)), ((), ()))
F32 = jnp.float32
BF16 = jnp.bfloat16


def dot(left, right, dims=NN):
    return lax.dot_general(left, right, dims, preferred_element_type=F32)


def norm_parts(values):
    center = values - jnp.mean(values, -1, keepdims=True)
    spread = jnp.mean(center * center, -1, keepdims=True)
    scale = lax.rsqrt(spread + EPSILON)
    return center * scale, scale


def norm_back(grad, gain, unit, scale):
    weighted = grad * gain
    first = jnp.mean(weighted, -1, keepdims=True)
    second = jnp.mean(weighted * unit, -1, keepdims=True)
    return scale * (weighted - first - unit * second)


def piece_copies(order_ref, pieces, whole_ref, sems):
    copies = []
    for place, piece in enumerate(pieces):
        rows = piece.shape[0]
        if len(pieces) == 1:
            target = whole_ref
        else:
            target = whole_ref.at[pl.ds(pl.multiple_of(order_ref[place] * rows, 16), rows), :]
        copies.append(pltpu.make_async_copy(piece, target, sems.at[place]))
    return copies


def project_kernel(
    halo_tiles, count, low_ref, order_ref, halo_ref, own_ref, gain_ref, shift_ref, bias_ref, *rest
):
    pieces = rest[:count]
    normed_ref, query_ref, key_ref, value_ref, weight_ref, sems = rest[count:]
    seq, tile = pl.program_id(0), pl.program_id(1)
    width = own_ref.shape[-1]

    @pl.when((seq == 0) & (tile == 0))
    def _():
        copies = piece_copies(order_ref, pieces, weight_ref, sems)
        for copy in copies:
            copy.start()
        for copy in copies:
            copy.wait()

    def keys_values(rows):
        unit, _ = norm_parts(rows.astype(F32))
        normed = (unit * gain_ref[...] + shift_ref[...]).astype(BF16)
        normed_ref[0] = normed
        key_ref[0] = dot(normed, weight_ref[:, width : 2 * width]).astype(BF16)
        value_ref[0] = (
            dot(normed, weight_ref[:, 2 * width :]) + bias_ref[:, width:]
        ).astype(BF16)

    @pl.when((tile >= low_ref[seq]) & (tile < halo_tiles))
    def _():
        keys_values(halo_ref[0])

    @pl.when(tile >= halo_tiles)
    def _():
        keys_values(own_ref[0])
        query_ref[0] = (
            dot(normed_ref[0], weight_ref[:, :width]) + bias_ref[:, :width]
        ).astype(BF16)


def project(low, order, halo, own, gain, shift, bias, pieces):
    seqs, block, width = own.shape
    halo_tiles = halo.shape[1] // ROW_TILE
    own_tiles = block // ROW_TILE
    length = halo.shape[1] + block
    spot = lambda s, t, low, order: (s, jnp.maximum(t, low[s]), 0)
    in_halo = lambda s, t, low, order: (
        s,
        jnp.minimum(jnp.maximum(t, low[s]), halo_tiles - 1),
        0,
    )
    in_own = lambda s, t, low, order: (s, jnp.maximum(t - halo_tiles, 0), 0)
    fixed = lambda s, t, low, order: (0, 0)
    tile = (1, ROW_TILE, width)
    return pl.pallas_call(
        functools.partial(project_kernel, halo_tiles, len(pieces)),
        grid_spec=pltpu.PrefetchScalarGridSpec(
            num_scalar_prefetch=2,
            grid=(seqs, halo_tiles + own_tiles),
            in_specs=[
                pl.BlockSpec(tile, in_halo),
                pl.BlockSpec(tile, in_own),
                pl.BlockSpec((1, width), fixed),
                pl.BlockSpec((1, width), fixed),
                pl.BlockSpec((1, 2 * width), fixed),
            ]
            + [pl.BlockSpec(memory_space=pl.ANY)] * len(pieces),
            out_specs=[
                pl.BlockSpec(tile, spot),
                pl.BlockSpec(tile, in_own),
                pl.BlockSpec(tile, spot),
                pl.BlockSpec(tile, spot),
            ],
            scratch_shapes=[
                pltpu.VMEM((width, 3 * width), BF16),
                pltpu.SemaphoreType.DMA((len(pieces),)),
            ],
        ),
        out_shape=[
            jax.ShapeDtypeStruct((seqs, length, width), BF16),
            jax.ShapeDtypeStruct((seqs, block, width), BF16),
            jax.ShapeDtypeStruct((seqs, length, width), BF16),
            jax.ShapeDtypeStruct((seqs, length, width), BF16),
        ],
        compiler_params=pltpu.CompilerParams(vmem_limit_bytes=VMEM_LIMIT),
        cost_estimate=pl.CostEstimate(
            flops=10 * seqs * block * width * width, bytes_accessed=24 << 20, transcendentals=0
        ),
        name="project",
    )(low, order, halo, own, gain, shift, bias, *pieces)


def two_heads(tile):
    left = lax.broadcasted_iota(jnp.int32, tile.shape, 1) < HD
    zero = jnp.zeros_like(tile)
    return jnp.concatenate([jnp.where(left, tile, zero), jnp.where(left, zero, tile)], 0)


def visible(first_key, starts, first_query):
    shape = (KEY_TILE, starts.shape[1])
    keys = first_key + lax.broadcasted_iota(jnp.int32, shape, 0)
    queries = first_query + lax.broadcasted_iota(jnp.int32, shape, 1)
    return (keys >= starts) & (keys <= queries)


def attend_kernel(halo, low_ref, query_ref, key_ref, value_ref, start_ref, out_ref, log_ref):
    seq = pl.program_id(0)
    block = query_ref.shape[1]
    tiles = block // QUERY_TILE
    for tile in range(tiles):
        here = slice(tile * QUERY_TILE, (tile + 1) * QUERY_TILE)
        query = query_ref[0, here, :] * 0.125
        starts = start_ref[0, :, here]

        def step(j, carry):
            high0, high1, total0, total1, mixed = carry
            place = pl.ds(pl.multiple_of(j * KEY_TILE, KEY_TILE), KEY_TILE)
            scores = dot(two_heads(key_ref[0, place, :]), query, NT)
            ok = visible(j * KEY_TILE, starts, halo + tile * QUERY_TILE)
            scores0 = jnp.where(ok, scores[:KEY_TILE], -1e30)
            scores1 = jnp.where(ok, scores[KEY_TILE:], -1e30)
            next0 = jnp.maximum(high0, jnp.max(scores0, 0, keepdims=True))
            next1 = jnp.maximum(high1, jnp.max(scores1, 0, keepdims=True))
            powers0 = jnp.exp(scores0 - next0)
            powers1 = jnp.exp(scores1 - next1)
            fade0 = jnp.exp(high0 - next0)
            fade1 = jnp.exp(high1 - next1)
            total0 = total0 * fade0 + jnp.sum(powers0, 0, keepdims=True)
            total1 = total1 * fade1 + jnp.sum(powers1, 0, keepdims=True)
            powers = jnp.concatenate([powers0.astype(BF16), powers1.astype(BF16)], 0)
            added = dot(two_heads(value_ref[0, place, :]), powers, TN)
            fade = jnp.concatenate(
                [
                    jnp.broadcast_to(fade0, (HD, QUERY_TILE)),
                    jnp.broadcast_to(fade1, (HD, QUERY_TILE)),
                ],
                0,
            )
            return next0, next1, total0, total1, mixed * fade + added

        row = jnp.zeros((1, QUERY_TILE), F32)
        high0, high1, total0, total1, mixed = lax.fori_loop(
            low_ref[seq * tiles + tile],
            (halo + (tile + 1) * QUERY_TILE) // KEY_TILE,
            step,
            (row - 1e30, row - 1e30, row, row, jnp.zeros((PAIR, QUERY_TILE), F32)),
        )
        total = jnp.concatenate(
            [
                jnp.broadcast_to(total0, (HD, QUERY_TILE)),
                jnp.broadcast_to(total1, (HD, QUERY_TILE)),
            ],
            0,
        )
        out_ref[0, here, :] = jnp.transpose(mixed / total).astype(BF16)
        log_ref[0, 0, 0:1, here] = high0 + jnp.log(total0)
        log_ref[0, 0, 1:2, here] = high1 + jnp.log(total1)


def attend(low, query, keys, values, starts):
    seqs, block, width = query.shape
    length = keys.shape[1]
    pairs = width // PAIR
    rows = pl.BlockSpec((1, block, PAIR), lambda s, p, low: (s, 0, p))
    full = pl.BlockSpec((1, length, PAIR), lambda s, p, low: (s, 0, p))
    return pl.pallas_call(
        functools.partial(attend_kernel, length - block),
        grid_spec=pltpu.PrefetchScalarGridSpec(
            num_scalar_prefetch=1,
            grid=(seqs, pairs),
            in_specs=[rows, full, full, pl.BlockSpec((1, 1, block), lambda s, p, low: (s, 0, 0))],
            out_specs=[rows, pl.BlockSpec((1, 1, 2, block), lambda s, p, low: (s, p, 0, 0))],
        ),
        out_shape=[
            jax.ShapeDtypeStruct((seqs, block, width), BF16),
            jax.ShapeDtypeStruct((seqs, pairs, 2, block), F32),
        ],
        compiler_params=pltpu.CompilerParams(vmem_limit_bytes=VMEM_LIMIT),
        cost_estimate=pl.CostEstimate(
            flops=16 << 30, bytes_accessed=16 << 20, transcendentals=8 << 20
        ),
        name="attend",
    )(low, query, keys, values, starts)


def attend_back_kernel(
    halo,
    low_ref,
    first_ref,
    query_ref,
    key_ref,
    value_ref,
    start_ref,
    out_ref,
    grad_ref,
    log_ref,
    gquery_ref,
    gkey_ref,
    gvalue_ref,
    turned_ref,
    center_ref,
    sumk_ref,
    sumv_ref,
):
    seq = pl.program_id(0)
    block = query_ref.shape[1]
    tiles = block // QUERY_TILE
    turned_ref[...] = jnp.zeros_like(turned_ref)
    products = jnp.transpose(grad_ref[0].astype(F32) * out_ref[0].astype(F32))
    center_ref[0:1, :] = jnp.sum(products[:HD], 0, keepdims=True)
    center_ref[1:2, :] = jnp.sum(products[HD:], 0, keepdims=True)
    left = lax.broadcasted_iota(jnp.int32, (KEY_TILE, PAIR), 1) < HD

    def step(j, nothing):
        place = pl.ds(pl.multiple_of(j * KEY_TILE, KEY_TILE), KEY_TILE)
        keys = two_heads(key_ref[0, place, :])
        values = two_heads(value_ref[0, place, :])
        sumk_ref[...] = jnp.zeros_like(sumk_ref)
        sumv_ref[...] = jnp.zeros_like(sumv_ref)
        for tile in range(tiles):
            here = slice(tile * QUERY_TILE, (tile + 1) * QUERY_TILE)
            last = (halo + (tile + 1) * QUERY_TILE) // KEY_TILE

            @pl.when((j >= low_ref[seq * tiles + tile]) & (j < last))
            def _():
                query = query_ref[0, here, :] * 0.125
                grad = grad_ref[0, here, :]
                scores = dot(keys, query, NT)
                gprobs = dot(values, grad, NT)
                ok = visible(j * KEY_TILE, start_ref[0, :, here], halo + tile * QUERY_TILE)
                probs, gscores = [], []
                for head in range(2):
                    part = slice(head * KEY_TILE, (head + 1) * KEY_TILE)
                    masked = jnp.where(ok, scores[part] - log_ref[0, 0, head : head + 1, here], -1e30)
                    prob = jnp.exp(masked)
                    gscore = prob * (gprobs[part] - center_ref[head : head + 1, here])
                    probs.append(prob.astype(BF16))
                    gscores.append(gscore.astype(BF16))
                probs = jnp.concatenate(probs, 0)
                gscores = jnp.concatenate(gscores, 0)
                sumv_ref[...] += dot(probs, grad)
                sumk_ref[...] += dot(gscores, query)
                turned_ref[:, here] += dot(keys, gscores, TN)

        gkey_ref[0, place, :] = jnp.where(left, sumk_ref[:KEY_TILE], sumk_ref[KEY_TILE:]).astype(BF16)
        gvalue_ref[0, place, :] = jnp.where(left, sumv_ref[:KEY_TILE], sumv_ref[KEY_TILE:]).astype(BF16)
        return nothing

    lax.fori_loop(first_ref[seq], (halo + block) // KEY_TILE, step, 0)
    gquery_ref[0] = (jnp.transpose(turned_ref[...]) * 0.125).astype(BF16)


def attend_back(low, first, query, keys, values, starts, mixed, grad, logs):
    seqs, block, width = query.shape
    length = keys.shape[1]
    pairs = width // PAIR
    rows = pl.BlockSpec((1, block, PAIR), lambda s, p, low, first: (s, 0, p))
    full = pl.BlockSpec((1, length, PAIR), lambda s, p, low, first: (s, 0, p))
    return pl.pallas_call(
        functools.partial(attend_back_kernel, length - block),
        grid_spec=pltpu.PrefetchScalarGridSpec(
            num_scalar_prefetch=2,
            grid=(seqs, pairs),
            in_specs=[
                rows,
                full,
                full,
                pl.BlockSpec((1, 1, block), lambda s, p, low, first: (s, 0, 0)),
                rows,
                rows,
                pl.BlockSpec((1, 1, 2, block), lambda s, p, low, first: (s, p, 0, 0)),
            ],
            out_specs=[rows, full, full],
            scratch_shapes=[
                pltpu.VMEM((PAIR, block), F32),
                pltpu.VMEM((8, block), F32),
                pltpu.VMEM((2 * KEY_TILE, PAIR), F32),
                pltpu.VMEM((2 * KEY_TILE, PAIR), F32),
            ],
        ),
        out_shape=[
            jax.ShapeDtypeStruct((seqs, block, width), BF16),
            jax.ShapeDtypeStruct((seqs, length, width), BF16),
            jax.ShapeDtypeStruct((seqs, length, width), BF16),
        ],
        compiler_params=pltpu.CompilerParams(vmem_limit_bytes=VMEM_LIMIT),
        cost_estimate=pl.CostEstimate(
            flops=40 << 30, bytes_accessed=28 << 20, transcendentals=8 << 20
        ),
        name="attend_back",
    )(low, first, query, keys, values, starts, mixed, grad, logs)


def mlp_kernel(
    counts,
    order_ref,
    factor_ref,
    mixed_ref,
    token_ref,
    teacher_ref,
    weight_ref,
    outbias_ref,
    gain_ref,
    shift_ref,
    upbias_ref,
    downbias_ref,
    *rest,
):
    out_pieces = rest[: counts[0]]
    up_pieces = rest[counts[0] : counts[0] + counts[1]]
    down_pieces = rest[counts[0] + counts[1] : sum(counts)]
    (
        layer_ref,
        gresid_ref,
        gmixed_ref,
        normed_ref,
        active_ref,
        ghidden_ref,
        gmlp_ref,
        gbranch_ref,
        sums_ref,
        upsums_ref,
        merge_ref,
        up_ref,
        down_ref,
        slope_ref,
        resid_ref,
        total_ref,
        sems,
    ) = rest[sum(counts) :]
    width = token_ref.shape[-1]
    chunks = active_ref.shape[-1] // width
    step = pl.program_id(0)
    copies = [
        piece_copies(order_ref, pieces, whole, sems.at[k])
        for k, (pieces, whole) in enumerate(
            ((out_pieces, merge_ref), (up_pieces, up_ref), (down_pieces, down_ref))
        )
    ]

    def arrive(k):
        @pl.when(step == 0)
        def _():
            for copy in copies[k]:
                copy.wait()

    @pl.when(step == 0)
    def _():
        for group in copies:
            for copy in group:
                copy.start()
        sums_ref[...] = jnp.zeros_like(sums_ref)
        upsums_ref[...] = jnp.zeros_like(upsums_ref)

    arrive(0)
    resid = (
        token_ref[...].astype(F32) + dot(mixed_ref[...], merge_ref[...]) + outbias_ref[...]
    )
    unit, scale = norm_parts(resid)
    normed_ref[...] = (unit * gain_ref[...] + shift_ref[...]).astype(BF16)
    resid_ref[...] = resid
    arrive(1)
    arrive(2)
    total_ref[...] = resid + downbias_ref[...]

    def forward(c, nothing):
        cols = pl.ds(pl.multiple_of(c * width, 128), width)
        hidden = dot(normed_ref[...], up_ref[:, cols]) + upbias_ref[:, cols]
        square = hidden * hidden
        curve = jnp.tanh(0.7978845608028654 * (hidden + 0.044715 * square * hidden))
        half = 0.5 * (1.0 + curve)
        active = (half * hidden).astype(BF16)
        active_ref[:, cols] = active
        slope_ref[:, cols] = half + 0.5 * hidden * (1.0 - curve * curve) * (
            0.7978845608028654 * (1.0 + 3.0 * 0.044715 * square)
        )
        total_ref[...] += dot(active, down_ref[cols, :])
        return nothing

    lax.fori_loop(0, chunks, forward, 0)
    result = total_ref[...]
    layer_ref[...] = result.astype(BF16)
    error = result - teacher_ref[...].astype(F32)
    weight = weight_ref[...]
    sums_ref[4:5, :] += jnp.sum(weight * (error * error), 0, keepdims=True)
    gresult = error * (weight * factor_ref[0])
    gmlp = gresult.astype(BF16)
    gmlp_ref[...] = gmlp
    gresid_ref[...] = gresult
    sums_ref[3:4, :] += jnp.sum(gmlp.astype(F32), 0, keepdims=True)
    total_ref[...] = jnp.zeros_like(total_ref)

    def backward(c, nothing):
        cols = pl.ds(pl.multiple_of(c * width, 128), width)
        gactive = dot(gmlp_ref[...], down_ref[cols, :], NT)
        ghidden = (gactive * slope_ref[:, cols]).astype(BF16)
        ghidden_ref[:, cols] = ghidden
        upsums_ref[0:1, cols] += jnp.sum(ghidden.astype(F32), 0, keepdims=True)
        total_ref[...] += dot(ghidden, up_ref[:, cols], NT)
        return nothing

    lax.fori_loop(0, chunks, backward, 0)
    gnormed = total_ref[...]
    unit, scale = norm_parts(resid_ref[...])
    sums_ref[1:2, :] += jnp.sum(gnormed * unit, 0, keepdims=True)
    sums_ref[2:3, :] += jnp.sum(gnormed, 0, keepdims=True)
    gresid = gresid_ref[...] + norm_back(gnormed, gain_ref[...], unit, scale)
    gresid_ref[...] = gresid
    gbranch = gresid.astype(BF16)
    gbranch_ref[...] = gbranch
    sums_ref[0:1, :] += jnp.sum(gbranch.astype(F32), 0, keepdims=True)
    gmixed_ref[...] = dot(gbranch, merge_ref[...], NT).astype(BF16)


def mlp(order, factor, mixed, tokens, teacher, weight, vectors, out_pieces, up_pieces, down_pieces):
    rows, width = tokens.shape
    outbias, gain, shift, upbias, downbias = vectors
    hidden = upbias.shape[1]
    tile = lambda n: pl.BlockSpec((ROW_TILE, n), lambda i, order: (i, 0))
    fixed = lambda m, n: pl.BlockSpec((m, n), lambda i, order: (0, 0))
    pieces = [*out_pieces, *up_pieces, *down_pieces]
    counts = (len(out_pieces), len(up_pieces), len(down_pieces))
    shape = jax.ShapeDtypeStruct
    return pl.pallas_call(
        functools.partial(mlp_kernel, counts),
        grid_spec=pltpu.PrefetchScalarGridSpec(
            num_scalar_prefetch=1,
            grid=(rows // ROW_TILE,),
            in_specs=[
                pl.BlockSpec(memory_space=pltpu.SMEM),
                tile(width),
                tile(width),
                tile(width),
                tile(1),
                fixed(1, width),
                fixed(1, width),
                fixed(1, width),
                fixed(1, hidden),
                fixed(1, width),
            ]
            + [pl.BlockSpec(memory_space=pl.ANY)] * len(pieces),
            out_specs=[
                tile(width),
                tile(width),
                tile(width),
                tile(width),
                tile(hidden),
                tile(hidden),
                tile(width),
                tile(width),
                fixed(8, width),
                fixed(8, hidden),
            ],
            scratch_shapes=[
                pltpu.VMEM((width, width), BF16),
                pltpu.VMEM((width, hidden), BF16),
                pltpu.VMEM((hidden, width), BF16),
                pltpu.VMEM((ROW_TILE, hidden), F32),
                pltpu.VMEM((ROW_TILE, width), F32),
                pltpu.VMEM((ROW_TILE, width), F32),
                pltpu.SemaphoreType.DMA((3, max(counts))),
            ],
        ),
        out_shape=[
            shape((rows, width), BF16),
            shape((rows, width), F32),
            shape((rows, width), BF16),
            shape((rows, width), BF16),
            shape((rows, hidden), BF16),
            shape((rows, hidden), BF16),
            shape((rows, width), BF16),
            shape((rows, width), BF16),
            shape((8, width), F32),
            shape((8, hidden), F32),
        ],
        compiler_params=pltpu.CompilerParams(vmem_limit_bytes=VMEM_LIMIT),
        cost_estimate=pl.CostEstimate(
            flops=4 * rows * width * (width + 2 * hidden),
            bytes_accessed=40 << 20,
            transcendentals=rows * hidden,
        ),
        name="mlp",
    )(
        order,
        factor,
        mixed,
        tokens,
        teacher,
        weight,
        outbias,
        gain,
        shift,
        upbias,
        downbias,
        *pieces,
    )


def halo_back_kernel(
    count, low_ref, order_ref, halo_ref, gkey_ref, gvalue_ref, *rest
):
    pieces = rest[:count]
    out_ref, sums_ref, weight_ref, sems = rest[count:]
    seq, tile = pl.program_id(0), pl.program_id(1)
    width = halo_ref.shape[-1]

    @pl.when((seq == 0) & (tile == 0))
    def _():
        copies = piece_copies(order_ref, pieces, weight_ref, sems)
        for copy in copies:
            copy.start()
        for copy in copies:
            copy.wait()
        sums_ref[...] = jnp.zeros_like(sums_ref)

    @pl.when(tile < low_ref[seq])
    def _():
        out_ref[...] = jnp.zeros_like(out_ref)

    @pl.when(tile >= low_ref[seq])
    def _():
        grad = dot(gkey_ref[0], weight_ref[:, width : 2 * width], NT)
        grad += dot(gvalue_ref[0], weight_ref[:, 2 * width :], NT)
        unit, _ = norm_parts(halo_ref[0].astype(F32))
        out_ref[0] = grad.astype(BF16)
        sums_ref[0:1, :] += jnp.sum(grad * unit, 0, keepdims=True)
        sums_ref[1:2, :] += jnp.sum(grad, 0, keepdims=True)


def halo_back(low, order, halo, gkeys, gvalues, pieces):
    seqs, rows, width = halo.shape
    halo_tiles = rows // ROW_TILE
    tile = (1, ROW_TILE, width)
    spot = lambda s, t, low, order: (s, jnp.minimum(jnp.maximum(t, low[s]), halo_tiles - 1), 0)
    plain = lambda s, t, low, order: (s, t, 0)
    return pl.pallas_call(
        functools.partial(halo_back_kernel, len(pieces)),
        grid_spec=pltpu.PrefetchScalarGridSpec(
            num_scalar_prefetch=2,
            grid=(seqs, halo_tiles),
            in_specs=[pl.BlockSpec(tile, spot)] * 3
            + [pl.BlockSpec(memory_space=pl.ANY)] * len(pieces),
            out_specs=[
                pl.BlockSpec(tile, plain),
                pl.BlockSpec((8, width), lambda s, t, low, order: (0, 0)),
            ],
            scratch_shapes=[
                pltpu.VMEM((width, 3 * width), BF16),
                pltpu.SemaphoreType.DMA((len(pieces),)),
            ],
        ),
        out_shape=[
            jax.ShapeDtypeStruct((seqs, rows, width), BF16),
            jax.ShapeDtypeStruct((8, width), F32),
        ],
        compiler_params=pltpu.CompilerParams(vmem_limit_bytes=VMEM_LIMIT),
        cost_estimate=pl.CostEstimate(
            flops=4 << 30, bytes_accessed=16 << 20, transcendentals=0
        ),
        name="halo_back",
    )(low, order, halo, gkeys, gvalues, *pieces)


def own_back_kernel(
    halo_tiles,
    count,
    low_ref,
    order_ref,
    own_ref,
    normed_ref,
    gquery_ref,
    gkey_ref,
    gvalue_ref,
    *rest,
):
    pieces = rest[:count]
    gnormed_ref, gweight_ref, sums_ref, weight_ref, total_ref, sems = rest[count:]
    seq, tile = pl.program_id(0), pl.program_id(1)
    width = own_ref.shape[-1]
    own = tile >= halo_tiles
    copies = piece_copies(order_ref, pieces, weight_ref, sems)

    @pl.when((seq == 0) & (tile == 0))
    def _():
        for copy in copies:
            copy.start()
        sums_ref[...] = jnp.zeros_like(sums_ref)
        total_ref[...] = jnp.zeros_like(total_ref)
        for copy in copies:
            copy.wait()

    def gather(index, grad_ref):
        cols = slice(index * width, (index + 1) * width)
        total_ref[:, cols] += dot(normed_ref[0], grad_ref[0], TN)

    @pl.when(tile >= low_ref[seq])
    def _():
        gather(1, gkey_ref)
        gather(2, gvalue_ref)
        sums_ref[3:4, :] += jnp.sum(gvalue_ref[0].astype(F32), 0, keepdims=True)

    @pl.when(own)
    def _():
        gather(0, gquery_ref)
        sums_ref[2:3, :] += jnp.sum(gquery_ref[0].astype(F32), 0, keepdims=True)
        grad = dot(gquery_ref[0], weight_ref[:, :width], NT)
        grad += dot(gkey_ref[0], weight_ref[:, width : 2 * width], NT)
        grad += dot(gvalue_ref[0], weight_ref[:, 2 * width :], NT)
        gnormed_ref[0] = grad
        unit, _ = norm_parts(own_ref[0].astype(F32))
        sums_ref[0:1, :] += jnp.sum(grad * unit, 0, keepdims=True)
        sums_ref[1:2, :] += jnp.sum(grad, 0, keepdims=True)

    @pl.when((seq == pl.num_programs(0) - 1) & (tile == pl.num_programs(1) - 1))
    def _():
        gweight_ref[...] = total_ref[...].astype(BF16)


def own_back(low, order, own, normed, gquery, gkeys, gvalues, pieces):
    seqs, block, width = own.shape
    length = normed.shape[1]
    halo_tiles = (length - block) // ROW_TILE
    own_tiles = block // ROW_TILE
    tile = (1, ROW_TILE, width)
    spot = lambda s, t, low, order: (s, jnp.maximum(t, low[s]), 0)
    in_own = lambda s, t, low, order: (s, jnp.maximum(t - halo_tiles, 0), 0)
    fixed = lambda s, t, low, order: (0, 0)
    return pl.pallas_call(
        functools.partial(own_back_kernel, halo_tiles, len(pieces)),
        grid_spec=pltpu.PrefetchScalarGridSpec(
            num_scalar_prefetch=2,
            grid=(seqs, halo_tiles + own_tiles),
            in_specs=[
                pl.BlockSpec(tile, in_own),
                pl.BlockSpec(tile, spot),
                pl.BlockSpec(tile, in_own),
                pl.BlockSpec(tile, spot),
                pl.BlockSpec(tile, spot),
            ]
            + [pl.BlockSpec(memory_space=pl.ANY)] * len(pieces),
            out_specs=[
                pl.BlockSpec(tile, in_own),
                pl.BlockSpec((width, 3 * width), fixed),
                pl.BlockSpec((8, width), fixed),
            ],
            scratch_shapes=[
                pltpu.VMEM((width, 3 * width), BF16),
                pltpu.VMEM((width, 3 * width), F32),
                pltpu.SemaphoreType.DMA((len(pieces),)),
            ],
        ),
        out_shape=[
            jax.ShapeDtypeStruct((seqs, block, width), F32),
            jax.ShapeDtypeStruct((width, 3 * width), BF16),
            jax.ShapeDtypeStruct((8, width), F32),
        ],
        compiler_params=pltpu.CompilerParams(vmem_limit_bytes=VMEM_LIMIT),
        cost_estimate=pl.CostEstimate(
            flops=16 << 30, bytes_accessed=24 << 20, transcendentals=0
        ),
        name="own_back",
    )(low, order, own, normed, gquery, gkeys, gvalues, *pieces)


def finish_kernel(own_ref, gnormed_ref, more_ref, gresid_ref, gain_ref, out_ref):
    unit, scale = norm_parts(own_ref[...].astype(F32))
    grad = gnormed_ref[...] + more_ref[...].astype(F32)
    out_ref[...] = (gresid_ref[...] + norm_back(grad, gain_ref[...], unit, scale)).astype(BF16)


def finish(own, gnormed, more, gresid, gain):
    rows, width = own.shape
    tile = pl.BlockSpec((ROW_TILE, width), lambda i: (i, 0))
    return pl.pallas_call(
        finish_kernel,
        grid=(rows // ROW_TILE,),
        in_specs=[tile, tile, tile, tile, pl.BlockSpec((1, width), lambda i: (0, 0))],
        out_specs=tile,
        out_shape=jax.ShapeDtypeStruct((rows, width), BF16),
        cost_estimate=pl.CostEstimate(
            flops=20 * rows * width, bytes_accessed=14 * rows * width, transcendentals=0
        ),
        name="finish",
    )(own, gnormed, more, gresid, gain)


def swap(x, axis, bit):
    size = lax.axis_size(axis)
    return lax.ppermute(x, axis, [(i, i ^ bit) for i in range(size)])


def shift(x, axis, step):
    size = lax.axis_size(axis)
    return lax.ppermute(
        x, axis, [(i, i + step) for i in range(size) if 0 <= i + step < size]
    )


def sum_over(x, axis):
    bit = 1
    while bit < lax.axis_size(axis):
        x = x + swap(x, axis, bit)
        bit *= 2
    return x


def max_over(x, axis):
    bit = 1
    while bit < lax.axis_size(axis):
        x = jnp.maximum(x, swap(x, axis, bit))
        bit *= 2
    return x


def gather_pieces(shard):
    size = lax.axis_size("fsdp")
    if size != 8:
        return [lax.all_gather(shard, "fsdp", axis=0, tiled=True)]
    near = [shard] + [swap(shard, "fsdp", 2 * d) for d in range(1, size // 2)]
    return near + [swap(piece, "fsdp", 1) for piece in near]


def piece_order():
    size = lax.axis_size("fsdp")
    me = lax.axis_index("fsdp").astype(jnp.int32)
    if size != 8:
        return jnp.zeros((1,), jnp.int32)
    return jnp.stack(
        [me ^ (2 * d) for d in range(size // 2)] + [me ^ (2 * d) ^ 1 for d in range(size // 2)]
    )


def reduce_rows(parts):
    size = lax.axis_size("fsdp")
    me = lax.axis_index("fsdp")
    rows, columns = parts.shape[1:]
    if size != 8:
        total = lax.psum_scatter(parts, "fsdp", scatter_dimension=0, tiled=False)
        return lax.psum(total, "seq").astype(F32)
    pairs = parts.reshape(size // 2, 2, rows, columns)
    core = me % 2
    chip = me // 2
    pick = lambda a, k, ax: lax.dynamic_index_in_dim(a, k, ax, keepdims=False)
    other = swap(pick(pairs, 1 - core, 1), "fsdp", 1)
    mine = (pick(pairs, core, 1).astype(F32) + other.astype(F32)).astype(BF16)
    arrived = [
        swap(pick(mine, chip ^ d, 0), "fsdp", 2 * d) for d in range(1, size // 2)
    ]
    total = pick(mine, chip, 0).astype(F32)
    for part in arrived:
        total = total + part.astype(F32)
    total = total.astype(BF16)
    groups = lax.axis_size("seq")
    place = lax.axis_index("seq")
    if groups == 4:
        halves = total.reshape(2, rows // 2, columns)
        odd = place % 2
        half = pick(halves, odd, 0).astype(F32) + swap(pick(halves, 1 - odd, 0), "seq", 1).astype(F32)
        half = half.astype(BF16)
        half = (half.astype(F32) + swap(half, "seq", 2).astype(F32)).astype(BF16)
        back = swap(half, "seq", 1)
        return jnp.where(
            odd == 0,
            jnp.concatenate([half, back], 0),
            jnp.concatenate([back, half], 0),
        ).astype(F32)
    return lax.psum(total, "seq").astype(F32)


def local(
    tokens,
    teacher,
    segment_ids,
    latent_flags,
    valid_mask,
    attngain,
    attnshift,
    qkvweight,
    qvbias,
    outweight,
    outbias,
    mlpgain,
    mlpshift,
    fcweight,
    fcbias,
    projweight,
    projbias,
):
    seqs, block, width = tokens.shape
    groups = lax.axis_size("seq")
    owners = lax.axis_size("fsdp")
    rows = seqs * block
    halo_rows = (groups - 1) * block
    far_rows = halo_rows - block
    me = lax.axis_index("fsdp")
    place = lax.axis_index("seq").astype(jnp.int32)
    hidden = fcweight.shape[1]

    near = shift(tokens, "seq", 1)

    shards = [attngain, attnshift, qvbias, outbias, mlpgain, mlpshift, fcbias, projbias]
    packed = jnp.concatenate(shards)
    table = jnp.where(
        lax.broadcasted_iota(jnp.int32, (owners, packed.shape[0]), 0) == me,
        packed[None],
        jnp.zeros((), BF16),
    )
    if owners == 8:
        table = sum_over(table, "fsdp")
    else:
        table = lax.psum(table, "fsdp")
    vectors = []
    at = 0
    for shard in shards:
        size = shard.shape[0]
        vectors.append(table[:, at : at + size].reshape(1, size * owners).astype(F32))
        at += size
    gain1, shift1, bias1, outbias_v, gain2, shift2, upbias, downbias = vectors

    order = piece_order()
    qkv_pieces = gather_pieces(qkvweight)
    out_pieces = gather_pieces(outweight)
    up_pieces = gather_pieces(fcweight)
    down_pieces = gather_pieces(projweight)

    weight = (valid_mask * (1 - latent_flags)).astype(F32)
    below = jnp.sum(
        (segment_ids[:, :, None] < jnp.arange(1, 4, dtype=jnp.int32)).astype(jnp.int32), 1
    )
    facts = jnp.concatenate([below.reshape(-1), jnp.sum(weight).astype(jnp.int32)[None]])
    facts = sum_over(facts, "seq")
    bounds = facts[:-1].reshape(seqs, 3)

    def start_of(positions):
        found = jnp.zeros((seqs,) + positions.shape, jnp.int32)
        for d in range(3):
            bound = bounds[:, d].reshape((seqs,) + (1,) * positions.ndim)
            found = jnp.maximum(found, jnp.where(bound <= positions[None], bound, 0))
        return found

    firsts = jnp.arange(groups, dtype=jnp.int32) * block
    reach = jnp.max(firsts[None] - start_of(firsts)) - block
    chunks = jnp.maximum(reach + HALO_CHUNK - 1, 0) // HALO_CHUNK
    chunks = max_over(chunks[None], "fsdp")[0]
    count = sum_over(facts[-1:], "fsdp")[0].astype(F32)
    base = (place - (groups - 1)) * block
    starts = start_of(place * block + jnp.arange(block, dtype=jnp.int32)) - base
    low_rows = starts[:, ::QUERY_TILE]
    low = (low_rows // KEY_TILE).reshape(-1)
    low_tile = starts[:, 0] // ROW_TILE
    first = low_tile * (ROW_TILE // KEY_TILE)
    starts = starts[:, None, :]

    halo = jnp.concatenate([jnp.zeros((seqs, far_rows, width), BF16), near], 1)

    def fetch(state):
        j, halo = state
        sent = lax.dynamic_slice_in_dim(halo, halo_rows - HALO_CHUNK * (j + 1), HALO_CHUNK, 1)
        came = shift(sent, "seq", 1)
        return j + 1, lax.dynamic_update_slice_in_dim(
            halo, came, far_rows - HALO_CHUNK * (j + 1), 1
        )

    if far_rows > 0:
        _, halo = lax.while_loop(lambda state: state[0] < chunks, fetch, (jnp.int32(0), halo))

    normed, query, keys, values = project(
        low_tile, order, halo, tokens, gain1, shift1, bias1, qkv_pieces
    )
    mixed, logs = attend(low, query, keys, values, starts)

    factor = (rows * owners * groups) / count
    (
        layer_out,
        gresid,
        gmixed,
        normed2,
        active,
        ghidden,
        gmlp,
        gbranch,
        sums,
        upsums,
    ) = mlp(
        order,
        factor.reshape(1),
        mixed.reshape(rows, width),
        tokens.reshape(rows, width),
        teacher.reshape(rows, width),
        weight.reshape(rows, 1),
        (outbias_v, gain2, shift2, upbias, downbias),
        out_pieces,
        up_pieces,
        down_pieces,
    )

    def outer(left, right):
        return lax.dot_general(left, right, TN, preferred_element_type=F32).astype(BF16)

    grad_down = reduce_rows(outer(active, gmlp).reshape(owners, hidden // owners, width))
    grad_up = reduce_rows(outer(normed2, ghidden).reshape(owners, width // owners, hidden))
    grad_merge = reduce_rows(
        outer(mixed.reshape(rows, width), gbranch).reshape(owners, width // owners, width)
    )
    small = jnp.concatenate([sums[:4].reshape(-1), upsums[0], jnp.sum(sums[4:5], 1)])
    small = sum_over(sum_over(small, "seq"), "fsdp")

    gquery, gkeys, gvalues = attend_back(
        low, first, query, keys, values, starts, mixed, gmixed.reshape(seqs, block, width), logs
    )
    ghalo, halo_sums = halo_back(low_tile, order, halo, gkeys, gvalues, qkv_pieces)

    def give(state):
        j, ghalo = state
        j = j - 1
        sent = lax.dynamic_slice_in_dim(ghalo, far_rows - HALO_CHUNK * (j + 1), HALO_CHUNK, 1)
        came = shift(sent, "seq", -1)
        spot = halo_rows - HALO_CHUNK * (j + 1)
        held = lax.dynamic_slice_in_dim(ghalo, spot, HALO_CHUNK, 1)
        total = (held.astype(F32) + came.astype(F32)).astype(BF16)
        return j, lax.dynamic_update_slice_in_dim(ghalo, total, spot, 1)

    if far_rows > 0:
        _, ghalo = lax.while_loop(lambda state: state[0] > 0, give, (chunks, ghalo))
    more = shift(ghalo[:, far_rows:], "seq", -1)

    gnormed, gweight, own_sums = own_back(
        low_tile, order, tokens, normed, gquery, gkeys, gvalues, qkv_pieces
    )
    late = jnp.concatenate([(own_sums[:2] + halo_sums[:2]).reshape(-1), own_sums[2:4].reshape(-1)])
    late = sum_over(sum_over(late, "seq"), "fsdp")
    grad_joint = reduce_rows(gweight.reshape(owners, width // owners, 3 * width))

    grad_tokens = finish(
        tokens.reshape(rows, width),
        gnormed.reshape(rows, width),
        more.reshape(rows, width),
        gresid,
        gain1,
    ).reshape(tokens.shape)

    def own_part(vector, at, size):
        share = size // owners
        return lax.dynamic_slice_in_dim(vector, at + me * share, share)

    loss = small[-1] / (width * count)
    return (
        loss,
        layer_out.reshape(tokens.shape),
        grad_tokens,
        own_part(late, 0, width),
        own_part(late, width, width),
        grad_joint,
        own_part(late, 2 * width, 2 * width),
        grad_merge,
        own_part(small, 0, width),
        own_part(small, width, width),
        own_part(small, 2 * width, width),
        grad_up,
        own_part(small, 4 * width, hidden),
        grad_down,
        own_part(small, 3 * width, width),
    )


def solution(mesh):
    placed = (
        P("fsdp", "seq", None),
        P("fsdp", "seq", None),
        P("fsdp", "seq"),
        P("fsdp", "seq"),
        P("fsdp", "seq"),
        P("fsdp"),
        P("fsdp"),
        P("fsdp", None),
        P("fsdp"),
        P("fsdp", None),
        P("fsdp"),
        P("fsdp"),
        P("fsdp"),
        P("fsdp", None),
        P("fsdp"),
        P("fsdp", None),
        P("fsdp"),
    )
    return jax.shard_map(
        local,
        mesh=mesh,
        in_specs=placed,
        out_specs=(
            P(),
            P("fsdp", "seq", None),
            P("fsdp", "seq", None),
            P("fsdp"),
            P("fsdp"),
            P("fsdp", None),
            P("fsdp"),
            P("fsdp", None),
            P("fsdp"),
            P("fsdp"),
            P("fsdp"),
            P("fsdp", None),
            P("fsdp"),
            P("fsdp", None),
            P("fsdp"),
        ),
        check_vma=False,
    )
```

```python
import functools

import jax
import jax.numpy as jnp
from jax import lax
from jax.experimental import pallas as pl
from jax.experimental.pallas import tpu as pltpu
from jax.sharding import PartitionSpec as P

H = 12
HD = 64
PAIR = 2 * HD
EPSILON = 1e-05
KEY_TILE = 128
QUERY_TILE = 256
ROW_TILE = 256
HALO_CHUNK = 128
SHARES = 8
VMEM_LIMIT = 62 * 1024 * 1024

NT = (((1,), (1,)), ((), ()))
NN = (((1,), (0,)), ((), ()))
TN = (((0,), (0,)), ((), ()))
F32 = jnp.float32
BF16 = jnp.bfloat16


def dot(left, right, dims=NN):
    return lax.dot_general(left, right, dims, preferred_element_type=F32)


def norm_parts(values):
    center = values - jnp.mean(values, -1, keepdims=True)
    spread = jnp.mean(center * center, -1, keepdims=True)
    scale = lax.rsqrt(spread + EPSILON)
    return center * scale, scale


def norm_back(grad, gain, unit, scale):
    weighted = grad * gain
    first = jnp.mean(weighted, -1, keepdims=True)
    second = jnp.mean(weighted * unit, -1, keepdims=True)
    return scale * (weighted - first - unit * second)


def piece_copies(order_ref, pieces, whole_ref, sems):
    copies = []
    for place, piece in enumerate(pieces):
        rows = piece.shape[0]
        if len(pieces) == 1:
            target = whole_ref
        else:
            target = whole_ref.at[pl.ds(pl.multiple_of(order_ref[place] * rows, 16), rows), :]
        copies.append(pltpu.make_async_copy(piece, target, sems.at[place]))
    return copies


def project_kernel(
    halo_tiles, count, low_ref, order_ref, halo_ref, own_ref, gain_ref, shift_ref, bias_ref, *rest
):
    pieces = rest[:count]
    normed_ref, query_ref, key_ref, value_ref, weight_ref, sems = rest[count:]
    seq, tile = pl.program_id(0), pl.program_id(1)
    width = own_ref.shape[-1]

    @pl.when((seq == 0) & (tile == 0))
    def _():
        copies = piece_copies(order_ref, pieces, weight_ref, sems)
        for copy in copies:
            copy.start()
        for copy in copies:
            copy.wait()

    def keys_values(rows):
        unit, _ = norm_parts(rows.astype(F32))
        normed = (unit * gain_ref[...] + shift_ref[...]).astype(BF16)
        normed_ref[0] = normed
        key_ref[0] = dot(normed, weight_ref[:, width : 2 * width]).astype(BF16)
        value_ref[0] = (
            dot(normed, weight_ref[:, 2 * width :]) + bias_ref[:, width:]
        ).astype(BF16)

    @pl.when((tile >= low_ref[seq]) & (tile < halo_tiles))
    def _():
        keys_values(halo_ref[0])

    @pl.when(tile >= halo_tiles)
    def _():
        keys_values(own_ref[0])
        query_ref[0] = (
            dot(normed_ref[0], weight_ref[:, :width]) + bias_ref[:, :width]
        ).astype(BF16)


def project(low, order, halo, own, gain, shift, bias, pieces):
    seqs, block, width = own.shape
    halo_tiles = halo.shape[1] // ROW_TILE
    own_tiles = block // ROW_TILE
    length = halo.shape[1] + block
    spot = lambda s, t, low, order: (s, jnp.maximum(t, low[s]), 0)
    in_halo = lambda s, t, low, order: (
        s,
        jnp.minimum(jnp.maximum(t, low[s]), halo_tiles - 1),
        0,
    )
    in_own = lambda s, t, low, order: (s, jnp.maximum(t - halo_tiles, 0), 0)
    fixed = lambda s, t, low, order: (0, 0)
    tile = (1, ROW_TILE, width)
    return pl.pallas_call(
        functools.partial(project_kernel, halo_tiles, len(pieces)),
        grid_spec=pltpu.PrefetchScalarGridSpec(
            num_scalar_prefetch=2,
            grid=(seqs, halo_tiles + own_tiles),
            in_specs=[
                pl.BlockSpec(tile, in_halo),
                pl.BlockSpec(tile, in_own),
                pl.BlockSpec((1, width), fixed),
                pl.BlockSpec((1, width), fixed),
                pl.BlockSpec((1, 2 * width), fixed),
            ]
            + [pl.BlockSpec(memory_space=pl.ANY)] * len(pieces),
            out_specs=[
                pl.BlockSpec(tile, spot),
                pl.BlockSpec(tile, in_own),
                pl.BlockSpec(tile, spot),
                pl.BlockSpec(tile, spot),
            ],
            scratch_shapes=[
                pltpu.VMEM((width, 3 * width), BF16),
                pltpu.SemaphoreType.DMA((len(pieces),)),
            ],
        ),
        out_shape=[
            jax.ShapeDtypeStruct((seqs, length, width), BF16),
            jax.ShapeDtypeStruct((seqs, block, width), BF16),
            jax.ShapeDtypeStruct((seqs, length, width), BF16),
            jax.ShapeDtypeStruct((seqs, length, width), BF16),
        ],
        compiler_params=pltpu.CompilerParams(vmem_limit_bytes=VMEM_LIMIT),
        cost_estimate=pl.CostEstimate(
            flops=10 * seqs * block * width * width, bytes_accessed=24 << 20, transcendentals=0
        ),
        name="project",
    )(low, order, halo, own, gain, shift, bias, *pieces)


def two_heads(tile):
    left = lax.broadcasted_iota(jnp.int32, tile.shape, 1) < HD
    zero = jnp.zeros_like(tile)
    return jnp.concatenate([jnp.where(left, tile, zero), jnp.where(left, zero, tile)], 0)


def visible(first_key, starts, first_query):
    shape = (KEY_TILE, starts.shape[1])
    keys = first_key + lax.broadcasted_iota(jnp.int32, shape, 0)
    queries = first_query + lax.broadcasted_iota(jnp.int32, shape, 1)
    return (keys >= starts) & (keys <= queries)


def attend_kernel(halo, low_ref, query_ref, key_ref, value_ref, start_ref, out_ref, log_ref):
    seq = pl.program_id(0)
    block = query_ref.shape[1]
    tiles = block // QUERY_TILE
    for tile in range(tiles):
        here = slice(tile * QUERY_TILE, (tile + 1) * QUERY_TILE)
        query = query_ref[0, here, :] * 0.125
        starts = start_ref[0, :, here]

        def step(j, carry):
            high0, high1, total0, total1, mixed = carry
            place = pl.ds(pl.multiple_of(j * KEY_TILE, KEY_TILE), KEY_TILE)
            scores = dot(two_heads(key_ref[0, place, :]), query, NT)
            ok = visible(j * KEY_TILE, starts, halo + tile * QUERY_TILE)
            scores0 = jnp.where(ok, scores[:KEY_TILE], -1e30)
            scores1 = jnp.where(ok, scores[KEY_TILE:], -1e30)
            next0 = jnp.maximum(high0, jnp.max(scores0, 0, keepdims=True))
            next1 = jnp.maximum(high1, jnp.max(scores1, 0, keepdims=True))
            powers0 = jnp.exp(scores0 - next0)
            powers1 = jnp.exp(scores1 - next1)
            fade0 = jnp.exp(high0 - next0)
            fade1 = jnp.exp(high1 - next1)
            total0 = total0 * fade0 + jnp.sum(powers0, 0, keepdims=True)
            total1 = total1 * fade1 + jnp.sum(powers1, 0, keepdims=True)
            powers = jnp.concatenate([powers0.astype(BF16), powers1.astype(BF16)], 0)
            added = dot(two_heads(value_ref[0, place, :]), powers, TN)
            fade = jnp.concatenate(
                [
                    jnp.broadcast_to(fade0, (HD, QUERY_TILE)),
                    jnp.broadcast_to(fade1, (HD, QUERY_TILE)),
                ],
                0,
            )
            return next0, next1, total0, total1, mixed * fade + added

        row = jnp.zeros((1, QUERY_TILE), F32)
        high0, high1, total0, total1, mixed = lax.fori_loop(
            low_ref[seq * tiles + tile],
            (halo + (tile + 1) * QUERY_TILE) // KEY_TILE,
            step,
            (row - 1e30, row - 1e30, row, row, jnp.zeros((PAIR, QUERY_TILE), F32)),
        )
        total = jnp.concatenate(
            [
                jnp.broadcast_to(total0, (HD, QUERY_TILE)),
                jnp.broadcast_to(total1, (HD, QUERY_TILE)),
            ],
            0,
        )
        out_ref[0, here, :] = jnp.transpose(mixed / total).astype(BF16)
        log_ref[0, 0, 0:1, here] = high0 + jnp.log(total0)
        log_ref[0, 0, 1:2, here] = high1 + jnp.log(total1)


def attend(low, query, keys, values, starts):
    seqs, block, width = query.shape
    length = keys.shape[1]
    pairs = width // PAIR
    rows = pl.BlockSpec((1, block, PAIR), lambda s, p, low: (s, 0, p))
    full = pl.BlockSpec((1, length, PAIR), lambda s, p, low: (s, 0, p))
    return pl.pallas_call(
        functools.partial(attend_kernel, length - block),
        grid_spec=pltpu.PrefetchScalarGridSpec(
            num_scalar_prefetch=1,
            grid=(seqs, pairs),
            in_specs=[rows, full, full, pl.BlockSpec((1, 1, block), lambda s, p, low: (s, 0, 0))],
            out_specs=[rows, pl.BlockSpec((1, 1, 2, block), lambda s, p, low: (s, p, 0, 0))],
        ),
        out_shape=[
            jax.ShapeDtypeStruct((seqs, block, width), BF16),
            jax.ShapeDtypeStruct((seqs, pairs, 2, block), F32),
        ],
        compiler_params=pltpu.CompilerParams(vmem_limit_bytes=VMEM_LIMIT),
        cost_estimate=pl.CostEstimate(
            flops=16 << 30, bytes_accessed=16 << 20, transcendentals=8 << 20
        ),
        name="attend",
    )(low, query, keys, values, starts)


def attend_back_kernel(
    halo,
    low_ref,
    first_ref,
    query_ref,
    key_ref,
    value_ref,
    start_ref,
    out_ref,
    grad_ref,
    log_ref,
    gquery_ref,
    gkey_ref,
    gvalue_ref,
    turned_ref,
    center_ref,
    sumk_ref,
    sumv_ref,
):
    seq = pl.program_id(0)
    block = query_ref.shape[1]
    tiles = block // QUERY_TILE
    turned_ref[...] = jnp.zeros_like(turned_ref)
    products = jnp.transpose(grad_ref[0].astype(F32) * out_ref[0].astype(F32))
    center_ref[0:1, :] = jnp.sum(products[:HD], 0, keepdims=True)
    center_ref[1:2, :] = jnp.sum(products[HD:], 0, keepdims=True)
    left = lax.broadcasted_iota(jnp.int32, (KEY_TILE, PAIR), 1) < HD

    def step(j, nothing):
        place = pl.ds(pl.multiple_of(j * KEY_TILE, KEY_TILE), KEY_TILE)
        keys = two_heads(key_ref[0, place, :])
        values = two_heads(value_ref[0, place, :])
        sumk_ref[...] = jnp.zeros_like(sumk_ref)
        sumv_ref[...] = jnp.zeros_like(sumv_ref)
        for tile in range(tiles):
            here = slice(tile * QUERY_TILE, (tile + 1) * QUERY_TILE)
            last = (halo + (tile + 1) * QUERY_TILE) // KEY_TILE

            @pl.when((j >= low_ref[seq * tiles + tile]) & (j < last))
            def _():
                query = query_ref[0, here, :] * 0.125
                grad = grad_ref[0, here, :]
                scores = dot(keys, query, NT)
                gprobs = dot(values, grad, NT)
                ok = visible(j * KEY_TILE, start_ref[0, :, here], halo + tile * QUERY_TILE)
                probs, gscores = [], []
                for head in range(2):
                    part = slice(head * KEY_TILE, (head + 1) * KEY_TILE)
                    masked = jnp.where(ok, scores[part] - log_ref[0, 0, head : head + 1, here], -1e30)
                    prob = jnp.exp(masked)
                    gscore = prob * (gprobs[part] - center_ref[head : head + 1, here])
                    probs.append(prob.astype(BF16))
                    gscores.append(gscore.astype(BF16))
                probs = jnp.concatenate(probs, 0)
                gscores = jnp.concatenate(gscores, 0)
                sumv_ref[...] += dot(probs, grad)
                sumk_ref[...] += dot(gscores, query)
                turned_ref[:, here] += dot(keys, gscores, TN)

        gkey_ref[0, place, :] = jnp.where(left, sumk_ref[:KEY_TILE], sumk_ref[KEY_TILE:]).astype(BF16)
        gvalue_ref[0, place, :] = jnp.where(left, sumv_ref[:KEY_TILE], sumv_ref[KEY_TILE:]).astype(BF16)
        return nothing

    lax.fori_loop(first_ref[seq], (halo + block) // KEY_TILE, step, 0)
    gquery_ref[0] = (jnp.transpose(turned_ref[...]) * 0.125).astype(BF16)


def attend_back(low, first, query, keys, values, starts, mixed, grad, logs):
    seqs, block, width = query.shape
    length = keys.shape[1]
    pairs = width // PAIR
    rows = pl.BlockSpec((1, block, PAIR), lambda s, p, low, first: (s, 0, p))
    full = pl.BlockSpec((1, length, PAIR), lambda s, p, low, first: (s, 0, p))
    return pl.pallas_call(
        functools.partial(attend_back_kernel, length - block),
        grid_spec=pltpu.PrefetchScalarGridSpec(
            num_scalar_prefetch=2,
            grid=(seqs, pairs),
            in_specs=[
                rows,
                full,
                full,
                pl.BlockSpec((1, 1, block), lambda s, p, low, first: (s, 0, 0)),
                rows,
                rows,
                pl.BlockSpec((1, 1, 2, block), lambda s, p, low, first: (s, p, 0, 0)),
            ],
            out_specs=[rows, full, full],
            scratch_shapes=[
                pltpu.VMEM((PAIR, block), F32),
                pltpu.VMEM((8, block), F32),
                pltpu.VMEM((2 * KEY_TILE, PAIR), F32),
                pltpu.VMEM((2 * KEY_TILE, PAIR), F32),
            ],
        ),
        out_shape=[
            jax.ShapeDtypeStruct((seqs, block, width), BF16),
            jax.ShapeDtypeStruct((seqs, length, width), BF16),
            jax.ShapeDtypeStruct((seqs, length, width), BF16),
        ],
        compiler_params=pltpu.CompilerParams(vmem_limit_bytes=VMEM_LIMIT),
        cost_estimate=pl.CostEstimate(
            flops=40 << 30, bytes_accessed=28 << 20, transcendentals=8 << 20
        ),
        name="attend_back",
    )(low, first, query, keys, values, starts, mixed, grad, logs)


def slab_copies(slab_ref, merge_ref, up_ref, down_ref, sems):
    owners = slab_ref.shape[0]
    width = slab_ref.shape[2]
    rows = width // owners
    chunks = up_ref.shape[1] // width
    groups = [[], [], []]
    for owner in range(owners):
        here = pl.ds(owner * rows, rows)
        groups[0].append((slab_ref.at[owner, pl.ds(0, rows), :], merge_ref.at[here, :]))
        for c in range(chunks):
            groups[1].append(
                (
                    slab_ref.at[owner, pl.ds((1 + c) * rows, rows), :],
                    up_ref.at[here, pl.ds(c * width, width)],
                )
            )
        groups[2].append(
            (
                slab_ref.at[owner, pl.ds((1 + chunks) * rows, chunks * rows), :],
                down_ref.at[pl.ds(owner * chunks * rows, chunks * rows), :],
            )
        )
    return [
        [pltpu.make_async_copy(*pair, sems.at[k, n]) for n, pair in enumerate(group)]
        for k, group in enumerate(groups)
    ]


def mlp_kernel(
    factor_ref,
    mixed_ref,
    token_ref,
    teacher_ref,
    weight_ref,
    outbias_ref,
    gain_ref,
    shift_ref,
    upbias_ref,
    downbias_ref,
    slab_ref,
    layer_ref,
    gresid_ref,
    gmixed_ref,
    normed_ref,
    active_ref,
    ghidden_ref,
    gmlp_ref,
    gbranch_ref,
    sums_ref,
    upsums_ref,
    merge_ref,
    up_ref,
    down_ref,
    slope_ref,
    resid_ref,
    total_ref,
    sems,
):
    width = token_ref.shape[-1]
    chunks = active_ref.shape[-1] // width
    step = pl.program_id(0)
    copies = slab_copies(slab_ref, merge_ref, up_ref, down_ref, sems)

    def arrive(k):
        @pl.when(step == 0)
        def _():
            for copy in copies[k]:
                copy.wait()

    @pl.when(step == 0)
    def _():
        for group in copies:
            for copy in group:
                copy.start()
        sums_ref[...] = jnp.zeros_like(sums_ref)
        upsums_ref[...] = jnp.zeros_like(upsums_ref)

    arrive(0)
    resid = (
        token_ref[...].astype(F32) + dot(mixed_ref[...], merge_ref[...]) + outbias_ref[...]
    )
    unit, scale = norm_parts(resid)
    normed_ref[...] = (unit * gain_ref[...] + shift_ref[...]).astype(BF16)
    resid_ref[...] = resid
    arrive(1)
    arrive(2)
    total_ref[...] = resid + downbias_ref[...]

    def forward(c, nothing):
        cols = pl.ds(pl.multiple_of(c * width, 128), width)
        hidden = dot(normed_ref[...], up_ref[:, cols]) + upbias_ref[:, cols]
        square = hidden * hidden
        curve = jnp.tanh(0.7978845608028654 * (hidden + 0.044715 * square * hidden))
        half = 0.5 * (1.0 + curve)
        active = (half * hidden).astype(BF16)
        active_ref[:, cols] = active
        slope_ref[:, cols] = half + 0.5 * hidden * (1.0 - curve * curve) * (
            0.7978845608028654 * (1.0 + 3.0 * 0.044715 * square)
        )
        total_ref[...] += dot(active, down_ref[cols, :])
        return nothing

    lax.fori_loop(0, chunks, forward, 0)
    result = total_ref[...]
    layer_ref[...] = result.astype(BF16)
    error = result - teacher_ref[...].astype(F32)
    weight = weight_ref[...]
    sums_ref[4:5, :] += jnp.sum(weight * (error * error), 0, keepdims=True)
    gresult = error * (weight * factor_ref[0])
    gmlp = gresult.astype(BF16)
    gmlp_ref[...] = gmlp
    gresid_ref[...] = gresult
    sums_ref[3:4, :] += jnp.sum(gmlp.astype(F32), 0, keepdims=True)
    total_ref[...] = jnp.zeros_like(total_ref)

    def backward(c, nothing):
        cols = pl.ds(pl.multiple_of(c * width, 128), width)
        gactive = dot(gmlp_ref[...], down_ref[cols, :], NT)
        ghidden = (gactive * slope_ref[:, cols]).astype(BF16)
        ghidden_ref[:, cols] = ghidden
        upsums_ref[0:1, cols] += jnp.sum(ghidden.astype(F32), 0, keepdims=True)
        total_ref[...] += dot(ghidden, up_ref[:, cols], NT)
        return nothing

    lax.fori_loop(0, chunks, backward, 0)
    gnormed = total_ref[...]
    unit, scale = norm_parts(resid_ref[...])
    sums_ref[1:2, :] += jnp.sum(gnormed * unit, 0, keepdims=True)
    sums_ref[2:3, :] += jnp.sum(gnormed, 0, keepdims=True)
    gresid = gresid_ref[...] + norm_back(gnormed, gain_ref[...], unit, scale)
    gresid_ref[...] = gresid
    gbranch = gresid.astype(BF16)
    gbranch_ref[...] = gbranch
    sums_ref[0:1, :] += jnp.sum(gbranch.astype(F32), 0, keepdims=True)
    gmixed_ref[...] = dot(gbranch, merge_ref[...], NT).astype(BF16)


def mlp(factor, mixed, tokens, teacher, weight, vectors, slab):
    rows, width = tokens.shape
    outbias, gain, shift, upbias, downbias = vectors
    hidden = upbias.shape[1]
    tile = lambda n: pl.BlockSpec((ROW_TILE, n), lambda i: (i, 0))
    fixed = lambda m, n: pl.BlockSpec((m, n), lambda i: (0, 0))
    shape = jax.ShapeDtypeStruct
    return pl.pallas_call(
        mlp_kernel,
        grid_spec=pltpu.PrefetchScalarGridSpec(
            num_scalar_prefetch=0,
            grid=(rows // ROW_TILE,),
            in_specs=[
                pl.BlockSpec(memory_space=pltpu.SMEM),
                tile(width),
                tile(width),
                tile(width),
                tile(1),
                fixed(1, width),
                fixed(1, width),
                fixed(1, width),
                fixed(1, hidden),
                fixed(1, width),
                pl.BlockSpec(memory_space=pl.ANY),
            ],
            out_specs=[
                tile(width),
                tile(width),
                tile(width),
                tile(width),
                tile(hidden),
                tile(hidden),
                tile(width),
                tile(width),
                fixed(8, width),
                fixed(8, hidden),
            ],
            scratch_shapes=[
                pltpu.VMEM((width, width), BF16),
                pltpu.VMEM((width, hidden), BF16),
                pltpu.VMEM((hidden, width), BF16),
                pltpu.VMEM((ROW_TILE, hidden), F32),
                pltpu.VMEM((ROW_TILE, width), F32),
                pltpu.VMEM((ROW_TILE, width), F32),
                pltpu.SemaphoreType.DMA((3, slab.shape[0] * (hidden // width))),
            ],
        ),
        out_shape=[
            shape((rows, width), BF16),
            shape((rows, width), F32),
            shape((rows, width), BF16),
            shape((rows, width), BF16),
            shape((rows, hidden), BF16),
            shape((rows, hidden), BF16),
            shape((rows, width), BF16),
            shape((rows, width), BF16),
            shape((8, width), F32),
            shape((8, hidden), F32),
        ],
        compiler_params=pltpu.CompilerParams(vmem_limit_bytes=VMEM_LIMIT),
        cost_estimate=pl.CostEstimate(
            flops=4 * rows * width * (width + 2 * hidden),
            bytes_accessed=40 << 20,
            transcendentals=rows * hidden,
        ),
        name="mlp",
    )(factor, mixed, tokens, teacher, weight, outbias, gain, shift, upbias, downbias, slab)


def outer_kernel(
    mixed_ref,
    gbranch_ref,
    normed_ref,
    ghidden_ref,
    active_ref,
    gmlp_ref,
    small_ref,
    slab_ref,
    split_ref,
    block_ref,
    small_sem,
    split_sems,
    block_sems,
):
    owners, rows, width = split_ref.shape[1:]
    chunks = block_ref.shape[2] // rows
    share = owners // chunks
    step = pl.program_id(0)
    small = pltpu.make_async_copy(
        small_ref, slab_ref.at[:, pl.ds((1 + 2 * chunks) * rows, small_ref.shape[1]), :], small_sem
    )

    def split_copy(index):
        return pltpu.make_async_copy(
            split_ref.at[index % 2],
            slab_ref.at[:, pl.ds(pl.multiple_of(index * rows, 16), rows), :],
            split_sems.at[index % 2],
        )

    def block_copy(index):
        return pltpu.make_async_copy(
            block_ref.at[index % 2],
            slab_ref.at[
                pl.ds(index * share, share), pl.ds((1 + chunks) * rows, chunks * rows), :
            ],
            block_sems.at[index % 2],
        )

    @pl.when(step == 0)
    def _():
        small.start()
        out = dot(mixed_ref[...], gbranch_ref[...], TN).astype(BF16)
        split_ref[0] = out.reshape(owners, rows, width)
        split_copy(0).start()

    @pl.when((step >= 1) & (step <= chunks))
    def _():
        @pl.when(step >= 2)
        def _():
            split_copy(step - 2).wait()

        out = dot(normed_ref[...], ghidden_ref[...], TN).astype(BF16)
        split_ref[step % 2] = out.reshape(owners, rows, width)
        split_copy(step).start()

    @pl.when(step > chunks)
    def _():
        index = step - 1 - chunks

        @pl.when(index >= 2)
        def _():
            block_copy(index - 2).wait()

        out = dot(active_ref[...], gmlp_ref[...], TN).astype(BF16)
        block_ref[index % 2] = out.reshape(share, chunks * rows, width)
        block_copy(index).start()

    @pl.when(step == 2 * chunks)
    def _():
        small.wait()
        split_copy(chunks - 1).wait()
        split_copy(chunks).wait()
        block_copy(chunks - 2).wait()
        block_copy(chunks - 1).wait()


def outer_all(mixed, gbranch, normed, ghidden, active, gmlp, small):
    tokens, width = mixed.shape
    owners, extra, _ = small.shape
    chunks = ghidden.shape[1] // width
    rows = width // owners
    whole = pl.BlockSpec((tokens, width), lambda i: (0, 0))
    return pl.pallas_call(
        outer_kernel,
        grid=(1 + 2 * chunks,),
        in_specs=[
            whole,
            whole,
            whole,
            pl.BlockSpec((tokens, width), lambda i: (0, jnp.clip(i - 1, 0, chunks - 1))),
            pl.BlockSpec((tokens, width), lambda i: (0, jnp.clip(i - 1 - chunks, 0, chunks - 1))),
            whole,
            pl.BlockSpec((owners, extra, width), lambda i: (0, 0, 0)),
        ],
        out_specs=pl.BlockSpec(memory_space=pl.ANY),
        out_shape=jax.ShapeDtypeStruct(
            (owners, (1 + 2 * chunks) * rows + extra, width), BF16
        ),
        scratch_shapes=[
            pltpu.VMEM((2, owners, rows, width), BF16),
            pltpu.VMEM((2, owners // chunks, chunks * rows, width), BF16),
            pltpu.SemaphoreType.DMA,
            pltpu.SemaphoreType.DMA((2,)),
            pltpu.SemaphoreType.DMA((2,)),
        ],
        compiler_params=pltpu.CompilerParams(vmem_limit_bytes=VMEM_LIMIT),
        cost_estimate=pl.CostEstimate(
            flops=2 * tokens * width * width * (1 + 2 * chunks),
            bytes_accessed=30 << 20,
            transcendentals=0,
        ),
        name="outer_all",
    )(mixed, gbranch, normed, ghidden, active, gmlp, small)


def halo_back_kernel(
    count, low_ref, order_ref, halo_ref, gkey_ref, gvalue_ref, *rest
):
    pieces = rest[:count]
    out_ref, sums_ref, weight_ref, sems = rest[count:]
    seq, tile = pl.program_id(0), pl.program_id(1)
    width = halo_ref.shape[-1]

    @pl.when((seq == 0) & (tile == 0))
    def _():
        copies = piece_copies(order_ref, pieces, weight_ref, sems)
        for copy in copies:
            copy.start()
        for copy in copies:
            copy.wait()
        sums_ref[...] = jnp.zeros_like(sums_ref)

    @pl.when(tile < low_ref[seq])
    def _():
        out_ref[...] = jnp.zeros_like(out_ref)

    @pl.when(tile >= low_ref[seq])
    def _():
        grad = dot(gkey_ref[0], weight_ref[:, width : 2 * width], NT)
        grad += dot(gvalue_ref[0], weight_ref[:, 2 * width :], NT)
        unit, _ = norm_parts(halo_ref[0].astype(F32))
        out_ref[0] = grad.astype(BF16)
        sums_ref[0:1, :] += jnp.sum(grad * unit, 0, keepdims=True)
        sums_ref[1:2, :] += jnp.sum(grad, 0, keepdims=True)


def halo_back(low, order, halo, gkeys, gvalues, pieces):
    seqs, rows, width = halo.shape
    halo_tiles = rows // ROW_TILE
    tile = (1, ROW_TILE, width)
    spot = lambda s, t, low, order: (s, jnp.minimum(jnp.maximum(t, low[s]), halo_tiles - 1), 0)
    plain = lambda s, t, low, order: (s, t, 0)
    return pl.pallas_call(
        functools.partial(halo_back_kernel, len(pieces)),
        grid_spec=pltpu.PrefetchScalarGridSpec(
            num_scalar_prefetch=2,
            grid=(seqs, halo_tiles),
            in_specs=[pl.BlockSpec(tile, spot)] * 3
            + [pl.BlockSpec(memory_space=pl.ANY)] * len(pieces),
            out_specs=[
                pl.BlockSpec(tile, plain),
                pl.BlockSpec((8, width), lambda s, t, low, order: (0, 0)),
            ],
            scratch_shapes=[
                pltpu.VMEM((width, 3 * width), BF16),
                pltpu.SemaphoreType.DMA((len(pieces),)),
            ],
        ),
        out_shape=[
            jax.ShapeDtypeStruct((seqs, rows, width), BF16),
            jax.ShapeDtypeStruct((8, width), F32),
        ],
        compiler_params=pltpu.CompilerParams(vmem_limit_bytes=VMEM_LIMIT),
        cost_estimate=pl.CostEstimate(
            flops=4 << 30, bytes_accessed=16 << 20, transcendentals=0
        ),
        name="halo_back",
    )(low, order, halo, gkeys, gvalues, *pieces)


def own_back_kernel(
    halo_tiles,
    count,
    low_ref,
    order_ref,
    own_ref,
    normed_ref,
    gquery_ref,
    gkey_ref,
    gvalue_ref,
    *rest,
):
    pieces = rest[:count]
    gnormed_ref, gweight_ref, sums_ref, weight_ref, total_ref, sems = rest[count:]
    seq, tile = pl.program_id(0), pl.program_id(1)
    width = own_ref.shape[-1]
    own = tile >= halo_tiles
    copies = piece_copies(order_ref, pieces, weight_ref, sems)

    @pl.when((seq == 0) & (tile == 0))
    def _():
        for copy in copies:
            copy.start()
        sums_ref[...] = jnp.zeros_like(sums_ref)
        total_ref[...] = jnp.zeros_like(total_ref)
        for copy in copies:
            copy.wait()

    def gather(index, grad_ref):
        cols = slice(index * width, (index + 1) * width)
        total_ref[:, cols] += dot(normed_ref[0], grad_ref[0], TN)

    @pl.when(tile >= low_ref[seq])
    def _():
        gather(1, gkey_ref)
        gather(2, gvalue_ref)
        sums_ref[3:4, :] += jnp.sum(gvalue_ref[0].astype(F32), 0, keepdims=True)

    @pl.when(own)
    def _():
        gather(0, gquery_ref)
        sums_ref[2:3, :] += jnp.sum(gquery_ref[0].astype(F32), 0, keepdims=True)
        grad = dot(gquery_ref[0], weight_ref[:, :width], NT)
        grad += dot(gkey_ref[0], weight_ref[:, width : 2 * width], NT)
        grad += dot(gvalue_ref[0], weight_ref[:, 2 * width :], NT)
        gnormed_ref[0] = grad
        unit, _ = norm_parts(own_ref[0].astype(F32))
        sums_ref[0:1, :] += jnp.sum(grad * unit, 0, keepdims=True)
        sums_ref[1:2, :] += jnp.sum(grad, 0, keepdims=True)

    @pl.when((seq == pl.num_programs(0) - 1) & (tile == pl.num_programs(1) - 1))
    def _():
        gweight_ref[...] = total_ref[...].astype(BF16)


def own_back(low, order, own, normed, gquery, gkeys, gvalues, pieces):
    seqs, block, width = own.shape
    length = normed.shape[1]
    halo_tiles = (length - block) // ROW_TILE
    own_tiles = block // ROW_TILE
    tile = (1, ROW_TILE, width)
    spot = lambda s, t, low, order: (s, jnp.maximum(t, low[s]), 0)
    in_own = lambda s, t, low, order: (s, jnp.maximum(t - halo_tiles, 0), 0)
    fixed = lambda s, t, low, order: (0, 0)
    return pl.pallas_call(
        functools.partial(own_back_kernel, halo_tiles, len(pieces)),
        grid_spec=pltpu.PrefetchScalarGridSpec(
            num_scalar_prefetch=2,
            grid=(seqs, halo_tiles + own_tiles),
            in_specs=[
                pl.BlockSpec(tile, in_own),
                pl.BlockSpec(tile, spot),
                pl.BlockSpec(tile, in_own),
                pl.BlockSpec(tile, spot),
                pl.BlockSpec(tile, spot),
            ]
            + [pl.BlockSpec(memory_space=pl.ANY)] * len(pieces),
            out_specs=[
                pl.BlockSpec(tile, in_own),
                pl.BlockSpec((width, 3 * width), fixed),
                pl.BlockSpec((8, width), fixed),
            ],
            scratch_shapes=[
                pltpu.VMEM((width, 3 * width), BF16),
                pltpu.VMEM((width, 3 * width), F32),
                pltpu.SemaphoreType.DMA((len(pieces),)),
            ],
        ),
        out_shape=[
            jax.ShapeDtypeStruct((seqs, block, width), F32),
            jax.ShapeDtypeStruct((width, 3 * width), BF16),
            jax.ShapeDtypeStruct((8, width), F32),
        ],
        compiler_params=pltpu.CompilerParams(vmem_limit_bytes=VMEM_LIMIT),
        cost_estimate=pl.CostEstimate(
            flops=16 << 30, bytes_accessed=24 << 20, transcendentals=0
        ),
        name="own_back",
    )(low, order, own, normed, gquery, gkeys, gvalues, *pieces)


def finish_kernel(seqs, own_ref, gnormed_ref, gresid_ref, gain_ref, *rest):
    near_refs, far_refs = rest[:seqs], rest[seqs:-2]
    out_ref, total_ref = rest[-2:]
    unit, scale = norm_parts(own_ref[0].astype(F32))
    for seq, near_ref in enumerate(near_refs):

        @pl.when(pl.program_id(0) == seq)
        def _():
            total_ref[...] = gnormed_ref[0] + near_ref[...].astype(F32)

    for far_ref in far_refs:

        @pl.when(pl.program_id(1) == pl.num_programs(1) - 1)
        def _():
            total_ref[-HALO_CHUNK:, :] += far_ref[0].astype(F32)

    out_ref[0] = (gresid_ref[0] + norm_back(total_ref[...], gain_ref[...], unit, scale)).astype(BF16)


def finish(own, gnormed, near, far, gresid, gain):
    seqs, block, width = own.shape
    tile = pl.BlockSpec((1, ROW_TILE, width), lambda s, t: (s, t, 0))
    last = pl.BlockSpec((1, HALO_CHUNK, width), lambda s, t: (s, 0, 0))
    return pl.pallas_call(
        functools.partial(finish_kernel, seqs),
        grid=(seqs, block // ROW_TILE),
        in_specs=[tile, tile, tile, pl.BlockSpec((1, width), lambda s, t: (0, 0))]
        + [pl.BlockSpec((ROW_TILE, width), lambda s, t: (t, 0))] * seqs
        + [last] * len(far),
        out_specs=tile,
        out_shape=jax.ShapeDtypeStruct(own.shape, BF16),
        scratch_shapes=[pltpu.VMEM((ROW_TILE, width), F32)],
        cost_estimate=pl.CostEstimate(
            flops=20 * seqs * block * width,
            bytes_accessed=14 * seqs * block * width,
            transcendentals=0,
        ),
        name="finish",
    )(own, gnormed, gresid, gain, *near, *far)


def swap(x, axis, bit):
    size = lax.axis_size(axis)
    return lax.ppermute(x, axis, [(i, i ^ bit) for i in range(size)])


def shift(x, axis, step):
    size = lax.axis_size(axis)
    return lax.ppermute(
        x, axis, [(i, i + step) for i in range(size) if 0 <= i + step < size]
    )


def sum_over(x, axis):
    bit = 1
    while bit < lax.axis_size(axis):
        x = x + swap(x, axis, bit)
        bit *= 2
    return x


def max_over(x, axis):
    bit = 1
    while bit < lax.axis_size(axis):
        x = jnp.maximum(x, swap(x, axis, bit))
        bit *= 2
    return x


def gather_near(shard):
    size = lax.axis_size("fsdp")
    if size != 8:
        return [lax.all_gather(shard, "fsdp", axis=0, tiled=True)]
    return [shard] + [swap(shard, "fsdp", 2 * d) for d in range(1, size // 2)]


def gather_rest(near):
    if lax.axis_size("fsdp") != 8:
        return near
    return near + [swap(piece, "fsdp", 1) for piece in near]


def piece_order():
    size = lax.axis_size("fsdp")
    me = lax.axis_index("fsdp").astype(jnp.int32)
    if size != 8:
        return jnp.zeros((1,), jnp.int32)
    return jnp.stack(
        [me ^ (2 * d) for d in range(size // 2)] + [me ^ (2 * d) ^ 1 for d in range(size // 2)]
    )


def sum_seq(total):
    if lax.axis_size("seq") != 4:
        return lax.psum(total, "seq")
    return sum_seq_rest(sum_seq_first(total))


def sum_seq_first(total):
    rows, columns = total.shape
    odd = lax.axis_index("seq") % 2
    halves = total.reshape(2, rows // 2, columns)
    pick = lambda k: lax.dynamic_index_in_dim(halves, k, 0, keepdims=False)
    return (pick(odd).astype(F32) + swap(pick(1 - odd), "seq", 1).astype(F32)).astype(BF16)


def sum_seq_rest(half):
    odd = lax.axis_index("seq") % 2
    half = (half.astype(F32) + swap(half, "seq", 2).astype(F32)).astype(BF16)
    back = swap(half, "seq", 1)
    return jnp.where(
        odd == 0, jnp.concatenate([half, back], 0), jnp.concatenate([back, half], 0)
    )


def reduce_rows(parts, extra, *first):
    size = lax.axis_size("fsdp")
    me = lax.axis_index("fsdp")
    if size != 8:
        parts = jnp.concatenate([parts, extra], 1)
        total = lax.psum_scatter(parts, "fsdp", scatter_dimension=0, tiled=False)
        return lax.psum(total, "seq"), *first
    rows, columns = parts.shape[1:]
    few = extra.shape[1]
    core = me % 2
    chip = me // 2
    pick = lambda a, k, ax: lax.dynamic_index_in_dim(a, k, ax, keepdims=False)
    parts = parts.reshape(size // 2, 2, rows, columns)
    extra = extra.reshape(size // 2, 2, few, columns)
    half = lambda k: jnp.concatenate([pick(parts, k, 1), pick(extra, k, 1)], 1)
    other = swap(half(1 - core), "fsdp", 1)
    mine = (half(core).astype(F32) + other.astype(F32)).astype(BF16)
    arrived = [
        swap(pick(mine, chip ^ d, 0), "fsdp", 2 * d) for d in range(1, size // 2)
    ]
    arrived, *first = lax.optimization_barrier((arrived, *first))
    total = pick(mine, chip, 0).astype(F32)
    for part in arrived:
        total = total + part.astype(F32)
    return sum_seq(total.astype(BF16)), *first


def gather_slab(outweight, fcweight, projweight, *first):
    width = outweight.shape[1]
    cuts = fcweight.shape[1] // width

    def join(out, up, down, axis):
        ups = [lax.slice_in_dim(up, c * width, (c + 1) * width, axis=-1) for c in range(cuts)]
        return jnp.concatenate([out, *ups, down], axis)

    if lax.axis_size("fsdp") == SHARES:
        slab = join(outweight, fcweight, projweight, 0)
        slab, *first = lax.optimization_barrier((slab, *first))
        return lax.all_gather(slab, "fsdp", axis=0, tiled=False), *first
    whole = [
        lax.all_gather(w, "fsdp", axis=0, tiled=True) for w in (outweight, fcweight, projweight)
    ]
    return join(*(w.reshape(SHARES, -1, w.shape[1]) for w in whole), 1), *first


def reduce_slab(slab, width, hidden):
    owners = lax.axis_size("fsdp")
    cuts = hidden // width
    rows = width // SHARES

    def part(array, axis):
        at = lambda a, b: lax.slice_in_dim(array, a * rows, b * rows, axis=axis)
        ups = [at(1 + c, 2 + c) for c in range(cuts)]
        rest = lax.slice_in_dim(array, (1 + 2 * cuts) * rows, array.shape[axis], axis=axis)
        return at(0, 1), jnp.concatenate(ups, -1), at(1 + cuts, 1 + 2 * cuts), rest

    if owners == SHARES:
        return part(slab.astype(F32), 0)
    *grads, rest = part(slab, 1)
    grads = [
        lax.psum(
            lax.psum_scatter(
                g.reshape(-1, g.shape[-1]), "fsdp", scatter_dimension=0, tiled=True
            ),
            "seq",
        ).astype(F32)
        for g in grads
    ]
    rest = lax.psum(rest.astype(F32), ("fsdp", "seq"))
    return *grads, rest


def local(
    tokens,
    teacher,
    segment_ids,
    latent_flags,
    valid_mask,
    attngain,
    attnshift,
    qkvweight,
    qvbias,
    outweight,
    outbias,
    mlpgain,
    mlpshift,
    fcweight,
    fcbias,
    projweight,
    projbias,
):
    seqs, block, width = tokens.shape
    groups = lax.axis_size("seq")
    owners = lax.axis_size("fsdp")
    rows = seqs * block
    halo_rows = (groups - 1) * block
    far_rows = halo_rows - block
    me = lax.axis_index("fsdp")
    place = lax.axis_index("seq").astype(jnp.int32)
    hidden = fcweight.shape[1]

    order = piece_order()
    qkv_pieces = gather_near(qkvweight)

    weight = (valid_mask * (1 - latent_flags)).astype(F32)
    below = jnp.sum(
        (segment_ids[:, :, None] < jnp.arange(1, 4, dtype=jnp.int32)).astype(jnp.int32), 1
    )
    facts = jnp.concatenate([below.reshape(-1), jnp.sum(weight).astype(jnp.int32)[None]])
    facts = sum_over(facts, "seq")
    bounds = facts[:-1].reshape(seqs, 3)

    sent, facts = lax.optimization_barrier((tokens, facts))
    near = [shift(sent[s], "seq", 1) for s in range(seqs)]
    far = shift(sent[:, block - HALO_CHUNK :], "seq", 2) if far_rows > 0 else None

    def start_of(positions):
        found = jnp.zeros((seqs,) + positions.shape, jnp.int32)
        for d in range(3):
            bound = bounds[:, d].reshape((seqs,) + (1,) * positions.ndim)
            found = jnp.maximum(found, jnp.where(bound <= positions[None], bound, 0))
        return found

    firsts = jnp.arange(groups, dtype=jnp.int32) * block
    reach = jnp.max(firsts[None] - start_of(firsts)) - block
    chunks = jnp.maximum(reach + HALO_CHUNK - 1, 0) // HALO_CHUNK

    shards = [attngain, attnshift, qvbias, outbias, mlpgain, mlpshift, fcbias, projbias]
    packed = jnp.concatenate(shards).astype(F32)
    table = jnp.where(
        lax.broadcasted_iota(jnp.int32, (owners, packed.shape[0]), 0) == me,
        packed[None],
        0.0,
    )
    line = lax.broadcasted_iota(jnp.int32, (8, packed.shape[0]), 0)
    table = jnp.concatenate(
        [
            table,
            jnp.where(line == 0, facts[-1].astype(F32), jnp.where(line == 1, chunks.astype(F32), 0.0)),
        ],
        0,
    )
    is_reach = lax.broadcasted_iota(jnp.int32, table.shape, 0) == owners + 1
    bit = 1
    while bit < owners:
        other = swap(table, "fsdp", bit)
        table = jnp.where(is_reach, jnp.maximum(table, other), table + other)
        bit *= 2
    qkv_pieces = gather_rest(qkv_pieces)
    slab, qkv_pieces, table, near[0] = gather_slab(
        outweight, fcweight, projweight, qkv_pieces, table, near[0]
    )

    count = table[owners, 0]
    chunks = table[owners + 1, 0].astype(jnp.int32)
    vectors = []
    at = 0
    for shard in shards:
        size = shard.shape[0]
        vectors.append(table[:owners, at : at + size].reshape(1, size * owners))
        at += size
    gain1, shift1, bias1, outbias_v, gain2, shift2, upbias, downbias = vectors


    base = (place - (groups - 1)) * block
    starts = start_of(place * block + jnp.arange(block, dtype=jnp.int32)) - base
    low_rows = starts[:, ::QUERY_TILE]
    low = (low_rows // KEY_TILE).reshape(-1)
    low_tile = starts[:, 0] // ROW_TILE
    first = low_tile * (ROW_TILE // KEY_TILE)
    starts = starts[:, None, :]

    halo = jnp.stack(near)
    if far_rows > 0:
        blank = jnp.zeros((seqs, far_rows - HALO_CHUNK, width), BF16)
        halo = jnp.concatenate([blank, far, halo], 1)

    def fetch(state):
        j, halo = state
        sent = lax.dynamic_slice_in_dim(halo, halo_rows - HALO_CHUNK * (j + 1), HALO_CHUNK, 1)
        came = shift(sent, "seq", 1)
        return j + 1, lax.dynamic_update_slice_in_dim(
            halo, came, far_rows - HALO_CHUNK * (j + 1), 1
        )

    if far_rows > 0:
        _, halo = lax.while_loop(lambda state: state[0] < chunks, fetch, (jnp.int32(1), halo))

    normed, query, keys, values = project(
        low_tile, order, halo, tokens, gain1, shift1, bias1, qkv_pieces
    )
    mixed, logs = attend(low, query, keys, values, starts)

    factor = (rows * owners * groups) / count
    (
        layer_out,
        gresid,
        gmixed,
        normed2,
        active,
        ghidden,
        gmlp,
        gbranch,
        sums,
        upsums,
    ) = mlp(
        factor.reshape(1),
        mixed.reshape(rows, width),
        tokens.reshape(rows, width),
        teacher.reshape(rows, width),
        weight.reshape(rows, 1),
        (outbias_v, gain2, shift2, upbias, downbias),
        slab,
    )

    small = jnp.concatenate(
        [upsums[0].reshape(SHARES, -1)] + [sums[k].reshape(SHARES, -1) for k in range(4)], 1
    )
    line = lax.broadcasted_iota(jnp.int32, (SHARES, 16, width), 1)
    small = jnp.where(line == 0, small[:, None, :], jnp.where(line == 1, sums[4], 0.0))
    outer = outer_all(
        mixed.reshape(rows, width), gbranch, normed2, ghidden, active, gmlp, small.astype(BF16)
    )
    outer, gmixed = lax.optimization_barrier((outer, gmixed))
    staged = owners == SHARES and groups == 4
    if owners == SHARES:
        outer = lax.psum_scatter(outer, "fsdp", scatter_dimension=0, tiled=False)
        outer = sum_seq_first(outer) if staged else sum_seq(outer)

    gquery, gkeys, gvalues = attend_back(
        low, first, query, keys, values, starts, mixed, gmixed.reshape(seqs, block, width), logs
    )
    ghalo, halo_sums = halo_back(low_tile, order, halo, gkeys, gvalues, qkv_pieces)

    def give(state):
        j, ghalo = state
        j = j - 1
        sent = lax.dynamic_slice_in_dim(ghalo, far_rows - HALO_CHUNK * (j + 1), HALO_CHUNK, 1)
        came = shift(sent, "seq", -1)
        spot = halo_rows - HALO_CHUNK * (j + 1)
        held = lax.dynamic_slice_in_dim(ghalo, spot, HALO_CHUNK, 1)
        total = (held.astype(F32) + came.astype(F32)).astype(BF16)
        return j, lax.dynamic_update_slice_in_dim(ghalo, total, spot, 1)

    if far_rows > 0:
        _, ghalo = lax.while_loop(lambda state: state[0] > 1, give, (chunks, ghalo))

    ghalo, gquery = lax.optimization_barrier((ghalo, gquery))
    near = [shift(ghalo[s, far_rows:], "seq", -1) for s in range(seqs)]
    far = []
    if far_rows > 0:
        far = [shift(ghalo[:, far_rows - HALO_CHUNK : far_rows], "seq", -2)]
    gnormed, gweight, own_sums = own_back(
        low_tile, order, tokens, normed, gquery, gkeys, gvalues, qkv_pieces
    )
    late = jnp.concatenate(
        [(own_sums[k] + halo_sums[k]).reshape(owners, -1) for k in range(2)]
        + [own_sums[2:4].reshape(owners, -1)],
        1,
    ).astype(BF16)
    late = jnp.pad(late, ((0, 0), (0, 2 * width + width - late.shape[1])))
    line = lax.broadcasted_iota(jnp.int32, (owners, 16, 3 * width), 1)
    late = jnp.where(line == 0, late[:, None, :], jnp.zeros((), BF16))
    gweight, near[0] = lax.optimization_barrier((gweight, near[0]))
    grad_tokens = finish(
        tokens,
        gnormed,
        near,
        far,
        gresid.reshape(tokens.shape),
        gain1,
    )

    joint, outer, grad_tokens = reduce_rows(
        gweight.reshape(owners, width // owners, 3 * width), late, outer, grad_tokens
    )
    joint = joint.astype(F32)
    if staged:
        outer = sum_seq_rest(outer)
    grad_merge, grad_up, grad_down, small = reduce_slab(outer, width, hidden)

    share = width // owners
    if owners == SHARES:
        at = hidden // owners
        cuts = [small[0, :at]] + [
            small[0, at + k * share : at + (k + 1) * share] for k in range(4)
        ]
        loss_row = small[1]
    else:
        at = hidden // SHARES
        wide = width // SHARES
        full = [small[:, 0, :at].reshape(-1)] + [
            small[:, 0, at + k * wide : at + (k + 1) * wide].reshape(-1) for k in range(4)
        ]
        cuts = [
            lax.dynamic_slice_in_dim(v, me * (v.shape[0] // owners), v.shape[0] // owners)
            for v in full
        ]
        loss_row = small[0, 1]
    loss = jnp.sum(loss_row) / (width * count)
    return (
        loss,
        layer_out.reshape(tokens.shape),
        grad_tokens,
        joint[share, :share],
        joint[share, share : 2 * share],
        joint[:share],
        joint[share, 2 * share : 4 * share],
        grad_merge,
        cuts[1],
        cuts[2],
        cuts[3],
        grad_up,
        cuts[0],
        grad_down,
        cuts[4],
    )


def solution(mesh):
    placed = (
        P("fsdp", "seq", None),
        P("fsdp", "seq", None),
        P("fsdp", "seq"),
        P("fsdp", "seq"),
        P("fsdp", "seq"),
        P("fsdp"),
        P("fsdp"),
        P("fsdp", None),
        P("fsdp"),
        P("fsdp", None),
        P("fsdp"),
        P("fsdp"),
        P("fsdp"),
        P("fsdp", None),
        P("fsdp"),
        P("fsdp", None),
        P("fsdp"),
    )
    return jax.shard_map(
        local,
        mesh=mesh,
        in_specs=placed,
        out_specs=(
            P(),
            P("fsdp", "seq", None),
            P("fsdp", "seq", None),
            P("fsdp"),
            P("fsdp"),
            P("fsdp", None),
            P("fsdp"),
            P("fsdp", None),
            P("fsdp"),
            P("fsdp"),
            P("fsdp"),
            P("fsdp", None),
            P("fsdp"),
            P("fsdp", None),
            P("fsdp"),
        ),
        check_vma=False,
    )
```

```python
import functools

import jax
import jax.numpy as jnp
from jax import lax
from jax.experimental import pallas as pl
from jax.experimental.pallas import tpu as pltpu
from jax.sharding import PartitionSpec as P

H = 12
HD = 64
PAIR = 2 * HD
EPSILON = 1e-05
KEY_TILE = 128
QUERY_TILE = 128
ROW_TILE = 256
MLP_TILE = 256
MLP_CHUNK = 1536
HALO_CHUNK = 128
SHARES = 8
SMALL_ROWS = 16
VMEM_LIMIT = 62 * 1024 * 1024

NT = (((1,), (1,)), ((), ()))
NN = (((1,), (0,)), ((), ()))
TN = (((0,), (0,)), ((), ()))
F32 = jnp.float32
BF16 = jnp.bfloat16


def dot(left, right, dims=NN):
    return lax.dot_general(left, right, dims, preferred_element_type=F32)


def norm_parts(values):
    center = values - jnp.mean(values, -1, keepdims=True)
    spread = jnp.mean(center * center, -1, keepdims=True)
    scale = lax.rsqrt(spread + EPSILON)
    return center * scale, scale


def norm_back(grad, gain, unit, scale):
    weighted = grad * gain
    first = jnp.mean(weighted, -1, keepdims=True)
    second = jnp.mean(weighted * unit, -1, keepdims=True)
    return scale * (weighted - first - unit * second)


def piece_copies(order_ref, pieces, whole_ref, sems):
    copies = []
    for place, piece in enumerate(pieces):
        rows = piece.shape[0]
        if len(pieces) == 1:
            target = whole_ref
        else:
            target = whole_ref.at[pl.ds(pl.multiple_of(order_ref[place] * rows, 16), rows), :]
        copies.append(pltpu.make_async_copy(piece, target, sems.at[place]))
    return copies


def project_own_kernel(count, order_ref, own_ref, gain_ref, shift_ref, bias_ref, *rest):
    pieces = rest[:count]
    normed_ref, query_ref, keyvalue_ref, whole_ref, weight_ref, sems, whole_sem = rest[count:]
    width = own_ref.shape[-1]
    seq = pl.program_id(0)
    whole = pltpu.make_async_copy(weight_ref, whole_ref, whole_sem)

    @pl.when(seq == 0)
    def _():
        copies = piece_copies(order_ref, pieces, weight_ref, sems)
        for copy in copies:
            copy.start()
        for copy in copies:
            copy.wait()
        whole.start()

    unit, _ = norm_parts(own_ref[0].astype(F32))
    normed = (unit * gain_ref[...] + shift_ref[...]).astype(BF16)
    normed_ref[0] = normed
    joint = (dot(normed, weight_ref[...]) + bias_ref[...]).astype(BF16)
    query_ref[0] = joint[:, :width]
    keyvalue_ref[0] = joint[:, width:]

    @pl.when(seq == pl.num_programs(0) - 1)
    def _():
        whole.wait()


def project_own(order, own, gain, shift, bias, pieces, length):
    seqs, block, width = own.shape
    last = length // block - 1
    fixed = lambda s, order: (0, 0)
    spot = lambda s, order: (s, 0, 0)
    end = lambda s, order: (s, last, 0)
    return pl.pallas_call(
        functools.partial(project_own_kernel, len(pieces)),
        grid_spec=pltpu.PrefetchScalarGridSpec(
            num_scalar_prefetch=1,
            grid=(seqs,),
            in_specs=[
                pl.BlockSpec((1, block, width), spot),
                pl.BlockSpec((1, width), fixed),
                pl.BlockSpec((1, width), fixed),
                pl.BlockSpec((1, 3 * width), fixed),
            ]
            + [pl.BlockSpec(memory_space=pl.ANY)] * len(pieces),
            out_specs=[
                pl.BlockSpec((1, block, width), end),
                pl.BlockSpec((1, block, width), spot),
                pl.BlockSpec((1, block, 2 * width), end),
                pl.BlockSpec(memory_space=pl.ANY),
            ],
            scratch_shapes=[
                pltpu.VMEM((width, 3 * width), BF16),
                pltpu.SemaphoreType.DMA((len(pieces),)),
                pltpu.SemaphoreType.DMA,
            ],
        ),
        out_shape=[
            jax.ShapeDtypeStruct((seqs, length, width), BF16),
            jax.ShapeDtypeStruct((seqs, block, width), BF16),
            jax.ShapeDtypeStruct((seqs, length, 2 * width), BF16),
            jax.ShapeDtypeStruct((width, 3 * width), BF16),
        ],
        compiler_params=pltpu.CompilerParams(vmem_limit_bytes=VMEM_LIMIT),
        cost_estimate=pl.CostEstimate(
            flops=6 * seqs * block * width * width, bytes_accessed=16 << 20, transcendentals=0
        ),
        name="project_own",
    )(order, own, gain, shift, bias, *pieces)


def every_tile(low_ref, seqs, tiles, work, every=False):
    for seq in range(seqs):

        def one(tile, nothing):
            work(seq, tile, pl.ds(pl.multiple_of(tile * ROW_TILE, ROW_TILE), ROW_TILE))
            return nothing

        lax.fori_loop(0 if every else low_ref[seq], tiles, one, 0)


def project_halo_kernel(
    low_ref, gain_ref, shift_ref, bias_ref, halo_any, whole_any, *rest
):
    (
        normed_any,
        keyvalue_any,
        halo_ref,
        normed_ref,
        keyvalue_ref,
        weight_ref,
        in_sems,
        normed_sems,
        keyvalue_sems,
        sem,
    ) = rest[2:]
    seqs, rows, width = halo_ref.shape
    tiles = rows // ROW_TILE
    weight = pltpu.make_async_copy(whole_any.at[:, pl.ds(width, 2 * width)], weight_ref, sem)
    weight.start()

    def arrive(seq, tile, at):
        return pltpu.make_async_copy(
            halo_any.at[seq, at], halo_ref.at[seq, at], in_sems.at[seq, tile]
        )

    def leave(seq, tile, at):
        return (
            pltpu.make_async_copy(
                normed_ref.at[seq, at], normed_any.at[seq, at], normed_sems.at[seq, tile]
            ),
            pltpu.make_async_copy(
                keyvalue_ref.at[seq, at], keyvalue_any.at[seq, at], keyvalue_sems.at[seq, tile]
            ),
        )

    def begin(seq, tile, at):
        arrive(seq, tile, at).start()

    def work(seq, tile, at):
        arrive(seq, tile, at).wait()
        unit, _ = norm_parts(halo_ref[seq, at, :].astype(F32))
        normed = (unit * gain_ref[...] + shift_ref[...]).astype(BF16)
        normed_ref[seq, at, :] = normed
        keyvalue_ref[seq, at, :] = (
            dot(normed, weight_ref[...]) + bias_ref[:, width:]
        ).astype(BF16)
        for copy in leave(seq, tile, at):
            copy.start()

    def end(seq, tile, at):
        for copy in leave(seq, tile, at):
            copy.wait()

    every_tile(low_ref, seqs, tiles, begin)
    weight.wait()
    every_tile(low_ref, seqs, tiles, work)
    every_tile(low_ref, seqs, tiles, end)


def project_halo(low, halo, gain, shift, bias, whole, normed, keyvalues):
    seqs, rows, width = halo.shape
    tiles = rows // ROW_TILE
    fixed = lambda i, low: (0, 0)
    anywhere = pl.BlockSpec(memory_space=pl.ANY)
    return pl.pallas_call(
        project_halo_kernel,
        grid_spec=pltpu.PrefetchScalarGridSpec(
            num_scalar_prefetch=1,
            grid=(1,),
            in_specs=[
                pl.BlockSpec((1, width), fixed),
                pl.BlockSpec((1, width), fixed),
                pl.BlockSpec((1, 3 * width), fixed),
                anywhere,
                anywhere,
                anywhere,
                anywhere,
            ],
            out_specs=[anywhere, anywhere],
            scratch_shapes=[
                pltpu.VMEM((seqs, rows, width), BF16),
                pltpu.VMEM((seqs, rows, width), BF16),
                pltpu.VMEM((seqs, rows, 2 * width), BF16),
                pltpu.VMEM((width, 2 * width), BF16),
                pltpu.SemaphoreType.DMA((seqs, tiles)),
                pltpu.SemaphoreType.DMA((seqs, tiles)),
                pltpu.SemaphoreType.DMA((seqs, tiles)),
                pltpu.SemaphoreType.DMA,
            ],
        ),
        out_shape=[
            jax.ShapeDtypeStruct(normed.shape, BF16),
            jax.ShapeDtypeStruct(keyvalues.shape, BF16),
        ],
        input_output_aliases={6: 0, 7: 1},
        compiler_params=pltpu.CompilerParams(vmem_limit_bytes=VMEM_LIMIT),
        cost_estimate=pl.CostEstimate(
            flops=2 * seqs * rows * width * width, bytes_accessed=16 << 20, transcendentals=0
        ),
        name="project_halo",
    )(low, gain, shift, bias, halo, whole, normed, keyvalues)


def two_heads(tile):
    left = lax.broadcasted_iota(jnp.int32, tile.shape, 1) < HD
    zero = jnp.zeros_like(tile)
    return jnp.concatenate([jnp.where(left, tile, zero), jnp.where(left, zero, tile)], 0)


def visible(first_key, starts, first_query):
    shape = (KEY_TILE, starts.shape[1])
    keys = first_key + lax.broadcasted_iota(jnp.int32, shape, 0)
    queries = first_query + lax.broadcasted_iota(jnp.int32, shape, 1)
    return (keys >= starts) & (keys <= queries)


def head_rows(first, second):
    shape = (HD, first.shape[1])
    return jnp.concatenate(
        [jnp.broadcast_to(first, shape), jnp.broadcast_to(second, shape)], 0
    )


def attend_kernel(halo, low_ref, query_ref, keyvalue_ref, start_ref, out_ref, log_ref):
    seq = pl.program_id(0)
    block = query_ref.shape[1]
    width = query_ref.shape[2]
    pairs = width // PAIR
    after = lambda c: slice(width + c.start, width + c.stop)
    tiles = block // QUERY_TILE
    def rows(tile, nothing):
        here = pl.ds(pl.multiple_of(tile * QUERY_TILE, QUERY_TILE), QUERY_TILE)
        starts = start_ref[0, :, here]
        cols = [slice(p * PAIR, (p + 1) * PAIR) for p in range(pairs)]

        def step(j, carry):
            place = pl.ds(pl.multiple_of(j * KEY_TILE, KEY_TILE), KEY_TILE)
            ok = visible(j * KEY_TILE, starts, halo + tile * QUERY_TILE)
            scores = [
                dot(two_heads(keyvalue_ref[0, place, c]), query_ref[0, here, c] * 0.125, NT)
                for c in cols
            ]
            left = []
            for p in range(pairs):
                highs, totals, mixed = carry[3 * p : 3 * p + 3]
                powers, fades, sums, nexts = [], [], [], []
                for h in range(2):
                    part = jnp.where(ok, scores[p][h * KEY_TILE : (h + 1) * KEY_TILE], -1e30)
                    high = highs[h : h + 1]
                    later = jnp.maximum(high, jnp.max(part, 0, keepdims=True))
                    power = jnp.exp(part - later)
                    fade = jnp.exp(high - later)
                    sums.append(totals[h : h + 1] * fade + jnp.sum(power, 0, keepdims=True))
                    powers.append(power.astype(BF16))
                    fades.append(fade)
                    nexts.append(later)
                added = dot(
                    two_heads(keyvalue_ref[0, place, after(cols[p])]), jnp.concatenate(powers, 0), TN
                )
                left += [
                    jnp.concatenate(nexts, 0),
                    jnp.concatenate(sums, 0),
                    mixed * head_rows(*fades) + added,
                ]
            return tuple(left)

        row = jnp.zeros((2, QUERY_TILE), F32)
        done = lax.fori_loop(
            low_ref[seq * tiles + tile],
            (halo + (tile + 1) * QUERY_TILE) // KEY_TILE,
            step,
            (row - 1e30, row, jnp.zeros((PAIR, QUERY_TILE), F32)) * pairs,
        )
        for p in range(pairs):
            highs, totals, mixed = done[3 * p : 3 * p + 3]
            total = head_rows(totals[0:1], totals[1:2])
            out_ref[0, here, cols[p]] = jnp.transpose(mixed / total).astype(BF16)
            log_ref[0, p, :, here] = highs + jnp.log(totals)
        return nothing

    lax.fori_loop(0, tiles, rows, 0)


def attend(low, query, keyvalues, starts):
    seqs, block, width = query.shape
    length = keyvalues.shape[1]
    pairs = width // PAIR
    rows = pl.BlockSpec((1, block, width), lambda s, low: (s, 0, 0))
    full = pl.BlockSpec((1, length, 2 * width), lambda s, low: (s, 0, 0))
    return pl.pallas_call(
        functools.partial(attend_kernel, length - block),
        grid_spec=pltpu.PrefetchScalarGridSpec(
            num_scalar_prefetch=1,
            grid=(seqs,),
            in_specs=[rows, full, pl.BlockSpec((1, 1, block), lambda s, low: (s, 0, 0))],
            out_specs=[rows, pl.BlockSpec((1, pairs, 2, block), lambda s, low: (s, 0, 0, 0))],
        ),
        out_shape=[
            jax.ShapeDtypeStruct((seqs, block, width), BF16),
            jax.ShapeDtypeStruct((seqs, pairs, 2, block), F32),
        ],
        compiler_params=pltpu.CompilerParams(vmem_limit_bytes=VMEM_LIMIT),
        cost_estimate=pl.CostEstimate(
            flops=16 << 30, bytes_accessed=16 << 20, transcendentals=8 << 20
        ),
        name="attend",
    )(low, query, keyvalues, starts)


def attend_back_kernel(
    halo,
    low_ref,
    first_ref,
    query_ref,
    keyvalue_ref,
    start_ref,
    out_ref,
    grad_ref,
    log_ref,
    gquery_ref,
    gkeyvalue_ref,
    turned_ref,
    center_ref,
    sumk_ref,
    sumv_ref,
):
    seq = pl.program_id(0)
    block = query_ref.shape[1]
    width = query_ref.shape[2]
    pairs = width // PAIR
    after = lambda c: slice(width + c.start, width + c.stop)
    tiles = block // QUERY_TILE
    cols = [slice(p * PAIR, (p + 1) * PAIR) for p in range(pairs)]
    turned_ref[...] = jnp.zeros_like(turned_ref)
    for p in range(pairs):
        products = jnp.transpose(grad_ref[0, :, cols[p]].astype(F32) * out_ref[0, :, cols[p]].astype(F32))
        center_ref[p, 0:1, :] = jnp.sum(products[:HD], 0, keepdims=True)
        center_ref[p, 1:2, :] = jnp.sum(products[HD:], 0, keepdims=True)
    left = lax.broadcasted_iota(jnp.int32, (KEY_TILE, PAIR), 1) < HD

    def step(j, nothing):
        place = pl.ds(pl.multiple_of(j * KEY_TILE, KEY_TILE), KEY_TILE)
        sumk_ref[...] = jnp.zeros_like(sumk_ref)
        sumv_ref[...] = jnp.zeros_like(sumv_ref)
        def rows(tile, nothing):
            here = pl.ds(pl.multiple_of(tile * QUERY_TILE, QUERY_TILE), QUERY_TILE)
            last = (halo + (tile + 1) * QUERY_TILE) // KEY_TILE

            @pl.when((j >= low_ref[seq * tiles + tile]) & (j < last))
            def _():
                ok = visible(j * KEY_TILE, start_ref[0, :, here], halo + tile * QUERY_TILE)
                keys = [two_heads(keyvalue_ref[0, place, c]) for c in cols]
                queries = [query_ref[0, here, c] * 0.125 for c in cols]
                grads = [grad_ref[0, here, c] for c in cols]
                scores = [dot(k, q, NT) for k, q in zip(keys, queries)]
                gprobs = [
                    dot(two_heads(keyvalue_ref[0, place, after(c)]), g, NT) for c, g in zip(cols, grads)
                ]
                for p in range(pairs):
                    probs, gscores = [], []
                    for head in range(2):
                        part = slice(head * KEY_TILE, (head + 1) * KEY_TILE)
                        row = slice(head, head + 1)
                        prob = jnp.exp(
                            jnp.where(ok, scores[p][part] - log_ref[0, p, row, here], -1e30)
                        )
                        gscore = prob * (gprobs[p][part] - center_ref[p, row, here])
                        probs.append(prob.astype(BF16))
                        gscores.append(gscore.astype(BF16))
                    probs = jnp.concatenate(probs, 0)
                    gscores = jnp.concatenate(gscores, 0)
                    sumv_ref[p] += dot(probs, grads[p])
                    sumk_ref[p] += dot(gscores, queries[p])
                    turned_ref[p, :, here] += dot(keys[p], gscores, TN)

            return nothing

        lax.fori_loop(0, tiles, rows, 0)

        for p in range(pairs):
            gkeyvalue_ref[0, place, cols[p]] = jnp.where(
                left, sumk_ref[p, :KEY_TILE], sumk_ref[p, KEY_TILE:]
            ).astype(BF16)
            gkeyvalue_ref[0, place, after(cols[p])] = jnp.where(
                left, sumv_ref[p, :KEY_TILE], sumv_ref[p, KEY_TILE:]
            ).astype(BF16)
        return nothing

    lax.fori_loop(first_ref[seq], (halo + block) // KEY_TILE, step, 0)
    for p in range(pairs):
        gquery_ref[0, :, cols[p]] = (jnp.transpose(turned_ref[p]) * 0.125).astype(BF16)


def attend_back(low, first, query, keyvalues, starts, mixed, grad, logs):
    seqs, block, width = query.shape
    length = keyvalues.shape[1]
    pairs = width // PAIR
    rows = pl.BlockSpec((1, block, width), lambda s, low, first: (s, 0, 0))
    full = pl.BlockSpec((1, length, 2 * width), lambda s, low, first: (s, 0, 0))
    return pl.pallas_call(
        functools.partial(attend_back_kernel, length - block),
        grid_spec=pltpu.PrefetchScalarGridSpec(
            num_scalar_prefetch=2,
            grid=(seqs,),
            in_specs=[
                rows,
                full,
                pl.BlockSpec((1, 1, block), lambda s, low, first: (s, 0, 0)),
                rows,
                rows,
                pl.BlockSpec((1, pairs, 2, block), lambda s, low, first: (s, 0, 0, 0)),
            ],
            out_specs=[rows, full],
            scratch_shapes=[
                pltpu.VMEM((pairs, PAIR, block), F32),
                pltpu.VMEM((pairs, 8, block), F32),
                pltpu.VMEM((pairs, 2 * KEY_TILE, PAIR), F32),
                pltpu.VMEM((pairs, 2 * KEY_TILE, PAIR), F32),
            ],
        ),
        out_shape=[
            jax.ShapeDtypeStruct((seqs, block, width), BF16),
            jax.ShapeDtypeStruct((seqs, length, 2 * width), BF16),
        ],
        compiler_params=pltpu.CompilerParams(vmem_limit_bytes=VMEM_LIMIT),
        cost_estimate=pl.CostEstimate(
            flops=40 << 30, bytes_accessed=28 << 20, transcendentals=8 << 20
        ),
        name="attend_back",
    )(low, first, query, keyvalues, starts, mixed, grad, logs)


def slab_copies(slab_ref, merge_ref, up_ref, down_ref, sems):
    owners = slab_ref.shape[0]
    width = slab_ref.shape[2]
    rows = width // owners
    chunks = up_ref.shape[1] // width
    groups = [[], [], []]
    for owner in range(owners):
        here = pl.ds(owner * rows, rows)
        groups[0].append((slab_ref.at[owner, pl.ds(0, rows), :], merge_ref.at[here, :]))
        for c in range(chunks):
            groups[1].append(
                (
                    slab_ref.at[owner, pl.ds((1 + c) * rows, rows), :],
                    up_ref.at[here, pl.ds(c * width, width)],
                )
            )
        groups[2].append(
            (
                slab_ref.at[owner, pl.ds((1 + chunks) * rows, chunks * rows), :],
                down_ref.at[pl.ds(owner * chunks * rows, chunks * rows), :],
            )
        )
    return [
        [pltpu.make_async_copy(*pair, sems.at[k, n]) for n, pair in enumerate(group)]
        for k, group in enumerate(groups)
    ]


def mlp_kernel(
    factor_ref,
    mixed_ref,
    token_ref,
    teacher_ref,
    weight_ref,
    outbias_ref,
    gain_ref,
    shift_ref,
    upbias_ref,
    downbias_ref,
    slab_ref,
    layer_ref,
    gresid_ref,
    gmixed_ref,
    sums_ref,
    upsums_ref,
    gslab_ref,
    merge_ref,
    up_ref,
    down_ref,
    slope_ref,
    normed_ref,
    active_ref,
    ghidden_ref,
    gmlp_ref,
    gbranch_ref,
    split_ref,
    block_ref,
    sems,
    split_sems,
    block_sems,
):
    width = token_ref.shape[-1]
    hidden = up_ref.shape[1]
    step = pl.program_id(0)
    here = pl.ds(pl.multiple_of(step * MLP_TILE, MLP_TILE), MLP_TILE)
    copies = slab_copies(slab_ref, merge_ref, up_ref, down_ref, sems)

    def arrive(k):
        @pl.when(step == 0)
        def _():
            for copy in copies[k]:
                copy.wait()

    @pl.when(step == 0)
    def _():
        for group in copies:
            for copy in group:
                copy.start()
        sums_ref[...] = jnp.zeros_like(sums_ref)
        upsums_ref[...] = jnp.zeros_like(upsums_ref)

    arrive(0)
    resid = (
        token_ref[...].astype(F32) + dot(mixed_ref[here, :], merge_ref[...]) + outbias_ref[...]
    )
    unit, scale = norm_parts(resid)
    normed = (unit * gain_ref[...] + shift_ref[...]).astype(BF16)
    normed_ref[here, :] = normed
    arrive(1)
    cuts = [slice(c, c + MLP_CHUNK) for c in range(0, hidden, MLP_CHUNK)]
    result = resid + downbias_ref[...]
    for n, cols in enumerate(cuts):
        inner = dot(normed, up_ref[:, cols]) + upbias_ref[:, cols]
        square = inner * inner
        curve = jnp.tanh(0.7978845608028654 * (inner + 0.044715 * square * inner))
        half = 0.5 * (1.0 + curve)
        active = (half * inner).astype(BF16)
        active_ref[here, cols] = active
        slope_ref[:, cols] = half + 0.5 * inner * (1.0 - curve * curve) * (
            0.7978845608028654 * (1.0 + 3.0 * 0.044715 * square)
        )
        if n == 0:
            arrive(2)
        result += dot(active_ref[here, cols], down_ref[cols, :])
    layer_ref[...] = result.astype(BF16)
    error = result - teacher_ref[...].astype(F32)
    weight = weight_ref[...]
    sums_ref[4:5, :] += jnp.sum(weight * (error * error), 0, keepdims=True)
    gresult = error * (weight * factor_ref[0])
    gmlp = gresult.astype(BF16)
    gmlp_ref[here, :] = gmlp
    sums_ref[3:4, :] += jnp.sum(gmlp.astype(F32), 0, keepdims=True)
    gnormed = jnp.zeros_like(result)
    for cols in cuts:
        gactive = dot(gmlp, down_ref[cols, :], NT)
        ghidden = (gactive * slope_ref[:, cols]).astype(BF16)
        ghidden_ref[here, cols] = ghidden
        upsums_ref[0:1, cols] += jnp.sum(ghidden.astype(F32), 0, keepdims=True)
        gnormed += dot(ghidden_ref[here, cols], up_ref[:, cols], NT)
    sums_ref[1:2, :] += jnp.sum(gnormed * unit, 0, keepdims=True)
    sums_ref[2:3, :] += jnp.sum(gnormed, 0, keepdims=True)
    gresid = gresult + norm_back(gnormed, gain_ref[...], unit, scale)
    gresid_ref[...] = gresid
    gbranch = gresid.astype(BF16)
    gbranch_ref[here, :] = gbranch
    sums_ref[0:1, :] += jnp.sum(gbranch.astype(F32), 0, keepdims=True)
    gmixed_ref[...] = dot(gbranch, merge_ref[...], NT).astype(BF16)

    owners, rows, _ = split_ref.shape[1:]
    chunks = hidden // width
    share = owners // chunks

    def split_copy(index):
        return pltpu.make_async_copy(
            split_ref.at[index % 2],
            gslab_ref.at[:, pl.ds(pl.multiple_of(index * rows, 16), rows), :],
            split_sems.at[index % 2],
        )

    def block_copy(index):
        return pltpu.make_async_copy(
            block_ref.at[index % 2],
            gslab_ref.at[
                pl.ds(index * share, share), pl.ds((1 + chunks) * rows, chunks * rows), :
            ],
            block_sems.at[index % 2],
        )

    @pl.when(step == pl.num_programs(0) - 1)
    def _():
        out = dot(mixed_ref[...], gbranch_ref[...], TN).astype(BF16)
        split_ref[0] = out.reshape(owners, rows, width)
        split_copy(0).start()

        def ups(index, nothing):
            @pl.when(index >= 2)
            def _():
                split_copy(index - 2).wait()

            cols = pl.ds(pl.multiple_of((index - 1) * width, 128), width)
            out = dot(normed_ref[...], ghidden_ref[:, cols], TN).astype(BF16)
            split_ref[index % 2] = out.reshape(owners, rows, width)
            split_copy(index).start()
            return nothing

        lax.fori_loop(1, chunks + 1, ups, 0)

        def downs(index, nothing):
            @pl.when(index >= 2)
            def _():
                block_copy(index - 2).wait()

            cols = pl.ds(pl.multiple_of(index * width, 128), width)
            out = dot(active_ref[:, cols], gmlp_ref[...], TN).astype(BF16)
            block_ref[index % 2] = out.reshape(share, chunks * rows, width)
            block_copy(index).start()
            return nothing

        lax.fori_loop(0, chunks, downs, 0)
        split_copy(chunks - 1).wait()
        split_copy(chunks).wait()
        block_copy(chunks - 2).wait()
        block_copy(chunks - 1).wait()


def mlp(factor, mixed, tokens, teacher, weight, vectors, slab, extra):
    rows, width = tokens.shape
    outbias, gain, shift, upbias, downbias = vectors
    hidden = upbias.shape[1]
    chunks = hidden // width
    owners = slab.shape[0]
    few = width // owners
    tile = lambda n: pl.BlockSpec((MLP_TILE, n), lambda i: (i, 0))
    fixed = lambda m, n: pl.BlockSpec((m, n), lambda i: (0, 0))
    anywhere = pl.BlockSpec(memory_space=pl.ANY)
    shape = jax.ShapeDtypeStruct
    return pl.pallas_call(
        mlp_kernel,
        grid=(rows // MLP_TILE,),
        in_specs=[
            pl.BlockSpec(memory_space=pltpu.SMEM),
            fixed(rows, width),
            tile(width),
            tile(width),
            tile(1),
            fixed(1, width),
            fixed(1, width),
            fixed(1, width),
            fixed(1, hidden),
            fixed(1, width),
            anywhere,
        ],
        out_specs=[
            tile(width),
            tile(width),
            tile(width),
            fixed(8, width),
            fixed(8, hidden),
            anywhere,
        ],
        out_shape=[
            shape((rows, width), BF16),
            shape((rows, width), F32),
            shape((rows, width), BF16),
            shape((8, width), F32),
            shape((8, hidden), F32),
            shape((owners, (1 + 2 * chunks) * few + extra, width), BF16),
        ],
        scratch_shapes=[
            pltpu.VMEM((width, width), BF16),
            pltpu.VMEM((width, hidden), BF16),
            pltpu.VMEM((hidden, width), BF16),
            pltpu.VMEM((MLP_TILE, hidden), F32),
            pltpu.VMEM((rows, width), BF16),
            pltpu.VMEM((rows, hidden), BF16),
            pltpu.VMEM((rows, hidden), BF16),
            pltpu.VMEM((rows, width), BF16),
            pltpu.VMEM((rows, width), BF16),
            pltpu.VMEM((2, owners, few, width), BF16),
            pltpu.VMEM((2, owners // chunks, chunks * few, width), BF16),
            pltpu.SemaphoreType.DMA((3, owners * chunks)),
            pltpu.SemaphoreType.DMA((2,)),
            pltpu.SemaphoreType.DMA((2,)),
        ],
        compiler_params=pltpu.CompilerParams(vmem_limit_bytes=VMEM_LIMIT),
        cost_estimate=pl.CostEstimate(
            flops=6 * rows * width * (width + 2 * hidden),
            bytes_accessed=40 << 20,
            transcendentals=rows * hidden,
        ),
        name="mlp",
    )(factor, mixed, tokens, teacher, weight, outbias, gain, shift, upbias, downbias, slab)


def halo_back_kernel(
    low_ref,
    halo_any,
    grad_any,
    whole_any,
    out_any,
    sums_ref,
    halo_ref,
    grad_ref,
    out_ref,
    weight_ref,
    halo_sems,
    grad_sems,
    out_sems,
    sem,
):
    seqs, rows, width = halo_ref.shape
    tiles = rows // ROW_TILE
    weight = pltpu.make_async_copy(whole_any.at[:, pl.ds(width, 2 * width)], weight_ref, sem)
    weight.start()

    def arrive(seq, tile, at):
        return (
            pltpu.make_async_copy(
                halo_any.at[seq, at], halo_ref.at[seq, at], halo_sems.at[seq, tile]
            ),
            pltpu.make_async_copy(
                grad_any.at[seq, at], grad_ref.at[seq, at], grad_sems.at[seq, tile]
            ),
        )

    def leave(seq, tile, at):
        return pltpu.make_async_copy(
            out_ref.at[seq, at], out_any.at[seq, at], out_sems.at[seq, tile]
        )

    def begin(seq, tile, at):
        @pl.when(tile >= low_ref[seq])
        def _():
            for copy in arrive(seq, tile, at):
                copy.start()

        @pl.when(tile < low_ref[seq])
        def _():
            out_ref[seq, at, :] = jnp.zeros((ROW_TILE, width), BF16)
            leave(seq, tile, at).start()

    def work(seq, tile, at):
        for copy in arrive(seq, tile, at):
            copy.wait()
        grad = dot(grad_ref[seq, at, :], weight_ref[...], NT)
        unit, _ = norm_parts(halo_ref[seq, at, :].astype(F32))
        out_ref[seq, at, :] = grad.astype(BF16)
        leave(seq, tile, at).start()
        sums_ref[0:1, :] += jnp.sum(grad * unit, 0, keepdims=True)
        sums_ref[1:2, :] += jnp.sum(grad, 0, keepdims=True)

    def end(seq, tile, at):
        leave(seq, tile, at).wait()

    every_tile(low_ref, seqs, tiles, begin, every=True)
    sums_ref[...] = jnp.zeros_like(sums_ref)
    weight.wait()
    every_tile(low_ref, seqs, tiles, work)
    every_tile(low_ref, seqs, tiles, end, every=True)


def halo_back(low, halo, gkeyvalues, whole):
    seqs, rows, width = halo.shape
    tiles = rows // ROW_TILE
    anywhere = pl.BlockSpec(memory_space=pl.ANY)
    return pl.pallas_call(
        halo_back_kernel,
        grid_spec=pltpu.PrefetchScalarGridSpec(
            num_scalar_prefetch=1,
            grid=(1,),
            in_specs=[anywhere, anywhere, anywhere],
            out_specs=[anywhere, pl.BlockSpec((8, width), lambda i, low: (0, 0))],
            scratch_shapes=[
                pltpu.VMEM((seqs, rows, width), BF16),
                pltpu.VMEM((seqs, rows, 2 * width), BF16),
                pltpu.VMEM((seqs, rows, width), BF16),
                pltpu.VMEM((width, 2 * width), BF16),
                pltpu.SemaphoreType.DMA((seqs, tiles)),
                pltpu.SemaphoreType.DMA((seqs, tiles)),
                pltpu.SemaphoreType.DMA((seqs, tiles)),
                pltpu.SemaphoreType.DMA,
            ],
        ),
        out_shape=[
            jax.ShapeDtypeStruct((seqs, rows, width), BF16),
            jax.ShapeDtypeStruct((8, width), F32),
        ],
        compiler_params=pltpu.CompilerParams(vmem_limit_bytes=VMEM_LIMIT),
        cost_estimate=pl.CostEstimate(
            flops=4 << 30, bytes_accessed=16 << 20, transcendentals=0
        ),
        name="halo_back",
    )(low, halo, gkeyvalues, whole)


def own_back_kernel(
    low_ref,
    own_any,
    normed_any,
    gquery_any,
    gkeyvalue_any,
    whole_any,
    gnormed_any,
    gweight_any,
    sums_ref,
    own_ref,
    normed_ref,
    gquery_ref,
    gkeyvalue_ref,
    weight_ref,
    total_ref,
    gnormed_ref,
    gweight_ref,
    sems,
    out_sems,
):
    seqs, block, width = own_ref.shape
    halo = normed_ref.shape[1] - block
    tiles = halo // ROW_TILE
    here = pl.ds(halo, block)
    before = pl.ds(0, halo)
    first = [
        pltpu.make_async_copy(normed_any.at[:, here], normed_ref.at[:, here], sems.at[0]),
        pltpu.make_async_copy(gkeyvalue_any.at[:, here], gkeyvalue_ref.at[:, here], sems.at[1]),
        pltpu.make_async_copy(gquery_any, gquery_ref, sems.at[2]),
    ]
    later = [
        pltpu.make_async_copy(normed_any.at[:, before], normed_ref.at[:, before], sems.at[3]),
        pltpu.make_async_copy(gkeyvalue_any.at[:, before], gkeyvalue_ref.at[:, before], sems.at[4]),
    ]
    last = [
        pltpu.make_async_copy(whole_any, weight_ref, sems.at[5]),
        pltpu.make_async_copy(own_any, own_ref, sems.at[6]),
    ]
    for copy in first + later + last:
        copy.start()
    for copy in first:
        copy.wait()
    rows = seqs * block
    gweight_ref[:, :width] = dot(
        normed_ref[:, halo:, :].reshape(rows, width), gquery_ref[...].reshape(rows, width), TN
    ).astype(BF16)

    def whole(k, nothing):
        cols = pl.ds(pl.multiple_of(k * width, 128), width)
        total_ref[:, cols] = dot(
            normed_ref[:, halo:, :].reshape(rows, width),
            gkeyvalue_ref[:, halo:, cols].reshape(rows, width),
            TN,
        )
        return nothing

    lax.fori_loop(0, 2, whole, 0)
    sums_ref[...] = jnp.zeros_like(sums_ref)
    sums_ref[2:3, :] = jnp.sum(
        gquery_ref[...].reshape(rows, width).astype(F32), 0, keepdims=True
    )
    sums_ref[3:4, :] = jnp.sum(
        gkeyvalue_ref[:, halo:, width:].reshape(rows, width).astype(F32), 0, keepdims=True
    )
    for copy in later:
        copy.wait()

    def add(seq, tile, at):
        total_ref[...] += dot(normed_ref[seq, at, :], gkeyvalue_ref[seq, at, :], TN)
        sums_ref[3:4, :] += jnp.sum(gkeyvalue_ref[seq, at, width:].astype(F32), 0, keepdims=True)

    every_tile(low_ref, seqs, tiles, add)
    gweight_ref[:, width:] = total_ref[...].astype(BF16)
    send = pltpu.make_async_copy(gweight_ref, gweight_any, out_sems.at[0])
    send.start()
    for copy in last:
        copy.wait()

    def lead(seq, nothing):
        grad = dot(gquery_ref[seq], weight_ref[:, :width], NT)
        grad += dot(gkeyvalue_ref[seq, halo:, :], weight_ref[:, width:], NT)
        gnormed_ref[seq] = grad
        unit, _ = norm_parts(own_ref[seq].astype(F32))
        sums_ref[0:1, :] += jnp.sum(grad * unit, 0, keepdims=True)
        sums_ref[1:2, :] += jnp.sum(grad, 0, keepdims=True)
        return nothing

    lax.fori_loop(0, seqs, lead, 0)
    back = pltpu.make_async_copy(gnormed_ref, gnormed_any, out_sems.at[1])
    back.start()
    send.wait()
    back.wait()


def own_back(low, own, normed, gquery, gkeyvalues, whole):
    seqs, block, width = own.shape
    length = normed.shape[1]
    anywhere = pl.BlockSpec(memory_space=pl.ANY)
    return pl.pallas_call(
        own_back_kernel,
        grid_spec=pltpu.PrefetchScalarGridSpec(
            num_scalar_prefetch=1,
            grid=(1,),
            in_specs=[anywhere] * 5,
            out_specs=[anywhere, anywhere, pl.BlockSpec((8, width), lambda i, low: (0, 0))],
            scratch_shapes=[
                pltpu.VMEM((seqs, block, width), BF16),
                pltpu.VMEM((seqs, length, width), BF16),
                pltpu.VMEM((seqs, block, width), BF16),
                pltpu.VMEM((seqs, length, 2 * width), BF16),
                pltpu.VMEM((width, 3 * width), BF16),
                pltpu.VMEM((width, 2 * width), F32),
                pltpu.VMEM((seqs, block, width), F32),
                pltpu.VMEM((width, 3 * width), BF16),
                pltpu.SemaphoreType.DMA((7,)),
                pltpu.SemaphoreType.DMA((2,)),
            ],
        ),
        out_shape=[
            jax.ShapeDtypeStruct((seqs, block, width), F32),
            jax.ShapeDtypeStruct((width, 3 * width), BF16),
            jax.ShapeDtypeStruct((8, width), F32),
        ],
        compiler_params=pltpu.CompilerParams(vmem_limit_bytes=VMEM_LIMIT),
        cost_estimate=pl.CostEstimate(
            flops=16 << 30, bytes_accessed=24 << 20, transcendentals=0
        ),
        name="own_back",
    )(low, own, normed, gquery, gkeyvalues, whole)


def finish_kernel(seqs, own_ref, gnormed_ref, gresid_ref, gain_ref, *rest):
    near_refs, far_refs = rest[:seqs], rest[seqs:-2]
    out_ref, total_ref = rest[-2:]
    unit, scale = norm_parts(own_ref[0].astype(F32))
    for seq, near_ref in enumerate(near_refs):

        @pl.when(pl.program_id(0) == seq)
        def _():
            total_ref[...] = gnormed_ref[0] + near_ref[...].astype(F32)

    for far_ref in far_refs:

        @pl.when(pl.program_id(1) == pl.num_programs(1) - 1)
        def _():
            total_ref[-HALO_CHUNK:, :] += far_ref[0].astype(F32)

    out_ref[0] = (gresid_ref[0] + norm_back(total_ref[...], gain_ref[...], unit, scale)).astype(BF16)


def finish(own, gnormed, near, far, gresid, gain):
    seqs, block, width = own.shape
    tile = pl.BlockSpec((1, ROW_TILE, width), lambda s, t: (s, t, 0))
    last = pl.BlockSpec((1, HALO_CHUNK, width), lambda s, t: (s, 0, 0))
    return pl.pallas_call(
        functools.partial(finish_kernel, seqs),
        grid=(seqs, block // ROW_TILE),
        in_specs=[tile, tile, tile, pl.BlockSpec((1, width), lambda s, t: (0, 0))]
        + [pl.BlockSpec((ROW_TILE, width), lambda s, t: (t, 0))] * seqs
        + [last] * len(far),
        out_specs=tile,
        out_shape=jax.ShapeDtypeStruct(own.shape, BF16),
        scratch_shapes=[pltpu.VMEM((ROW_TILE, width), F32)],
        cost_estimate=pl.CostEstimate(
            flops=20 * seqs * block * width,
            bytes_accessed=14 * seqs * block * width,
            transcendentals=0,
        ),
        name="finish",
    )(own, gnormed, gresid, gain, *near, *far)


def swap(x, axis, bit):
    size = lax.axis_size(axis)
    return lax.ppermute(x, axis, [(i, i ^ bit) for i in range(size)])


def shift(x, axis, step):
    size = lax.axis_size(axis)
    return lax.ppermute(
        x, axis, [(i, i + step) for i in range(size) if 0 <= i + step < size]
    )


def sum_over(x, axis):
    bit = 1
    while bit < lax.axis_size(axis):
        x = x + swap(x, axis, bit)
        bit *= 2
    return x


def max_over(x, axis):
    bit = 1
    while bit < lax.axis_size(axis):
        x = jnp.maximum(x, swap(x, axis, bit))
        bit *= 2
    return x


def gather_near(shard):
    size = lax.axis_size("fsdp")
    if size != 8:
        return [lax.all_gather(shard, "fsdp", axis=0, tiled=True)]
    return [shard] + [swap(shard, "fsdp", 2 * d) for d in range(1, size // 2)]


def gather_rest(near):
    if lax.axis_size("fsdp") != 8:
        return near
    return near + [swap(piece, "fsdp", 1) for piece in near]


def piece_order():
    size = lax.axis_size("fsdp")
    me = lax.axis_index("fsdp").astype(jnp.int32)
    if size != 8:
        return jnp.zeros((1,), jnp.int32)
    return jnp.stack(
        [me ^ (2 * d) for d in range(size // 2)] + [me ^ (2 * d) ^ 1 for d in range(size // 2)]
    )


def sum_seq(total):
    if lax.axis_size("seq") != 4:
        return lax.psum(total, "seq")
    return sum_seq_rest(sum_seq_first(total))


def sum_seq_first(total):
    rows, columns = total.shape
    odd = lax.axis_index("seq") % 2
    halves = total.reshape(2, rows // 2, columns)
    pick = lambda k: lax.dynamic_index_in_dim(halves, k, 0, keepdims=False)
    return (pick(odd).astype(F32) + swap(pick(1 - odd), "seq", 1).astype(F32)).astype(BF16)


def sum_seq_rest(half):
    odd = lax.axis_index("seq") % 2
    half = (half.astype(F32) + swap(half, "seq", 2).astype(F32)).astype(BF16)
    back = swap(half, "seq", 1)
    return jnp.where(
        odd == 0, jnp.concatenate([half, back], 0), jnp.concatenate([back, half], 0)
    )


def reduce_rows(parts, extra, *first):
    size = lax.axis_size("fsdp")
    me = lax.axis_index("fsdp")
    if size != 8:
        parts = jnp.concatenate([parts, extra], 1)
        total = lax.psum_scatter(parts, "fsdp", scatter_dimension=0, tiled=False)
        return lax.psum(total, "seq"), *first
    rows, columns = parts.shape[1:]
    few = extra.shape[1]
    core = me % 2
    chip = me // 2
    pick = lambda a, k, ax: lax.dynamic_index_in_dim(a, k, ax, keepdims=False)
    parts = parts.reshape(size // 2, 2, rows, columns)
    extra = extra.reshape(size // 2, 2, few, columns)
    half = lambda k: jnp.concatenate([pick(parts, k, 1), pick(extra, k, 1)], 1)
    other = swap(half(1 - core), "fsdp", 1)
    mine = (half(core).astype(F32) + other.astype(F32)).astype(BF16)
    arrived = [
        swap(pick(mine, chip ^ d, 0), "fsdp", 2 * d) for d in range(1, size // 2)
    ]
    arrived, *first = lax.optimization_barrier((arrived, *first))
    total = pick(mine, chip, 0).astype(F32)
    for part in arrived:
        total = total + part.astype(F32)
    return sum_seq(total.astype(BF16)), *first


def gather_slab(outweight, fcweight, projweight, *first):
    width = outweight.shape[1]
    cuts = fcweight.shape[1] // width

    def join(out, up, down, axis):
        ups = [lax.slice_in_dim(up, c * width, (c + 1) * width, axis=-1) for c in range(cuts)]
        return jnp.concatenate([out, *ups, down], axis)

    if lax.axis_size("fsdp") == SHARES:
        slab = join(outweight, fcweight, projweight, 0)
        slab, *first = lax.optimization_barrier((slab, *first))
        return lax.all_gather(slab, "fsdp", axis=0, tiled=False), *first
    whole = [
        lax.all_gather(w, "fsdp", axis=0, tiled=True) for w in (outweight, fcweight, projweight)
    ]
    return join(*(w.reshape(SHARES, -1, w.shape[1]) for w in whole), 1), *first


def reduce_slab(slab, width, hidden):
    owners = lax.axis_size("fsdp")
    cuts = hidden // width
    rows = width // SHARES

    def part(array, axis):
        at = lambda a, b: lax.slice_in_dim(array, a * rows, b * rows, axis=axis)
        ups = [at(1 + c, 2 + c) for c in range(cuts)]
        rest = lax.slice_in_dim(array, (1 + 2 * cuts) * rows, array.shape[axis], axis=axis)
        return at(0, 1), jnp.concatenate(ups, -1), at(1 + cuts, 1 + 2 * cuts), rest

    if owners == SHARES:
        return part(slab.astype(F32), 0)
    *grads, rest = part(slab, 1)
    grads = [
        lax.psum(
            lax.psum_scatter(
                g.reshape(-1, g.shape[-1]), "fsdp", scatter_dimension=0, tiled=True
            ),
            "seq",
        ).astype(F32)
        for g in grads
    ]
    rest = lax.psum(rest.astype(F32), ("fsdp", "seq"))
    return *grads, rest


def local(
    tokens,
    teacher,
    segment_ids,
    latent_flags,
    valid_mask,
    attngain,
    attnshift,
    qkvweight,
    qvbias,
    outweight,
    outbias,
    mlpgain,
    mlpshift,
    fcweight,
    fcbias,
    projweight,
    projbias,
):
    seqs, block, width = tokens.shape
    groups = lax.axis_size("seq")
    owners = lax.axis_size("fsdp")
    rows = seqs * block
    halo_rows = (groups - 1) * block
    far_rows = halo_rows - block
    me = lax.axis_index("fsdp")
    place = lax.axis_index("seq").astype(jnp.int32)
    hidden = fcweight.shape[1]

    order = piece_order()
    qkv_pieces = gather_near(qkvweight)

    weight = (valid_mask * (1 - latent_flags)).astype(F32)
    below = jnp.sum(
        (segment_ids[:, :, None] < jnp.arange(1, 4, dtype=jnp.int32)).astype(jnp.int32), 1
    )
    facts = jnp.concatenate([below.reshape(-1), jnp.sum(weight).astype(jnp.int32)[None]])
    facts = sum_over(facts, "seq")
    bounds = facts[:-1].reshape(seqs, 3)

    sent, facts = lax.optimization_barrier((tokens, facts))
    near = [shift(sent[s], "seq", 1) for s in range(seqs)]
    far = shift(sent[:, block - HALO_CHUNK :], "seq", 2) if far_rows > 0 else None

    def start_of(positions):
        found = jnp.zeros((seqs,) + positions.shape, jnp.int32)
        for d in range(3):
            bound = bounds[:, d].reshape((seqs,) + (1,) * positions.ndim)
            found = jnp.maximum(found, jnp.where(bound <= positions[None], bound, 0))
        return found

    firsts = jnp.arange(groups, dtype=jnp.int32) * block
    reach = jnp.max(firsts[None] - start_of(firsts)) - block
    chunks = jnp.maximum(reach + HALO_CHUNK - 1, 0) // HALO_CHUNK

    shards = [attngain, attnshift, qvbias, outbias, mlpgain, mlpshift, fcbias, projbias]
    packed = jnp.concatenate(shards).astype(F32)
    table = jnp.where(
        lax.broadcasted_iota(jnp.int32, (owners, packed.shape[0]), 0) == me,
        packed[None],
        0.0,
    )
    line = lax.broadcasted_iota(jnp.int32, (8, packed.shape[0]), 0)
    table = jnp.concatenate(
        [
            table,
            jnp.where(line == 0, facts[-1].astype(F32), jnp.where(line == 1, chunks.astype(F32), 0.0)),
        ],
        0,
    )
    is_reach = lax.broadcasted_iota(jnp.int32, table.shape, 0) == owners + 1
    bit = 1
    while bit < owners:
        other = swap(table, "fsdp", bit)
        table = jnp.where(is_reach, jnp.maximum(table, other), table + other)
        bit *= 2
    qkv_pieces = gather_rest(qkv_pieces)
    slab, qkv_pieces, table, near[0] = gather_slab(
        outweight, fcweight, projweight, qkv_pieces, table, near[0]
    )

    count = table[owners, 0]
    chunks = table[owners + 1, 0].astype(jnp.int32)
    vectors = []
    at = 0
    for shard in shards:
        size = shard.shape[0]
        vectors.append(table[:owners, at : at + size].reshape(1, size * owners))
        at += size
    gain1, shift1, bias1, outbias_v, gain2, shift2, upbias, downbias = vectors


    base = (place - (groups - 1)) * block
    starts = start_of(place * block + jnp.arange(block, dtype=jnp.int32)) - base
    low_rows = starts[:, ::QUERY_TILE]
    low = (low_rows // KEY_TILE).reshape(-1)
    low_tile = starts[:, 0] // ROW_TILE
    first = low_tile * (ROW_TILE // KEY_TILE)
    starts = starts[:, None, :]

    bias1 = jnp.concatenate([bias1[:, :width], jnp.zeros((1, width), F32), bias1[:, width:]], 1)
    normed, query, keyvalues, qkv = project_own(
        order, tokens, gain1, shift1, bias1, qkv_pieces, halo_rows + block
    )
    halo = jnp.stack(near)
    if far_rows > 0:
        blank = jnp.zeros((seqs, far_rows - HALO_CHUNK, width), BF16)
        halo = jnp.concatenate([blank, far, halo], 1)

    def fetch(state):
        j, halo = state
        sent = lax.dynamic_slice_in_dim(halo, halo_rows - HALO_CHUNK * (j + 1), HALO_CHUNK, 1)
        came = shift(sent, "seq", 1)
        return j + 1, lax.dynamic_update_slice_in_dim(
            halo, came, far_rows - HALO_CHUNK * (j + 1), 1
        )

    if far_rows > 0:
        _, halo = lax.while_loop(lambda state: state[0] < chunks, fetch, (jnp.int32(1), halo))

    normed, keyvalues = project_halo(
        low_tile, halo, gain1, shift1, bias1, qkv, normed, keyvalues
    )
    mixed, logs = attend(low, query, keyvalues, starts)

    factor = (rows * owners * groups) / count
    layer_out, gresid, gmixed, sums, upsums, outer = mlp(
        factor.reshape(1),
        mixed.reshape(rows, width),
        tokens.reshape(rows, width),
        teacher.reshape(rows, width),
        weight.reshape(rows, 1),
        (outbias_v, gain2, shift2, upbias, downbias),
        slab,
        SMALL_ROWS,
    )

    small = jnp.concatenate(
        [upsums[0].reshape(SHARES, -1)] + [sums[k].reshape(SHARES, -1) for k in range(4)], 1
    )
    line = lax.broadcasted_iota(jnp.int32, (SHARES, SMALL_ROWS, width), 1)
    small = jnp.where(line == 0, small[:, None, :], jnp.where(line == 1, sums[4], 0.0))
    outer = lax.dynamic_update_slice_in_dim(
        outer, small.astype(BF16), outer.shape[1] - SMALL_ROWS, 1
    )
    outer, gmixed = lax.optimization_barrier((outer, gmixed))
    staged = owners == SHARES and groups == 4
    if owners == SHARES:
        outer = lax.psum_scatter(outer, "fsdp", scatter_dimension=0, tiled=False)
        outer = sum_seq_first(outer) if staged else sum_seq(outer)

    gquery, gkeyvalues = attend_back(
        low, first, query, keyvalues, starts, mixed, gmixed.reshape(seqs, block, width), logs
    )
    ghalo, halo_sums = halo_back(low_tile, halo, gkeyvalues, qkv)

    def give(state):
        j, ghalo = state
        j = j - 1
        sent = lax.dynamic_slice_in_dim(ghalo, far_rows - HALO_CHUNK * (j + 1), HALO_CHUNK, 1)
        came = shift(sent, "seq", -1)
        spot = halo_rows - HALO_CHUNK * (j + 1)
        held = lax.dynamic_slice_in_dim(ghalo, spot, HALO_CHUNK, 1)
        total = (held.astype(F32) + came.astype(F32)).astype(BF16)
        return j, lax.dynamic_update_slice_in_dim(ghalo, total, spot, 1)

    if far_rows > 0:
        _, ghalo = lax.while_loop(lambda state: state[0] > 1, give, (chunks, ghalo))

    ghalo, gquery = lax.optimization_barrier((ghalo, gquery))
    near = [shift(ghalo[s, far_rows:], "seq", -1) for s in range(seqs)]
    far = []
    if far_rows > 0:
        far = [shift(ghalo[:, far_rows - HALO_CHUNK : far_rows], "seq", -2)]
    gnormed, gweight, own_sums = own_back(
        low_tile, tokens, normed, gquery, gkeyvalues, qkv
    )
    late = jnp.concatenate(
        [(own_sums[k] + halo_sums[k]).reshape(owners, -1) for k in range(2)]
        + [own_sums[2:4].reshape(owners, -1)],
        1,
    ).astype(BF16)
    late = jnp.pad(late, ((0, 0), (0, 2 * width + width - late.shape[1])))
    line = lax.broadcasted_iota(jnp.int32, (owners, 16, 3 * width), 1)
    late = jnp.where(line == 0, late[:, None, :], jnp.zeros((), BF16))
    gweight, near[0] = lax.optimization_barrier((gweight, near[0]))
    grad_tokens = finish(
        tokens,
        gnormed,
        near,
        far,
        gresid.reshape(tokens.shape),
        gain1,
    )

    joint, outer, grad_tokens = reduce_rows(
        gweight.reshape(owners, width // owners, 3 * width), late, outer, grad_tokens
    )
    joint = joint.astype(F32)
    if staged:
        outer = sum_seq_rest(outer)
    grad_merge, grad_up, grad_down, small = reduce_slab(outer, width, hidden)

    share = width // owners
    if owners == SHARES:
        at = hidden // owners
        cuts = [small[0, :at]] + [
            small[0, at + k * share : at + (k + 1) * share] for k in range(4)
        ]
        loss_row = small[1]
    else:
        at = hidden // SHARES
        wide = width // SHARES
        full = [small[:, 0, :at].reshape(-1)] + [
            small[:, 0, at + k * wide : at + (k + 1) * wide].reshape(-1) for k in range(4)
        ]
        cuts = [
            lax.dynamic_slice_in_dim(v, me * (v.shape[0] // owners), v.shape[0] // owners)
            for v in full
        ]
        loss_row = small[0, 1]
    loss = jnp.sum(loss_row) / (width * count)
    return (
        loss,
        layer_out.reshape(tokens.shape),
        grad_tokens,
        joint[share, :share],
        joint[share, share : 2 * share],
        joint[:share],
        joint[share, 2 * share : 4 * share],
        grad_merge,
        cuts[1],
        cuts[2],
        cuts[3],
        grad_up,
        cuts[0],
        grad_down,
        cuts[4],
    )


def solution(mesh):
    placed = (
        P("fsdp", "seq", None),
        P("fsdp", "seq", None),
        P("fsdp", "seq"),
        P("fsdp", "seq"),
        P("fsdp", "seq"),
        P("fsdp"),
        P("fsdp"),
        P("fsdp", None),
        P("fsdp"),
        P("fsdp", None),
        P("fsdp"),
        P("fsdp"),
        P("fsdp"),
        P("fsdp", None),
        P("fsdp"),
        P("fsdp", None),
        P("fsdp"),
    )
    return jax.shard_map(
        local,
        mesh=mesh,
        in_specs=placed,
        out_specs=(
            P(),
            P("fsdp", "seq", None),
            P("fsdp", "seq", None),
            P("fsdp"),
            P("fsdp"),
            P("fsdp", None),
            P("fsdp"),
            P("fsdp", None),
            P("fsdp"),
            P("fsdp"),
            P("fsdp"),
            P("fsdp", None),
            P("fsdp"),
            P("fsdp", None),
            P("fsdp"),
        ),
        check_vma=False,
    )
```

```python
import functools

import jax
import jax.numpy as jnp
from jax import lax
from jax.experimental import pallas as pl
from jax.experimental.pallas import tpu as pltpu
from jax.sharding import PartitionSpec as P

H = 12
HD = 64
PAIR = 2 * HD
EPSILON = 1e-05
KEY_TILE = 128
QUERY_TILE = 128
ROW_TILE = 256
MLP_TILE = 256
MLP_CHUNK = 1536
HALO_CHUNK = 128
SHARES = 8
SMALL_ROWS = 16
VMEM_LIMIT = 62 * 1024 * 1024

NT = (((1,), (1,)), ((), ()))
NN = (((1,), (0,)), ((), ()))
TN = (((0,), (0,)), ((), ()))
F32 = jnp.float32
BF16 = jnp.bfloat16


def dot(left, right, dims=NN):
    return lax.dot_general(left, right, dims, preferred_element_type=F32)


def norm_parts(values):
    center = values - jnp.mean(values, -1, keepdims=True)
    spread = jnp.mean(center * center, -1, keepdims=True)
    scale = lax.rsqrt(spread + EPSILON)
    return center * scale, scale


def norm_back(grad, gain, unit, scale):
    weighted = grad * gain
    first = jnp.mean(weighted, -1, keepdims=True)
    second = jnp.mean(weighted * unit, -1, keepdims=True)
    return scale * (weighted - first - unit * second)


def piece_copies(order_ref, pieces, whole_ref, sems):
    copies = []
    for place, piece in enumerate(pieces):
        rows = piece.shape[0]
        if len(pieces) == 1:
            target = whole_ref
        else:
            target = whole_ref.at[pl.ds(pl.multiple_of(order_ref[place] * rows, 16), rows), :]
        copies.append(pltpu.make_async_copy(piece, target, sems.at[place]))
    return copies


def project_own_kernel(count, order_ref, own_ref, gain_ref, shift_ref, bias_ref, *rest):
    pieces = rest[:count]
    normed_ref, query_ref, keyvalue_ref, whole_ref, weight_ref, sems, whole_sem = rest[count:]
    width = own_ref.shape[-1]
    seq = pl.program_id(0)
    whole = pltpu.make_async_copy(weight_ref, whole_ref, whole_sem)

    @pl.when(seq == 0)
    def _():
        copies = piece_copies(order_ref, pieces, weight_ref, sems)
        for copy in copies:
            copy.start()
        for copy in copies:
            copy.wait()
        whole.start()

    unit, _ = norm_parts(own_ref[0].astype(F32))
    normed = (unit * gain_ref[...] + shift_ref[...]).astype(BF16)
    normed_ref[0] = normed
    joint = (dot(normed, weight_ref[...]) + bias_ref[...]).astype(BF16)
    query_ref[0] = joint[:, :width]
    keyvalue_ref[0] = joint[:, width:]

    @pl.when(seq == pl.num_programs(0) - 1)
    def _():
        whole.wait()


def project_own(order, own, gain, shift, bias, pieces, length):
    seqs, block, width = own.shape
    last = length // block - 1
    fixed = lambda s, order: (0, 0)
    spot = lambda s, order: (s, 0, 0)
    end = lambda s, order: (s, last, 0)
    return pl.pallas_call(
        functools.partial(project_own_kernel, len(pieces)),
        grid_spec=pltpu.PrefetchScalarGridSpec(
            num_scalar_prefetch=1,
            grid=(seqs,),
            in_specs=[
                pl.BlockSpec((1, block, width), spot),
                pl.BlockSpec((1, width), fixed),
                pl.BlockSpec((1, width), fixed),
                pl.BlockSpec((1, 3 * width), fixed),
            ]
            + [pl.BlockSpec(memory_space=pl.ANY)] * len(pieces),
            out_specs=[
                pl.BlockSpec((1, block, width), end),
                pl.BlockSpec((1, block, width), spot),
                pl.BlockSpec((1, block, 2 * width), end),
                pl.BlockSpec(memory_space=pl.ANY),
            ],
            scratch_shapes=[
                pltpu.VMEM((width, 3 * width), BF16),
                pltpu.SemaphoreType.DMA((len(pieces),)),
                pltpu.SemaphoreType.DMA,
            ],
        ),
        out_shape=[
            jax.ShapeDtypeStruct((seqs, length, width), BF16),
            jax.ShapeDtypeStruct((seqs, block, width), BF16),
            jax.ShapeDtypeStruct((seqs, length, 2 * width), BF16),
            jax.ShapeDtypeStruct((width, 3 * width), BF16),
        ],
        compiler_params=pltpu.CompilerParams(vmem_limit_bytes=VMEM_LIMIT),
        cost_estimate=pl.CostEstimate(
            flops=6 * seqs * block * width * width, bytes_accessed=16 << 20, transcendentals=0
        ),
        name="project_own",
    )(order, own, gain, shift, bias, *pieces)


def every_tile(low_ref, seqs, tiles, work, every=False):
    for seq in range(seqs):

        def one(tile, nothing):
            work(seq, tile, pl.ds(pl.multiple_of(tile * ROW_TILE, ROW_TILE), ROW_TILE))
            return nothing

        lax.fori_loop(0 if every else low_ref[seq], tiles, one, 0)


def project_halo_kernel(
    low_ref, gain_ref, shift_ref, bias_ref, halo_any, whole_any, *rest
):
    (
        normed_any,
        keyvalue_any,
        halo_ref,
        normed_ref,
        keyvalue_ref,
        weight_ref,
        in_sems,
        normed_sems,
        keyvalue_sems,
        sem,
    ) = rest[2:]
    seqs, rows, width = halo_ref.shape
    tiles = rows // ROW_TILE
    weight = pltpu.make_async_copy(whole_any.at[:, pl.ds(width, 2 * width)], weight_ref, sem)
    weight.start()

    def arrive(seq, tile, at):
        return pltpu.make_async_copy(
            halo_any.at[seq, at], halo_ref.at[seq, at], in_sems.at[seq, tile]
        )

    def leave(seq, tile, at):
        return (
            pltpu.make_async_copy(
                normed_ref.at[seq, at], normed_any.at[seq, at], normed_sems.at[seq, tile]
            ),
            pltpu.make_async_copy(
                keyvalue_ref.at[seq, at], keyvalue_any.at[seq, at], keyvalue_sems.at[seq, tile]
            ),
        )

    def begin(seq, tile, at):
        arrive(seq, tile, at).start()

    def work(seq, tile, at):
        arrive(seq, tile, at).wait()
        unit, _ = norm_parts(halo_ref[seq, at, :].astype(F32))
        normed = (unit * gain_ref[...] + shift_ref[...]).astype(BF16)
        normed_ref[seq, at, :] = normed
        keyvalue_ref[seq, at, :] = (
            dot(normed, weight_ref[...]) + bias_ref[:, width:]
        ).astype(BF16)
        for copy in leave(seq, tile, at):
            copy.start()

    def end(seq, tile, at):
        for copy in leave(seq, tile, at):
            copy.wait()

    every_tile(low_ref, seqs, tiles, begin)
    weight.wait()
    every_tile(low_ref, seqs, tiles, work)
    every_tile(low_ref, seqs, tiles, end)


def project_halo(low, halo, gain, shift, bias, whole, normed, keyvalues):
    seqs, rows, width = halo.shape
    tiles = rows // ROW_TILE
    fixed = lambda i, low: (0, 0)
    anywhere = pl.BlockSpec(memory_space=pl.ANY)
    return pl.pallas_call(
        project_halo_kernel,
        grid_spec=pltpu.PrefetchScalarGridSpec(
            num_scalar_prefetch=1,
            grid=(1,),
            in_specs=[
                pl.BlockSpec((1, width), fixed),
                pl.BlockSpec((1, width), fixed),
                pl.BlockSpec((1, 3 * width), fixed),
                anywhere,
                anywhere,
                anywhere,
                anywhere,
            ],
            out_specs=[anywhere, anywhere],
            scratch_shapes=[
                pltpu.VMEM((seqs, rows, width), BF16),
                pltpu.VMEM((seqs, rows, width), BF16),
                pltpu.VMEM((seqs, rows, 2 * width), BF16),
                pltpu.VMEM((width, 2 * width), BF16),
                pltpu.SemaphoreType.DMA((seqs, tiles)),
                pltpu.SemaphoreType.DMA((seqs, tiles)),
                pltpu.SemaphoreType.DMA((seqs, tiles)),
                pltpu.SemaphoreType.DMA,
            ],
        ),
        out_shape=[
            jax.ShapeDtypeStruct(normed.shape, BF16),
            jax.ShapeDtypeStruct(keyvalues.shape, BF16),
        ],
        input_output_aliases={6: 0, 7: 1},
        compiler_params=pltpu.CompilerParams(vmem_limit_bytes=VMEM_LIMIT),
        cost_estimate=pl.CostEstimate(
            flops=2 * seqs * rows * width * width, bytes_accessed=16 << 20, transcendentals=0
        ),
        name="project_halo",
    )(low, gain, shift, bias, halo, whole, normed, keyvalues)


def two_heads(tile):
    left = lax.broadcasted_iota(jnp.int32, tile.shape, 1) < HD
    zero = jnp.zeros_like(tile)
    return jnp.concatenate([jnp.where(left, tile, zero), jnp.where(left, zero, tile)], 0)


def visible(first_key, starts, first_query):
    shape = (KEY_TILE, starts.shape[1])
    keys = first_key + lax.broadcasted_iota(jnp.int32, shape, 0)
    queries = first_query + lax.broadcasted_iota(jnp.int32, shape, 1)
    return (keys >= starts) & (keys <= queries)


def head_rows(first, second):
    shape = (HD, first.shape[1])
    return jnp.concatenate(
        [jnp.broadcast_to(first, shape), jnp.broadcast_to(second, shape)], 0
    )


def attend_kernel(halo, low_ref, query_ref, keyvalue_ref, start_ref, out_ref, log_ref):
    seq = pl.program_id(0)
    block = query_ref.shape[1]
    width = query_ref.shape[2]
    pairs = width // PAIR
    after = lambda c: slice(width + c.start, width + c.stop)
    tiles = block // QUERY_TILE
    def rows(tile, nothing):
        here = pl.ds(pl.multiple_of(tile * QUERY_TILE, QUERY_TILE), QUERY_TILE)
        starts = start_ref[0, :, here]
        cols = [slice(p * PAIR, (p + 1) * PAIR) for p in range(pairs)]

        def step(j, carry):
            place = pl.ds(pl.multiple_of(j * KEY_TILE, KEY_TILE), KEY_TILE)
            ok = visible(j * KEY_TILE, starts, halo + tile * QUERY_TILE)
            scores = [
                dot(two_heads(keyvalue_ref[0, place, c]), query_ref[0, here, c] * 0.125, NT)
                for c in cols
            ]
            left = []
            for p in range(pairs):
                highs, totals, mixed = carry[3 * p : 3 * p + 3]
                powers, fades, sums, nexts = [], [], [], []
                for h in range(2):
                    part = jnp.where(ok, scores[p][h * KEY_TILE : (h + 1) * KEY_TILE], -1e30)
                    high = highs[h : h + 1]
                    later = jnp.maximum(high, jnp.max(part, 0, keepdims=True))
                    power = jnp.exp(part - later)
                    fade = jnp.exp(high - later)
                    sums.append(totals[h : h + 1] * fade + jnp.sum(power, 0, keepdims=True))
                    powers.append(power.astype(BF16))
                    fades.append(fade)
                    nexts.append(later)
                added = dot(
                    two_heads(keyvalue_ref[0, place, after(cols[p])]), jnp.concatenate(powers, 0), TN
                )
                left += [
                    jnp.concatenate(nexts, 0),
                    jnp.concatenate(sums, 0),
                    mixed * head_rows(*fades) + added,
                ]
            return tuple(left)

        row = jnp.zeros((2, QUERY_TILE), F32)
        done = lax.fori_loop(
            low_ref[seq * tiles + tile],
            (halo + (tile + 1) * QUERY_TILE) // KEY_TILE,
            step,
            (row - 1e30, row, jnp.zeros((PAIR, QUERY_TILE), F32)) * pairs,
        )
        for p in range(pairs):
            highs, totals, mixed = done[3 * p : 3 * p + 3]
            total = head_rows(totals[0:1], totals[1:2])
            out_ref[0, here, cols[p]] = jnp.transpose(mixed / total).astype(BF16)
            log_ref[0, p, :, here] = highs + jnp.log(totals)
        return nothing

    lax.fori_loop(0, tiles, rows, 0)


def attend(low, query, keyvalues, starts):
    seqs, block, width = query.shape
    length = keyvalues.shape[1]
    pairs = width // PAIR
    rows = pl.BlockSpec((1, block, width), lambda s, low: (s, 0, 0))
    full = pl.BlockSpec((1, length, 2 * width), lambda s, low: (s, 0, 0))
    return pl.pallas_call(
        functools.partial(attend_kernel, length - block),
        grid_spec=pltpu.PrefetchScalarGridSpec(
            num_scalar_prefetch=1,
            grid=(seqs,),
            in_specs=[rows, full, pl.BlockSpec((1, 1, block), lambda s, low: (s, 0, 0))],
            out_specs=[rows, pl.BlockSpec((1, pairs, 2, block), lambda s, low: (s, 0, 0, 0))],
        ),
        out_shape=[
            jax.ShapeDtypeStruct((seqs, block, width), BF16),
            jax.ShapeDtypeStruct((seqs, pairs, 2, block), F32),
        ],
        compiler_params=pltpu.CompilerParams(vmem_limit_bytes=VMEM_LIMIT),
        cost_estimate=pl.CostEstimate(
            flops=16 << 30, bytes_accessed=16 << 20, transcendentals=8 << 20
        ),
        name="attend",
    )(low, query, keyvalues, starts)


def attend_back_kernel(
    halo,
    low_ref,
    first_ref,
    query_ref,
    keyvalue_ref,
    start_ref,
    out_ref,
    grad_ref,
    log_ref,
    gquery_ref,
    gkeyvalue_ref,
    turned_ref,
    center_ref,
    sumk_ref,
    sumv_ref,
):
    seq = pl.program_id(0)
    block = query_ref.shape[1]
    width = query_ref.shape[2]
    pairs = width // PAIR
    after = lambda c: slice(width + c.start, width + c.stop)
    tiles = block // QUERY_TILE
    cols = [slice(p * PAIR, (p + 1) * PAIR) for p in range(pairs)]
    turned_ref[...] = jnp.zeros_like(turned_ref)
    for p in range(pairs):
        products = jnp.transpose(grad_ref[0, :, cols[p]].astype(F32) * out_ref[0, :, cols[p]].astype(F32))
        center_ref[p, 0:1, :] = jnp.sum(products[:HD], 0, keepdims=True)
        center_ref[p, 1:2, :] = jnp.sum(products[HD:], 0, keepdims=True)
    left = lax.broadcasted_iota(jnp.int32, (KEY_TILE, PAIR), 1) < HD

    def step(j, nothing):
        place = pl.ds(pl.multiple_of(j * KEY_TILE, KEY_TILE), KEY_TILE)
        sumk_ref[...] = jnp.zeros_like(sumk_ref)
        sumv_ref[...] = jnp.zeros_like(sumv_ref)
        def rows(tile, nothing):
            here = pl.ds(pl.multiple_of(tile * QUERY_TILE, QUERY_TILE), QUERY_TILE)
            last = (halo + (tile + 1) * QUERY_TILE) // KEY_TILE

            @pl.when((j >= low_ref[seq * tiles + tile]) & (j < last))
            def _():
                ok = visible(j * KEY_TILE, start_ref[0, :, here], halo + tile * QUERY_TILE)
                keys = [two_heads(keyvalue_ref[0, place, c]) for c in cols]
                queries = [query_ref[0, here, c] * 0.125 for c in cols]
                grads = [grad_ref[0, here, c] for c in cols]
                scores = [dot(k, q, NT) for k, q in zip(keys, queries)]
                gprobs = [
                    dot(two_heads(keyvalue_ref[0, place, after(c)]), g, NT) for c, g in zip(cols, grads)
                ]
                for p in range(pairs):
                    probs, gscores = [], []
                    for head in range(2):
                        part = slice(head * KEY_TILE, (head + 1) * KEY_TILE)
                        row = slice(head, head + 1)
                        prob = jnp.exp(
                            jnp.where(ok, scores[p][part] - log_ref[0, p, row, here], -1e30)
                        )
                        gscore = prob * (gprobs[p][part] - center_ref[p, row, here])
                        probs.append(prob.astype(BF16))
                        gscores.append(gscore.astype(BF16))
                    probs = jnp.concatenate(probs, 0)
                    gscores = jnp.concatenate(gscores, 0)
                    sumv_ref[p] += dot(probs, grads[p])
                    sumk_ref[p] += dot(gscores, queries[p])
                    turned_ref[p, :, here] += dot(keys[p], gscores, TN)

            return nothing

        lax.fori_loop(0, tiles, rows, 0)

        for p in range(pairs):
            gkeyvalue_ref[0, place, cols[p]] = jnp.where(
                left, sumk_ref[p, :KEY_TILE], sumk_ref[p, KEY_TILE:]
            ).astype(BF16)
            gkeyvalue_ref[0, place, after(cols[p])] = jnp.where(
                left, sumv_ref[p, :KEY_TILE], sumv_ref[p, KEY_TILE:]
            ).astype(BF16)
        return nothing

    lax.fori_loop(first_ref[seq], (halo + block) // KEY_TILE, step, 0)
    for p in range(pairs):
        gquery_ref[0, :, cols[p]] = (jnp.transpose(turned_ref[p]) * 0.125).astype(BF16)


def attend_back(low, first, query, keyvalues, starts, mixed, grad, logs):
    seqs, block, width = query.shape
    length = keyvalues.shape[1]
    pairs = width // PAIR
    rows = pl.BlockSpec((1, block, width), lambda s, low, first: (s, 0, 0))
    full = pl.BlockSpec((1, length, 2 * width), lambda s, low, first: (s, 0, 0))
    return pl.pallas_call(
        functools.partial(attend_back_kernel, length - block),
        grid_spec=pltpu.PrefetchScalarGridSpec(
            num_scalar_prefetch=2,
            grid=(seqs,),
            in_specs=[
                rows,
                full,
                pl.BlockSpec((1, 1, block), lambda s, low, first: (s, 0, 0)),
                rows,
                rows,
                pl.BlockSpec((1, pairs, 2, block), lambda s, low, first: (s, 0, 0, 0)),
            ],
            out_specs=[rows, full],
            scratch_shapes=[
                pltpu.VMEM((pairs, PAIR, block), F32),
                pltpu.VMEM((pairs, 8, block), F32),
                pltpu.VMEM((pairs, 2 * KEY_TILE, PAIR), F32),
                pltpu.VMEM((pairs, 2 * KEY_TILE, PAIR), F32),
            ],
        ),
        out_shape=[
            jax.ShapeDtypeStruct((seqs, block, width), BF16),
            jax.ShapeDtypeStruct((seqs, length, 2 * width), BF16),
        ],
        compiler_params=pltpu.CompilerParams(vmem_limit_bytes=VMEM_LIMIT),
        cost_estimate=pl.CostEstimate(
            flops=40 << 30, bytes_accessed=28 << 20, transcendentals=8 << 20
        ),
        name="attend_back",
    )(low, first, query, keyvalues, starts, mixed, grad, logs)


def slab_copies(slab_ref, merge_ref, up_ref, down_ref, sems):
    owners = slab_ref.shape[0]
    width = slab_ref.shape[2]
    rows = width // owners
    chunks = up_ref.shape[1] // width
    groups = [[], [], []]
    for owner in range(owners):
        here = pl.ds(owner * rows, rows)
        groups[0].append((slab_ref.at[owner, pl.ds(0, rows), :], merge_ref.at[here, :]))
        for c in range(chunks):
            groups[1].append(
                (
                    slab_ref.at[owner, pl.ds((1 + c) * rows, rows), :],
                    up_ref.at[here, pl.ds(c * width, width)],
                )
            )
        groups[2].append(
            (
                slab_ref.at[owner, pl.ds((1 + chunks) * rows, chunks * rows), :],
                down_ref.at[pl.ds(owner * chunks * rows, chunks * rows), :],
            )
        )
    return [
        [pltpu.make_async_copy(*pair, sems.at[k, n]) for n, pair in enumerate(group)]
        for k, group in enumerate(groups)
    ]


def mlp_kernel(
    factor_ref,
    mixed_ref,
    token_ref,
    teacher_ref,
    weight_ref,
    outbias_ref,
    gain_ref,
    shift_ref,
    upbias_ref,
    downbias_ref,
    slab_ref,
    layer_ref,
    gresid_ref,
    gmixed_ref,
    sums_ref,
    upsums_ref,
    gslab_ref,
    merge_ref,
    up_ref,
    down_ref,
    slope_ref,
    normed_ref,
    active_ref,
    ghidden_ref,
    gmlp_ref,
    gbranch_ref,
    split_ref,
    block_ref,
    sems,
    split_sems,
    block_sems,
):
    width = token_ref.shape[-1]
    hidden = up_ref.shape[1]
    step = pl.program_id(0)
    here = pl.ds(pl.multiple_of(step * MLP_TILE, MLP_TILE), MLP_TILE)
    copies = slab_copies(slab_ref, merge_ref, up_ref, down_ref, sems)

    def arrive(k):
        @pl.when(step == 0)
        def _():
            for copy in copies[k]:
                copy.wait()

    @pl.when(step == 0)
    def _():
        for group in copies:
            for copy in group:
                copy.start()
        sums_ref[...] = jnp.zeros_like(sums_ref)
        upsums_ref[...] = jnp.zeros_like(upsums_ref)

    arrive(0)
    resid = (
        token_ref[...].astype(F32) + dot(mixed_ref[here, :], merge_ref[...]) + outbias_ref[...]
    )
    unit, scale = norm_parts(resid)
    normed = (unit * gain_ref[...] + shift_ref[...]).astype(BF16)
    normed_ref[here, :] = normed
    arrive(1)
    cuts = [slice(c, c + MLP_CHUNK) for c in range(0, hidden, MLP_CHUNK)]
    result = resid + downbias_ref[...]
    for n, cols in enumerate(cuts):
        inner = dot(normed, up_ref[:, cols]) + upbias_ref[:, cols]
        square = inner * inner
        curve = jnp.tanh(0.7978845608028654 * (inner + 0.044715 * square * inner))
        half = 0.5 * (1.0 + curve)
        active = (half * inner).astype(BF16)
        active_ref[here, cols] = active
        slope_ref[:, cols] = half + 0.5 * inner * (1.0 - curve * curve) * (
            0.7978845608028654 * (1.0 + 3.0 * 0.044715 * square)
        )
        if n == 0:
            arrive(2)
        result += dot(active_ref[here, cols], down_ref[cols, :])
    layer_ref[...] = result.astype(BF16)
    error = result - teacher_ref[...].astype(F32)
    weight = weight_ref[...]
    sums_ref[4:5, :] += jnp.sum(weight * (error * error), 0, keepdims=True)
    gresult = error * (weight * factor_ref[0])
    gmlp = gresult.astype(BF16)
    gmlp_ref[here, :] = gmlp
    sums_ref[3:4, :] += jnp.sum(gmlp.astype(F32), 0, keepdims=True)
    gnormed = jnp.zeros_like(result)
    for cols in cuts:
        gactive = dot(gmlp, down_ref[cols, :], NT)
        ghidden = (gactive * slope_ref[:, cols]).astype(BF16)
        ghidden_ref[here, cols] = ghidden
        upsums_ref[0:1, cols] += jnp.sum(ghidden.astype(F32), 0, keepdims=True)
        gnormed += dot(ghidden_ref[here, cols], up_ref[:, cols], NT)
    sums_ref[1:2, :] += jnp.sum(gnormed * unit, 0, keepdims=True)
    sums_ref[2:3, :] += jnp.sum(gnormed, 0, keepdims=True)
    gresid = gresult + norm_back(gnormed, gain_ref[...], unit, scale)
    gresid_ref[...] = gresid
    gbranch = gresid.astype(BF16)
    gbranch_ref[here, :] = gbranch
    sums_ref[0:1, :] += jnp.sum(gbranch.astype(F32), 0, keepdims=True)
    gmixed_ref[...] = dot(gbranch, merge_ref[...], NT).astype(BF16)

    owners, rows, _ = split_ref.shape[1:]
    chunks = hidden // width
    share = owners // chunks

    def split_copy(index):
        return pltpu.make_async_copy(
            split_ref.at[index % 2],
            gslab_ref.at[:, pl.ds(pl.multiple_of(index * rows, 16), rows), :],
            split_sems.at[index % 2],
        )

    def block_copy(index):
        return pltpu.make_async_copy(
            block_ref.at[index % 2],
            gslab_ref.at[
                pl.ds(index * share, share), pl.ds((1 + chunks) * rows, chunks * rows), :
            ],
            block_sems.at[index % 2],
        )

    @pl.when(step == pl.num_programs(0) - 1)
    def _():
        out = dot(mixed_ref[...], gbranch_ref[...], TN).astype(BF16)
        split_ref[0] = out.reshape(owners, rows, width)
        split_copy(0).start()

        def ups(index, nothing):
            @pl.when(index >= 2)
            def _():
                split_copy(index - 2).wait()

            cols = pl.ds(pl.multiple_of((index - 1) * width, 128), width)
            out = dot(normed_ref[...], ghidden_ref[:, cols], TN).astype(BF16)
            split_ref[index % 2] = out.reshape(owners, rows, width)
            split_copy(index).start()
            return nothing

        lax.fori_loop(1, chunks + 1, ups, 0)

        def downs(index, nothing):
            @pl.when(index >= 2)
            def _():
                block_copy(index - 2).wait()

            cols = pl.ds(pl.multiple_of(index * width, 128), width)
            out = dot(active_ref[:, cols], gmlp_ref[...], TN).astype(BF16)
            block_ref[index % 2] = out.reshape(share, chunks * rows, width)
            block_copy(index).start()
            return nothing

        lax.fori_loop(0, chunks, downs, 0)
        split_copy(chunks - 1).wait()
        split_copy(chunks).wait()
        block_copy(chunks - 2).wait()
        block_copy(chunks - 1).wait()


def mlp(factor, mixed, tokens, teacher, weight, vectors, slab, extra):
    rows, width = tokens.shape
    outbias, gain, shift, upbias, downbias = vectors
    hidden = upbias.shape[1]
    chunks = hidden // width
    owners = slab.shape[0]
    few = width // owners
    tile = lambda n: pl.BlockSpec((MLP_TILE, n), lambda i: (i, 0))
    fixed = lambda m, n: pl.BlockSpec((m, n), lambda i: (0, 0))
    anywhere = pl.BlockSpec(memory_space=pl.ANY)
    shape = jax.ShapeDtypeStruct
    return pl.pallas_call(
        mlp_kernel,
        grid=(rows // MLP_TILE,),
        in_specs=[
            pl.BlockSpec(memory_space=pltpu.SMEM),
            fixed(rows, width),
            tile(width),
            tile(width),
            tile(1),
            fixed(1, width),
            fixed(1, width),
            fixed(1, width),
            fixed(1, hidden),
            fixed(1, width),
            anywhere,
        ],
        out_specs=[
            tile(width),
            tile(width),
            tile(width),
            fixed(8, width),
            fixed(8, hidden),
            anywhere,
        ],
        out_shape=[
            shape((rows, width), BF16),
            shape((rows, width), F32),
            shape((rows, width), BF16),
            shape((8, width), F32),
            shape((8, hidden), F32),
            shape((owners, (1 + 2 * chunks) * few + extra, width), BF16),
        ],
        scratch_shapes=[
            pltpu.VMEM((width, width), BF16),
            pltpu.VMEM((width, hidden), BF16),
            pltpu.VMEM((hidden, width), BF16),
            pltpu.VMEM((MLP_TILE, hidden), F32),
            pltpu.VMEM((rows, width), BF16),
            pltpu.VMEM((rows, hidden), BF16),
            pltpu.VMEM((rows, hidden), BF16),
            pltpu.VMEM((rows, width), BF16),
            pltpu.VMEM((rows, width), BF16),
            pltpu.VMEM((2, owners, few, width), BF16),
            pltpu.VMEM((2, owners // chunks, chunks * few, width), BF16),
            pltpu.SemaphoreType.DMA((3, owners * chunks)),
            pltpu.SemaphoreType.DMA((2,)),
            pltpu.SemaphoreType.DMA((2,)),
        ],
        compiler_params=pltpu.CompilerParams(vmem_limit_bytes=VMEM_LIMIT),
        cost_estimate=pl.CostEstimate(
            flops=6 * rows * width * (width + 2 * hidden),
            bytes_accessed=40 << 20,
            transcendentals=rows * hidden,
        ),
        name="mlp",
    )(factor, mixed, tokens, teacher, weight, outbias, gain, shift, upbias, downbias, slab)


def halo_back_kernel(
    low_ref,
    halo_any,
    grad_any,
    whole_any,
    out_any,
    sums_ref,
    halo_ref,
    grad_ref,
    out_ref,
    weight_ref,
    halo_sems,
    grad_sems,
    out_sems,
    sem,
):
    seqs, rows, width = halo_ref.shape
    tiles = rows // ROW_TILE
    weight = pltpu.make_async_copy(whole_any.at[:, pl.ds(width, 2 * width)], weight_ref, sem)
    weight.start()

    def arrive(seq, tile, at):
        return (
            pltpu.make_async_copy(
                halo_any.at[seq, at], halo_ref.at[seq, at], halo_sems.at[seq, tile]
            ),
            pltpu.make_async_copy(
                grad_any.at[seq, at], grad_ref.at[seq, at], grad_sems.at[seq, tile]
            ),
        )

    def leave(seq, tile, at):
        return pltpu.make_async_copy(
            out_ref.at[seq, at], out_any.at[seq, at], out_sems.at[seq, tile]
        )

    def begin(seq, tile, at):
        @pl.when(tile >= low_ref[seq])
        def _():
            for copy in arrive(seq, tile, at):
                copy.start()

        @pl.when(tile < low_ref[seq])
        def _():
            out_ref[seq, at, :] = jnp.zeros((ROW_TILE, width), BF16)
            leave(seq, tile, at).start()

    def work(seq, tile, at):
        for copy in arrive(seq, tile, at):
            copy.wait()
        grad = dot(grad_ref[seq, at, :], weight_ref[...], NT)
        unit, _ = norm_parts(halo_ref[seq, at, :].astype(F32))
        out_ref[seq, at, :] = grad.astype(BF16)
        leave(seq, tile, at).start()
        sums_ref[0:1, :] += jnp.sum(grad * unit, 0, keepdims=True)
        sums_ref[1:2, :] += jnp.sum(grad, 0, keepdims=True)

    def end(seq, tile, at):
        leave(seq, tile, at).wait()

    every_tile(low_ref, seqs, tiles, begin, every=True)
    sums_ref[...] = jnp.zeros_like(sums_ref)
    weight.wait()
    every_tile(low_ref, seqs, tiles, work)
    every_tile(low_ref, seqs, tiles, end, every=True)


def halo_back(low, halo, gkeyvalues, whole):
    seqs, rows, width = halo.shape
    tiles = rows // ROW_TILE
    anywhere = pl.BlockSpec(memory_space=pl.ANY)
    return pl.pallas_call(
        halo_back_kernel,
        grid_spec=pltpu.PrefetchScalarGridSpec(
            num_scalar_prefetch=1,
            grid=(1,),
            in_specs=[anywhere, anywhere, anywhere],
            out_specs=[anywhere, pl.BlockSpec((8, width), lambda i, low: (0, 0))],
            scratch_shapes=[
                pltpu.VMEM((seqs, rows, width), BF16),
                pltpu.VMEM((seqs, rows, 2 * width), BF16),
                pltpu.VMEM((seqs, rows, width), BF16),
                pltpu.VMEM((width, 2 * width), BF16),
                pltpu.SemaphoreType.DMA((seqs, tiles)),
                pltpu.SemaphoreType.DMA((seqs, tiles)),
                pltpu.SemaphoreType.DMA((seqs, tiles)),
                pltpu.SemaphoreType.DMA,
            ],
        ),
        out_shape=[
            jax.ShapeDtypeStruct((seqs, rows, width), BF16),
            jax.ShapeDtypeStruct((8, width), F32),
        ],
        compiler_params=pltpu.CompilerParams(vmem_limit_bytes=VMEM_LIMIT),
        cost_estimate=pl.CostEstimate(
            flops=4 << 30, bytes_accessed=16 << 20, transcendentals=0
        ),
        name="halo_back",
    )(low, halo, gkeyvalues, whole)


def own_back_kernel(
    low_ref,
    order_ref,
    own_any,
    normed_any,
    gquery_any,
    gkeyvalue_any,
    whole_any,
    gnormed_any,
    keep_any,
    give_any,
    sums_ref,
    own_ref,
    normed_ref,
    gquery_ref,
    gkeyvalue_ref,
    weight_ref,
    total_ref,
    gnormed_ref,
    gweight_ref,
    sems,
    out_sems,
):
    seqs, block, width = own_ref.shape
    halo = normed_ref.shape[1] - block
    tiles = halo // ROW_TILE
    here = pl.ds(halo, block)
    before = pl.ds(0, halo)
    first = [
        pltpu.make_async_copy(normed_any.at[:, here], normed_ref.at[:, here], sems.at[0]),
        pltpu.make_async_copy(gkeyvalue_any.at[:, here], gkeyvalue_ref.at[:, here], sems.at[1]),
        pltpu.make_async_copy(gquery_any, gquery_ref, sems.at[2]),
    ]
    later = [
        pltpu.make_async_copy(normed_any.at[:, before], normed_ref.at[:, before], sems.at[3]),
        pltpu.make_async_copy(gkeyvalue_any.at[:, before], gkeyvalue_ref.at[:, before], sems.at[4]),
    ]
    last = [
        pltpu.make_async_copy(whole_any, weight_ref, sems.at[5]),
        pltpu.make_async_copy(own_any, own_ref, sems.at[6]),
    ]
    for copy in first + later + last:
        copy.start()
    for copy in first:
        copy.wait()
    rows = seqs * block
    gweight_ref[:, :width] = dot(
        normed_ref[:, halo:, :].reshape(rows, width), gquery_ref[...].reshape(rows, width), TN
    ).astype(BF16)

    def whole(k, nothing):
        cols = pl.ds(pl.multiple_of(k * width, 128), width)
        total_ref[:, cols] = dot(
            normed_ref[:, halo:, :].reshape(rows, width),
            gkeyvalue_ref[:, halo:, cols].reshape(rows, width),
            TN,
        )
        return nothing

    lax.fori_loop(0, 2, whole, 0)
    sums_ref[...] = jnp.zeros_like(sums_ref)
    sums_ref[2:3, :] = jnp.sum(
        gquery_ref[...].reshape(rows, width).astype(F32), 0, keepdims=True
    )
    sums_ref[3:4, :] = jnp.sum(
        gkeyvalue_ref[:, halo:, width:].reshape(rows, width).astype(F32), 0, keepdims=True
    )
    for copy in later:
        copy.wait()

    def add(seq, tile, at):
        total_ref[...] += dot(normed_ref[seq, at, :], gkeyvalue_ref[seq, at, :], TN)
        sums_ref[3:4, :] += jnp.sum(gkeyvalue_ref[seq, at, width:].astype(F32), 0, keepdims=True)

    every_tile(low_ref, seqs, tiles, add)
    gweight_ref[:, width:] = total_ref[...].astype(BF16)
    slots = keep_any.shape[0]
    share = width // (2 * slots)
    sends = [
        pltpu.make_async_copy(
            gweight_ref.at[pl.ds(pl.multiple_of(order_ref[k] * share, 16), share), :],
            (keep_any, give_any)[k // slots].at[k % slots, pl.ds(0, share), :],
            out_sems.at[1 + k],
        )
        for k in range(2 * slots)
    ]
    for copy in sends:
        copy.start()
    for copy in last:
        copy.wait()

    def lead(seq, nothing):
        grad = dot(gquery_ref[seq], weight_ref[:, :width], NT)
        grad += dot(gkeyvalue_ref[seq, halo:, :], weight_ref[:, width:], NT)
        gnormed_ref[seq] = grad
        unit, _ = norm_parts(own_ref[seq].astype(F32))
        sums_ref[0:1, :] += jnp.sum(grad * unit, 0, keepdims=True)
        sums_ref[1:2, :] += jnp.sum(grad, 0, keepdims=True)
        return nothing

    lax.fori_loop(0, seqs, lead, 0)
    back = pltpu.make_async_copy(gnormed_ref, gnormed_any, out_sems.at[0])
    back.start()
    for copy in sends:
        copy.wait()
    back.wait()


def own_back(low, order, own, normed, gquery, gkeyvalues, whole):
    seqs, block, width = own.shape
    length = normed.shape[1]
    anywhere = pl.BlockSpec(memory_space=pl.ANY)
    return pl.pallas_call(
        own_back_kernel,
        grid_spec=pltpu.PrefetchScalarGridSpec(
            num_scalar_prefetch=2,
            grid=(1,),
            in_specs=[anywhere] * 5,
            out_specs=[
                anywhere,
                anywhere,
                anywhere,
                pl.BlockSpec((8, width), lambda i, low, order: (0, 0)),
            ],
            scratch_shapes=[
                pltpu.VMEM((seqs, block, width), BF16),
                pltpu.VMEM((seqs, length, width), BF16),
                pltpu.VMEM((seqs, block, width), BF16),
                pltpu.VMEM((seqs, length, 2 * width), BF16),
                pltpu.VMEM((width, 3 * width), BF16),
                pltpu.VMEM((width, 2 * width), F32),
                pltpu.VMEM((seqs, block, width), F32),
                pltpu.VMEM((width, 3 * width), BF16),
                pltpu.SemaphoreType.DMA((7,)),
                pltpu.SemaphoreType.DMA((1 + SHARES,)),
            ],
        ),
        out_shape=[
            jax.ShapeDtypeStruct((seqs, block, width), F32),
            jax.ShapeDtypeStruct((SHARES // 2, width // SHARES + SMALL_ROWS, 3 * width), BF16),
            jax.ShapeDtypeStruct((SHARES // 2, width // SHARES + SMALL_ROWS, 3 * width), BF16),
            jax.ShapeDtypeStruct((8, width), F32),
        ],
        compiler_params=pltpu.CompilerParams(vmem_limit_bytes=VMEM_LIMIT),
        cost_estimate=pl.CostEstimate(
            flops=16 << 30, bytes_accessed=24 << 20, transcendentals=0
        ),
        name="own_back",
    )(low, order, own, normed, gquery, gkeyvalues, whole)


def finish_kernel(seqs, own_ref, gnormed_ref, gresid_ref, gain_ref, *rest):
    near_refs, far_refs = rest[:seqs], rest[seqs:-2]
    out_ref, total_ref = rest[-2:]
    unit, scale = norm_parts(own_ref[0].astype(F32))
    for seq, near_ref in enumerate(near_refs):

        @pl.when(pl.program_id(0) == seq)
        def _():
            total_ref[...] = gnormed_ref[0] + near_ref[...].astype(F32)

    for far_ref in far_refs:

        @pl.when(pl.program_id(1) == pl.num_programs(1) - 1)
        def _():
            total_ref[-HALO_CHUNK:, :] += far_ref[0].astype(F32)

    out_ref[0] = (gresid_ref[0] + norm_back(total_ref[...], gain_ref[...], unit, scale)).astype(BF16)


def finish(own, gnormed, near, far, gresid, gain):
    seqs, block, width = own.shape
    tile = pl.BlockSpec((1, ROW_TILE, width), lambda s, t: (s, t, 0))
    last = pl.BlockSpec((1, HALO_CHUNK, width), lambda s, t: (s, 0, 0))
    return pl.pallas_call(
        functools.partial(finish_kernel, seqs),
        grid=(seqs, block // ROW_TILE),
        in_specs=[tile, tile, tile, pl.BlockSpec((1, width), lambda s, t: (0, 0))]
        + [pl.BlockSpec((ROW_TILE, width), lambda s, t: (t, 0))] * seqs
        + [last] * len(far),
        out_specs=tile,
        out_shape=jax.ShapeDtypeStruct(own.shape, BF16),
        scratch_shapes=[pltpu.VMEM((ROW_TILE, width), F32)],
        cost_estimate=pl.CostEstimate(
            flops=20 * seqs * block * width,
            bytes_accessed=14 * seqs * block * width,
            transcendentals=0,
        ),
        name="finish",
    )(own, gnormed, gresid, gain, *near, *far)


def swap(x, axis, bit):
    size = lax.axis_size(axis)
    return lax.ppermute(x, axis, [(i, i ^ bit) for i in range(size)])


def shift(x, axis, step):
    size = lax.axis_size(axis)
    return lax.ppermute(
        x, axis, [(i, i + step) for i in range(size) if 0 <= i + step < size]
    )


def sum_over(x, axis):
    bit = 1
    while bit < lax.axis_size(axis):
        x = x + swap(x, axis, bit)
        bit *= 2
    return x


def max_over(x, axis):
    bit = 1
    while bit < lax.axis_size(axis):
        x = jnp.maximum(x, swap(x, axis, bit))
        bit *= 2
    return x


def gather_near(shard):
    size = lax.axis_size("fsdp")
    if size != 8:
        return [lax.all_gather(shard, "fsdp", axis=0, tiled=True)]
    return [shard] + [swap(shard, "fsdp", 2 * d) for d in range(1, size // 2)]


def gather_rest(near):
    if lax.axis_size("fsdp") != 8:
        return near
    return near + [swap(piece, "fsdp", 1) for piece in near]


def piece_order():
    size = lax.axis_size("fsdp")
    me = lax.axis_index("fsdp").astype(jnp.int32)
    if size != 8:
        return jnp.zeros((1,), jnp.int32)
    return jnp.stack(
        [me ^ (2 * d) for d in range(size // 2)] + [me ^ (2 * d) ^ 1 for d in range(size // 2)]
    )


def sum_seq(total):
    if lax.axis_size("seq") != 4:
        return lax.psum(total, "seq")
    return sum_seq_rest(sum_seq_second(sum_seq_first(total)))


def sum_seq_first(total):
    rows, columns = total.shape
    odd = lax.axis_index("seq") % 2
    halves = total.reshape(2, rows // 2, columns)
    pick = lambda k: lax.dynamic_index_in_dim(halves, k, 0, keepdims=False)
    return (pick(odd).astype(F32) + swap(pick(1 - odd), "seq", 1).astype(F32)).astype(BF16)


def sum_seq_second(half):
    return (half.astype(F32) + swap(half, "seq", 2).astype(F32)).astype(BF16)


def sum_seq_rest(half):
    odd = lax.axis_index("seq") % 2
    back = swap(half, "seq", 1)
    return jnp.where(
        odd == 0, jnp.concatenate([half, back], 0), jnp.concatenate([back, half], 0)
    )


def reduce_rows(keep, give, half, *first):
    other = swap(give, "fsdp", 1)
    staged = lax.axis_size("seq") == 4
    if staged:
        half = sum_seq_first(half)
    mine = [
        (keep[d].astype(F32) + other[d].astype(F32)).astype(BF16) for d in range(keep.shape[0])
    ]
    arrived = [swap(part, "fsdp", 2 * d) for d, part in enumerate(mine) if d > 0]
    arrived, half, *first = lax.optimization_barrier((arrived, half, *first))
    if staged:
        half = sum_seq_rest(sum_seq_second(half))
    total = mine[0].astype(F32)
    for part in arrived:
        total = total + part.astype(F32)
    return sum_seq(total.astype(BF16)), half, *first


def gather_slab(outweight, fcweight, projweight, *first):
    width = outweight.shape[1]
    cuts = fcweight.shape[1] // width

    def join(out, up, down, axis):
        ups = [lax.slice_in_dim(up, c * width, (c + 1) * width, axis=-1) for c in range(cuts)]
        return jnp.concatenate([out, *ups, down], axis)

    if lax.axis_size("fsdp") == SHARES:
        slab = join(outweight, fcweight, projweight, 0)
        slab, *first = lax.optimization_barrier((slab, *first))
        return lax.all_gather(slab, "fsdp", axis=0, tiled=False), *first
    whole = [
        lax.all_gather(w, "fsdp", axis=0, tiled=True) for w in (outweight, fcweight, projweight)
    ]
    return join(*(w.reshape(SHARES, -1, w.shape[1]) for w in whole), 1), *first


def reduce_slab(slab, width, hidden):
    owners = lax.axis_size("fsdp")
    cuts = hidden // width
    rows = width // SHARES

    def part(array, axis):
        at = lambda a, b: lax.slice_in_dim(array, a * rows, b * rows, axis=axis)
        ups = [at(1 + c, 2 + c) for c in range(cuts)]
        rest = lax.slice_in_dim(array, (1 + 2 * cuts) * rows, array.shape[axis], axis=axis)
        return at(0, 1), jnp.concatenate(ups, -1), at(1 + cuts, 1 + 2 * cuts), rest

    if owners == SHARES:
        return part(slab.astype(F32), 0)
    *grads, rest = part(slab, 1)
    grads = [
        lax.psum(
            lax.psum_scatter(
                g.reshape(-1, g.shape[-1]), "fsdp", scatter_dimension=0, tiled=True
            ),
            "seq",
        ).astype(F32)
        for g in grads
    ]
    rest = lax.psum(rest.astype(F32), ("fsdp", "seq"))
    return *grads, rest


def local(
    tokens,
    teacher,
    segment_ids,
    latent_flags,
    valid_mask,
    attngain,
    attnshift,
    qkvweight,
    qvbias,
    outweight,
    outbias,
    mlpgain,
    mlpshift,
    fcweight,
    fcbias,
    projweight,
    projbias,
):
    seqs, block, width = tokens.shape
    groups = lax.axis_size("seq")
    owners = lax.axis_size("fsdp")
    rows = seqs * block
    halo_rows = (groups - 1) * block
    far_rows = halo_rows - block
    me = lax.axis_index("fsdp")
    place = lax.axis_index("seq").astype(jnp.int32)
    hidden = fcweight.shape[1]

    order = piece_order()
    qkv_pieces = gather_near(qkvweight)

    weight = (valid_mask * (1 - latent_flags)).astype(F32)
    below = jnp.sum(
        (segment_ids[:, :, None] < jnp.arange(1, 4, dtype=jnp.int32)).astype(jnp.int32), 1
    )
    facts = jnp.concatenate([below.reshape(-1), jnp.sum(weight).astype(jnp.int32)[None]])

    shards = [attngain, attnshift, qvbias, outbias, mlpgain, mlpshift, fcbias, projbias]
    sent = [tokens[k] for k in range(seqs)] + [tokens[:, block - HALO_CHUNK :]]
    bit = 1
    while bit < groups:
        facts = facts + swap(facts, "seq", bit)
        if bit == 1:
            facts, shards = lax.optimization_barrier((facts, shards))
        bit *= 2

    sent, facts = lax.optimization_barrier((sent, facts))
    near = [shift(sent[k], "seq", 1) for k in range(seqs)]
    far = shift(sent[seqs], "seq", 2) if far_rows > 0 else None
    bounds = facts[:-1].reshape(seqs, 3)

    def start_of(positions):
        found = jnp.zeros((seqs,) + positions.shape, jnp.int32)
        for d in range(3):
            bound = bounds[:, d].reshape((seqs,) + (1,) * positions.ndim)
            found = jnp.maximum(found, jnp.where(bound <= positions[None], bound, 0))
        return found

    firsts = jnp.arange(groups, dtype=jnp.int32) * block
    reach = jnp.max(firsts[None] - start_of(firsts)) - block
    chunks = jnp.maximum(reach + HALO_CHUNK - 1, 0) // HALO_CHUNK

    facts = jnp.stack([facts[-1], chunks])
    bit = 1
    while bit < owners:
        other = swap(facts, "fsdp", bit)
        facts = jnp.where(jnp.arange(2) == 1, jnp.maximum(facts, other), facts + other)
        bit *= 2

    packed = jnp.concatenate(
        [jnp.pad(v[None], ((0, 0), (0, -v.shape[0] % 128))) for v in shards], 1
    )
    table = jnp.where(
        lax.broadcasted_iota(jnp.int32, (owners, packed.shape[1]), 0) == me,
        packed,
        jnp.zeros((), BF16),
    )
    table = sum_over(table, "fsdp")

    qkv_pieces = gather_rest(qkv_pieces)
    slab, qkv_pieces, table, facts, near[0] = gather_slab(
        outweight, fcweight, projweight, qkv_pieces, table, facts, near[0]
    )
    count = facts[0].astype(F32)
    chunks = facts[1]

    vectors = []
    at = 0
    for shard in shards:
        size = shard.shape[0]
        vectors.append(table[:, at : at + size].reshape(1, size * owners).astype(F32))
        at += size + -size % 128
    gain1, shift1, bias1, outbias_v, gain2, shift2, upbias, downbias = vectors


    base = (place - (groups - 1)) * block
    starts = start_of(place * block + jnp.arange(block, dtype=jnp.int32)) - base
    low_rows = starts[:, ::QUERY_TILE]
    low = (low_rows // KEY_TILE).reshape(-1)
    low_tile = starts[:, 0] // ROW_TILE
    first = low_tile * (ROW_TILE // KEY_TILE)
    starts = starts[:, None, :]

    bias1 = jnp.concatenate([bias1[:, :width], jnp.zeros((1, width), F32), bias1[:, width:]], 1)
    normed, query, keyvalues, qkv = project_own(
        order, tokens, gain1, shift1, bias1, qkv_pieces, halo_rows + block
    )
    near[-1], query = lax.optimization_barrier((near[-1], query))
    halo = jnp.stack(near)
    if far_rows > 0:
        blank = jnp.zeros((seqs, far_rows - HALO_CHUNK, width), BF16)
        halo = jnp.concatenate([blank, far, halo], 1)

    def fetch(state):
        j, halo = state
        sent = lax.dynamic_slice_in_dim(halo, halo_rows - HALO_CHUNK * (j + 1), HALO_CHUNK, 1)
        came = shift(sent, "seq", 1)
        return j + 1, lax.dynamic_update_slice_in_dim(
            halo, came, far_rows - HALO_CHUNK * (j + 1), 1
        )

    if far_rows > 0:
        _, halo = lax.while_loop(lambda state: state[0] < chunks, fetch, (jnp.int32(1), halo))

    normed, keyvalues = project_halo(
        low_tile, halo, gain1, shift1, bias1, qkv, normed, keyvalues
    )
    mixed, logs = attend(low, query, keyvalues, starts)

    factor = (rows * owners * groups) / count
    layer_out, gresid, gmixed, sums, upsums, outer = mlp(
        factor.reshape(1),
        mixed.reshape(rows, width),
        tokens.reshape(rows, width),
        teacher.reshape(rows, width),
        weight.reshape(rows, 1),
        (outbias_v, gain2, shift2, upbias, downbias),
        slab,
        SMALL_ROWS,
    )

    small = jnp.concatenate(
        [upsums[0].reshape(SHARES, -1)] + [sums[k].reshape(SHARES, -1) for k in range(4)], 1
    )
    line = lax.broadcasted_iota(jnp.int32, (SHARES, SMALL_ROWS, width), 1)
    small = jnp.where(line == 0, small[:, None, :], jnp.where(line == 1, sums[4], 0.0))
    outer = lax.dynamic_update_slice_in_dim(
        outer, small.astype(BF16), outer.shape[1] - SMALL_ROWS, 1
    )
    outer, gmixed = lax.optimization_barrier((outer, gmixed))
    staged = owners == SHARES and groups == 4
    if owners == SHARES:
        outer = lax.psum_scatter(outer, "fsdp", scatter_dimension=0, tiled=False)
        outer = outer if staged else sum_seq(outer)

    gquery, gkeyvalues = attend_back(
        low, first, query, keyvalues, starts, mixed, gmixed.reshape(seqs, block, width), logs
    )
    ghalo, halo_sums = halo_back(low_tile, halo, gkeyvalues, qkv)

    def give(state):
        j, ghalo = state
        j = j - 1
        sent = lax.dynamic_slice_in_dim(ghalo, far_rows - HALO_CHUNK * (j + 1), HALO_CHUNK, 1)
        came = shift(sent, "seq", -1)
        spot = halo_rows - HALO_CHUNK * (j + 1)
        held = lax.dynamic_slice_in_dim(ghalo, spot, HALO_CHUNK, 1)
        total = (held.astype(F32) + came.astype(F32)).astype(BF16)
        return j, lax.dynamic_update_slice_in_dim(ghalo, total, spot, 1)

    if far_rows > 0:
        _, ghalo = lax.while_loop(lambda state: state[0] > 1, give, (chunks, ghalo))

    ghalo, gquery = lax.optimization_barrier((ghalo, gquery))
    near = [shift(ghalo[k, far_rows:], "seq", -1) for k in range(seqs)]
    far = []
    if far_rows > 0:
        far = [shift(ghalo[:, far_rows - HALO_CHUNK : far_rows], "seq", -2)]
    sort = order if owners == SHARES else jnp.arange(SHARES, dtype=jnp.int32)
    gnormed, keep, give, own_sums = own_back(
        low_tile, sort, tokens, normed, gquery, gkeyvalues, qkv
    )
    keep, give, own_sums, halo_sums, near[0] = lax.optimization_barrier(
        (keep, give, own_sums, halo_sums, near[0])
    )
    late = jnp.concatenate(
        [(own_sums[k] + halo_sums[k]).reshape(SHARES, -1) for k in range(2)]
        + [own_sums[2:4].reshape(SHARES, -1)],
        1,
    ).astype(BF16)
    late = jnp.pad(late, ((0, 0), (0, 3 * width - late.shape[1])))
    slots = SHARES // 2
    late = jnp.stack([lax.dynamic_index_in_dim(late, sort[k], 0) for k in range(SHARES)])
    late = jnp.pad(late, ((0, 0), (0, SMALL_ROWS - 1), (0, 0)))
    share = width // SHARES
    keep = lax.dynamic_update_slice_in_dim(keep, late[:slots], share, 1)
    give = lax.dynamic_update_slice_in_dim(give, late[slots:], share, 1)

    grad_tokens = finish(
        tokens,
        gnormed,
        near,
        far,
        gresid.reshape(tokens.shape),
        gain1,
    )

    if owners == SHARES:
        joint, outer, grad_tokens = reduce_rows(keep, give, outer, grad_tokens)
    else:
        joint = jnp.concatenate([keep, give])
        small_late = lax.psum(joint[:, share].astype(F32), ("fsdp", "seq"))
        joint = joint[:, :share].reshape(width, 3 * width)
        joint = lax.psum_scatter(joint, "fsdp", scatter_dimension=0, tiled=True)
        joint = lax.psum(joint, "seq")
    joint = joint.astype(F32)
    grad_merge, grad_up, grad_down, small = reduce_slab(outer, width, hidden)

    share = width // owners
    if owners == SHARES:
        at = hidden // owners
        cuts = [small[0, :at]] + [
            small[0, at + k * share : at + (k + 1) * share] for k in range(4)
        ]
        loss_row = small[1]
    else:
        at = hidden // SHARES
        wide = width // SHARES
        full = [small[:, 0, :at].reshape(-1)] + [
            small[:, 0, at + k * wide : at + (k + 1) * wide].reshape(-1) for k in range(4)
        ]
        cuts = [
            lax.dynamic_slice_in_dim(v, me * (v.shape[0] // owners), v.shape[0] // owners)
            for v in full
        ]
        loss_row = small[0, 1]
    loss = jnp.sum(loss_row) / (width * count)
    share = width // owners
    if owners == SHARES:
        late = [joint[share, k * share : (k + 1) * share] for k in range(2)]
        late.append(joint[share, 2 * share : 4 * share])
    else:
        late = []
        for vector in (small_late[:, : width // SHARES], small_late[:, width // SHARES : 2 * width // SHARES], small_late[:, 2 * width // SHARES : 4 * width // SHARES]):
            vector = vector.reshape(-1)
            late.append(
                lax.dynamic_slice_in_dim(
                    vector, me * (vector.shape[0] // owners), vector.shape[0] // owners
                )
            )
    return (
        loss,
        layer_out.reshape(tokens.shape),
        grad_tokens,
        late[0],
        late[1],
        joint[:share],
        late[2],
        grad_merge,
        cuts[1],
        cuts[2],
        cuts[3],
        grad_up,
        cuts[0],
        grad_down,
        cuts[4],
    )


def solution(mesh):
    placed = (
        P("fsdp", "seq", None),
        P("fsdp", "seq", None),
        P("fsdp", "seq"),
        P("fsdp", "seq"),
        P("fsdp", "seq"),
        P("fsdp"),
        P("fsdp"),
        P("fsdp", None),
        P("fsdp"),
        P("fsdp", None),
        P("fsdp"),
        P("fsdp"),
        P("fsdp"),
        P("fsdp", None),
        P("fsdp"),
        P("fsdp", None),
        P("fsdp"),
    )
    return jax.shard_map(
        local,
        mesh=mesh,
        in_specs=placed,
        out_specs=(
            P(),
            P("fsdp", "seq", None),
            P("fsdp", "seq", None),
            P("fsdp"),
            P("fsdp"),
            P("fsdp", None),
            P("fsdp"),
            P("fsdp", None),
            P("fsdp"),
            P("fsdp"),
            P("fsdp"),
            P("fsdp", None),
            P("fsdp"),
            P("fsdp", None),
            P("fsdp"),
        ),
        check_vma=False,
    )
```

```python
import functools

import jax
import jax.numpy as jnp
from jax import lax
from jax.experimental import pallas as pl
from jax.experimental.pallas import tpu as pltpu
from jax.sharding import PartitionSpec as P

H = 12
HD = 64
PAIR = 2 * HD
EPSILON = 1e-05
KEY_TILE = 128
QUERY_TILE = 128
ROW_TILE = 256
MLP_TILE = 256
MLP_CHUNK = 1536
HALO_CHUNK = 128
SHARES = 8
SMALL_ROWS = 16
VMEM_LIMIT = 62 * 1024 * 1024

NT = (((1,), (1,)), ((), ()))
NN = (((1,), (0,)), ((), ()))
TN = (((0,), (0,)), ((), ()))
F32 = jnp.float32
BF16 = jnp.bfloat16


def dot(left, right, dims=NN):
    return lax.dot_general(left, right, dims, preferred_element_type=F32)


def norm_parts(values):
    center = values - jnp.mean(values, -1, keepdims=True)
    spread = jnp.mean(center * center, -1, keepdims=True)
    scale = lax.rsqrt(spread + EPSILON)
    return center * scale, scale


def norm_back(grad, gain, unit, scale):
    weighted = grad * gain
    first = jnp.mean(weighted, -1, keepdims=True)
    second = jnp.mean(weighted * unit, -1, keepdims=True)
    return scale * (weighted - first - unit * second)


def piece_copies(order_ref, pieces, whole_ref, sems):
    copies = []
    for place, piece in enumerate(pieces):
        rows = piece.shape[0]
        if len(pieces) == 1:
            target = whole_ref
        else:
            target = whole_ref.at[pl.ds(pl.multiple_of(order_ref[place] * rows, 16), rows), :]
        copies.append(pltpu.make_async_copy(piece, target, sems.at[place]))
    return copies


def project_own_kernel(count, order_ref, own_ref, gain_ref, shift_ref, bias_ref, *rest):
    pieces = rest[:count]
    normed_ref, query_ref, keyvalue_ref, whole_ref, weight_ref, sems, whole_sem = rest[count:]
    width = own_ref.shape[-1]
    seq = pl.program_id(0)
    whole = pltpu.make_async_copy(weight_ref, whole_ref, whole_sem)

    @pl.when(seq == 0)
    def _():
        copies = piece_copies(order_ref, pieces, weight_ref, sems)
        for copy in copies:
            copy.start()
        for copy in copies:
            copy.wait()
        whole.start()

    unit, _ = norm_parts(own_ref[0].astype(F32))
    normed = (unit * gain_ref[...] + shift_ref[...]).astype(BF16)
    normed_ref[0] = normed
    joint = (dot(normed, weight_ref[...]) + bias_ref[...]).astype(BF16)
    query_ref[0] = joint[:, :width]
    keyvalue_ref[0] = joint[:, width:]

    @pl.when(seq == pl.num_programs(0) - 1)
    def _():
        whole.wait()


def project_own(order, own, gain, shift, bias, pieces, length):
    seqs, block, width = own.shape
    last = length // block - 1
    fixed = lambda s, order: (0, 0)
    spot = lambda s, order: (s, 0, 0)
    end = lambda s, order: (s, last, 0)
    return pl.pallas_call(
        functools.partial(project_own_kernel, len(pieces)),
        grid_spec=pltpu.PrefetchScalarGridSpec(
            num_scalar_prefetch=1,
            grid=(seqs,),
            in_specs=[
                pl.BlockSpec((1, block, width), spot),
                pl.BlockSpec((1, width), fixed),
                pl.BlockSpec((1, width), fixed),
                pl.BlockSpec((1, 3 * width), fixed),
            ]
            + [pl.BlockSpec(memory_space=pl.ANY)] * len(pieces),
            out_specs=[
                pl.BlockSpec((1, block, width), end),
                pl.BlockSpec((1, block, width), spot),
                pl.BlockSpec((1, block, 2 * width), end),
                pl.BlockSpec(memory_space=pl.ANY),
            ],
            scratch_shapes=[
                pltpu.VMEM((width, 3 * width), BF16),
                pltpu.SemaphoreType.DMA((len(pieces),)),
                pltpu.SemaphoreType.DMA,
            ],
        ),
        out_shape=[
            jax.ShapeDtypeStruct((seqs, length, width), BF16),
            jax.ShapeDtypeStruct((seqs, block, width), BF16),
            jax.ShapeDtypeStruct((seqs, length, 2 * width), BF16),
            jax.ShapeDtypeStruct((width, 3 * width), BF16),
        ],
        compiler_params=pltpu.CompilerParams(vmem_limit_bytes=VMEM_LIMIT),
        cost_estimate=pl.CostEstimate(
            flops=6 * seqs * block * width * width, bytes_accessed=16 << 20, transcendentals=0
        ),
        name="project_own",
    )(order, own, gain, shift, bias, *pieces)


def every_tile(low_ref, seqs, tiles, work, every=False):
    for seq in range(seqs):

        def one(tile, nothing):
            work(seq, tile, pl.ds(pl.multiple_of(tile * ROW_TILE, ROW_TILE), ROW_TILE))
            return nothing

        lax.fori_loop(0 if every else low_ref[seq], tiles, one, 0)


def project_halo_kernel(
    low_ref, gain_ref, shift_ref, bias_ref, halo_any, whole_any, *rest
):
    (
        normed_any,
        keyvalue_any,
        halo_ref,
        normed_ref,
        keyvalue_ref,
        weight_ref,
        in_sems,
        normed_sems,
        keyvalue_sems,
        sem,
    ) = rest[2:]
    seqs, rows, width = halo_ref.shape
    tiles = rows // ROW_TILE
    weight = pltpu.make_async_copy(whole_any.at[:, pl.ds(width, 2 * width)], weight_ref, sem)
    weight.start()

    def arrive(seq, tile, at):
        return pltpu.make_async_copy(
            halo_any.at[seq, at], halo_ref.at[seq, at], in_sems.at[seq, tile]
        )

    def leave(seq, tile, at):
        return (
            pltpu.make_async_copy(
                normed_ref.at[seq, at], normed_any.at[seq, at], normed_sems.at[seq, tile]
            ),
            pltpu.make_async_copy(
                keyvalue_ref.at[seq, at], keyvalue_any.at[seq, at], keyvalue_sems.at[seq, tile]
            ),
        )

    def begin(seq, tile, at):
        arrive(seq, tile, at).start()

    def work(seq, tile, at):
        arrive(seq, tile, at).wait()
        unit, _ = norm_parts(halo_ref[seq, at, :].astype(F32))
        normed = (unit * gain_ref[...] + shift_ref[...]).astype(BF16)
        normed_ref[seq, at, :] = normed
        keyvalue_ref[seq, at, :] = (
            dot(normed, weight_ref[...]) + bias_ref[:, width:]
        ).astype(BF16)
        for copy in leave(seq, tile, at):
            copy.start()

    def end(seq, tile, at):
        for copy in leave(seq, tile, at):
            copy.wait()

    every_tile(low_ref, seqs, tiles, begin)
    weight.wait()
    every_tile(low_ref, seqs, tiles, work)
    every_tile(low_ref, seqs, tiles, end)


def project_halo(low, halo, gain, shift, bias, whole, normed, keyvalues):
    seqs, rows, width = halo.shape
    tiles = rows // ROW_TILE
    fixed = lambda i, low: (0, 0)
    anywhere = pl.BlockSpec(memory_space=pl.ANY)
    return pl.pallas_call(
        project_halo_kernel,
        grid_spec=pltpu.PrefetchScalarGridSpec(
            num_scalar_prefetch=1,
            grid=(1,),
            in_specs=[
                pl.BlockSpec((1, width), fixed),
                pl.BlockSpec((1, width), fixed),
                pl.BlockSpec((1, 3 * width), fixed),
                anywhere,
                anywhere,
                anywhere,
                anywhere,
            ],
            out_specs=[anywhere, anywhere],
            scratch_shapes=[
                pltpu.VMEM((seqs, rows, width), BF16),
                pltpu.VMEM((seqs, rows, width), BF16),
                pltpu.VMEM((seqs, rows, 2 * width), BF16),
                pltpu.VMEM((width, 2 * width), BF16),
                pltpu.SemaphoreType.DMA((seqs, tiles)),
                pltpu.SemaphoreType.DMA((seqs, tiles)),
                pltpu.SemaphoreType.DMA((seqs, tiles)),
                pltpu.SemaphoreType.DMA,
            ],
        ),
        out_shape=[
            jax.ShapeDtypeStruct(normed.shape, BF16),
            jax.ShapeDtypeStruct(keyvalues.shape, BF16),
        ],
        input_output_aliases={6: 0, 7: 1},
        compiler_params=pltpu.CompilerParams(vmem_limit_bytes=VMEM_LIMIT),
        cost_estimate=pl.CostEstimate(
            flops=2 * seqs * rows * width * width, bytes_accessed=16 << 20, transcendentals=0
        ),
        name="project_halo",
    )(low, gain, shift, bias, halo, whole, normed, keyvalues)


def two_heads(tile):
    left = lax.broadcasted_iota(jnp.int32, tile.shape, 1) < HD
    zero = jnp.zeros_like(tile)
    return jnp.concatenate([jnp.where(left, tile, zero), jnp.where(left, zero, tile)], 0)


def visible(first_key, starts, first_query):
    shape = (KEY_TILE, starts.shape[1])
    keys = first_key + lax.broadcasted_iota(jnp.int32, shape, 0)
    queries = first_query + lax.broadcasted_iota(jnp.int32, shape, 1)
    return (keys >= starts) & (keys <= queries)


def head_rows(first, second):
    shape = (HD, first.shape[1])
    return jnp.concatenate(
        [jnp.broadcast_to(first, shape), jnp.broadcast_to(second, shape)], 0
    )


def attend_kernel(halo, low_ref, query_ref, keyvalue_ref, start_ref, out_ref, log_ref):
    seq = pl.program_id(0)
    block = query_ref.shape[1]
    width = query_ref.shape[2]
    pairs = width // PAIR
    after = lambda c: slice(width + c.start, width + c.stop)
    tiles = block // QUERY_TILE
    def rows(tile, nothing):
        here = pl.ds(pl.multiple_of(tile * QUERY_TILE, QUERY_TILE), QUERY_TILE)
        starts = start_ref[0, :, here]
        cols = [slice(p * PAIR, (p + 1) * PAIR) for p in range(pairs)]

        def step(j, carry):
            place = pl.ds(pl.multiple_of(j * KEY_TILE, KEY_TILE), KEY_TILE)
            ok = visible(j * KEY_TILE, starts, halo + tile * QUERY_TILE)
            scores = [
                dot(two_heads(keyvalue_ref[0, place, c]), query_ref[0, here, c] * 0.125, NT)
                for c in cols
            ]
            left = []
            for p in range(pairs):
                highs, totals, mixed = carry[3 * p : 3 * p + 3]
                powers, fades, sums, nexts = [], [], [], []
                for h in range(2):
                    part = jnp.where(ok, scores[p][h * KEY_TILE : (h + 1) * KEY_TILE], -1e30)
                    high = highs[h : h + 1]
                    later = jnp.maximum(high, jnp.max(part, 0, keepdims=True))
                    power = jnp.exp(part - later)
                    fade = jnp.exp(high - later)
                    sums.append(totals[h : h + 1] * fade + jnp.sum(power, 0, keepdims=True))
                    powers.append(power.astype(BF16))
                    fades.append(fade)
                    nexts.append(later)
                added = dot(
                    two_heads(keyvalue_ref[0, place, after(cols[p])]), jnp.concatenate(powers, 0), TN
                )
                left += [
                    jnp.concatenate(nexts, 0),
                    jnp.concatenate(sums, 0),
                    mixed * head_rows(*fades) + added,
                ]
            return tuple(left)

        row = jnp.zeros((2, QUERY_TILE), F32)
        done = lax.fori_loop(
            low_ref[seq * tiles + tile],
            (halo + (tile + 1) * QUERY_TILE) // KEY_TILE,
            step,
            (row - 1e30, row, jnp.zeros((PAIR, QUERY_TILE), F32)) * pairs,
        )
        for p in range(pairs):
            highs, totals, mixed = done[3 * p : 3 * p + 3]
            total = head_rows(totals[0:1], totals[1:2])
            out_ref[0, here, cols[p]] = jnp.transpose(mixed / total).astype(BF16)
            log_ref[0, p, :, here] = highs + jnp.log(totals)
        return nothing

    lax.fori_loop(0, tiles, rows, 0)


def attend(low, query, keyvalues, starts):
    seqs, block, width = query.shape
    length = keyvalues.shape[1]
    pairs = width // PAIR
    rows = pl.BlockSpec((1, block, width), lambda s, low: (s, 0, 0))
    full = pl.BlockSpec((1, length, 2 * width), lambda s, low: (s, 0, 0))
    return pl.pallas_call(
        functools.partial(attend_kernel, length - block),
        grid_spec=pltpu.PrefetchScalarGridSpec(
            num_scalar_prefetch=1,
            grid=(seqs,),
            in_specs=[rows, full, pl.BlockSpec((1, 1, block), lambda s, low: (s, 0, 0))],
            out_specs=[rows, pl.BlockSpec((1, pairs, 2, block), lambda s, low: (s, 0, 0, 0))],
        ),
        out_shape=[
            jax.ShapeDtypeStruct((seqs, block, width), BF16),
            jax.ShapeDtypeStruct((seqs, pairs, 2, block), F32),
        ],
        compiler_params=pltpu.CompilerParams(vmem_limit_bytes=VMEM_LIMIT),
        cost_estimate=pl.CostEstimate(
            flops=16 << 30, bytes_accessed=16 << 20, transcendentals=8 << 20
        ),
        name="attend",
    )(low, query, keyvalues, starts)


def attend_back_kernel(
    halo,
    low_ref,
    first_ref,
    query_ref,
    keyvalue_ref,
    start_ref,
    out_ref,
    grad_ref,
    log_ref,
    gquery_ref,
    gkeyvalue_ref,
    turned_ref,
    center_ref,
    sumk_ref,
    sumv_ref,
):
    seq = pl.program_id(0)
    block = query_ref.shape[1]
    width = query_ref.shape[2]
    pairs = width // PAIR
    after = lambda c: slice(width + c.start, width + c.stop)
    tiles = block // QUERY_TILE
    cols = [slice(p * PAIR, (p + 1) * PAIR) for p in range(pairs)]
    turned_ref[...] = jnp.zeros_like(turned_ref)
    for p in range(pairs):
        products = jnp.transpose(grad_ref[0, :, cols[p]].astype(F32) * out_ref[0, :, cols[p]].astype(F32))
        center_ref[p, 0:1, :] = jnp.sum(products[:HD], 0, keepdims=True)
        center_ref[p, 1:2, :] = jnp.sum(products[HD:], 0, keepdims=True)
    left = lax.broadcasted_iota(jnp.int32, (KEY_TILE, PAIR), 1) < HD

    def step(j, nothing):
        place = pl.ds(pl.multiple_of(j * KEY_TILE, KEY_TILE), KEY_TILE)
        sumk_ref[...] = jnp.zeros_like(sumk_ref)
        sumv_ref[...] = jnp.zeros_like(sumv_ref)
        def rows(tile, nothing):
            here = pl.ds(pl.multiple_of(tile * QUERY_TILE, QUERY_TILE), QUERY_TILE)
            last = (halo + (tile + 1) * QUERY_TILE) // KEY_TILE

            @pl.when((j >= low_ref[seq * tiles + tile]) & (j < last))
            def _():
                ok = visible(j * KEY_TILE, start_ref[0, :, here], halo + tile * QUERY_TILE)
                keys = [two_heads(keyvalue_ref[0, place, c]) for c in cols]
                queries = [query_ref[0, here, c] * 0.125 for c in cols]
                grads = [grad_ref[0, here, c] for c in cols]
                scores = [dot(k, q, NT) for k, q in zip(keys, queries)]
                gprobs = [
                    dot(two_heads(keyvalue_ref[0, place, after(c)]), g, NT) for c, g in zip(cols, grads)
                ]
                for p in range(pairs):
                    probs, gscores = [], []
                    for head in range(2):
                        part = slice(head * KEY_TILE, (head + 1) * KEY_TILE)
                        row = slice(head, head + 1)
                        prob = jnp.exp(
                            jnp.where(ok, scores[p][part] - log_ref[0, p, row, here], -1e30)
                        )
                        gscore = prob * (gprobs[p][part] - center_ref[p, row, here])
                        probs.append(prob.astype(BF16))
                        gscores.append(gscore.astype(BF16))
                    probs = jnp.concatenate(probs, 0)
                    gscores = jnp.concatenate(gscores, 0)
                    sumv_ref[p] += dot(probs, grads[p])
                    sumk_ref[p] += dot(gscores, queries[p])
                    turned_ref[p, :, here] += dot(keys[p], gscores, TN)

            return nothing

        lax.fori_loop(0, tiles, rows, 0)

        for p in range(pairs):
            gkeyvalue_ref[0, place, cols[p]] = jnp.where(
                left, sumk_ref[p, :KEY_TILE], sumk_ref[p, KEY_TILE:]
            ).astype(BF16)
            gkeyvalue_ref[0, place, after(cols[p])] = jnp.where(
                left, sumv_ref[p, :KEY_TILE], sumv_ref[p, KEY_TILE:]
            ).astype(BF16)
        return nothing

    lax.fori_loop(first_ref[seq], (halo + block) // KEY_TILE, step, 0)
    for p in range(pairs):
        gquery_ref[0, :, cols[p]] = (jnp.transpose(turned_ref[p]) * 0.125).astype(BF16)


def attend_back(low, first, query, keyvalues, starts, mixed, grad, logs):
    seqs, block, width = query.shape
    length = keyvalues.shape[1]
    pairs = width // PAIR
    rows = pl.BlockSpec((1, block, width), lambda s, low, first: (s, 0, 0))
    full = pl.BlockSpec((1, length, 2 * width), lambda s, low, first: (s, 0, 0))
    return pl.pallas_call(
        functools.partial(attend_back_kernel, length - block),
        grid_spec=pltpu.PrefetchScalarGridSpec(
            num_scalar_prefetch=2,
            grid=(seqs,),
            in_specs=[
                rows,
                full,
                pl.BlockSpec((1, 1, block), lambda s, low, first: (s, 0, 0)),
                rows,
                rows,
                pl.BlockSpec((1, pairs, 2, block), lambda s, low, first: (s, 0, 0, 0)),
            ],
            out_specs=[rows, full],
            scratch_shapes=[
                pltpu.VMEM((pairs, PAIR, block), F32),
                pltpu.VMEM((pairs, 8, block), F32),
                pltpu.VMEM((pairs, 2 * KEY_TILE, PAIR), F32),
                pltpu.VMEM((pairs, 2 * KEY_TILE, PAIR), F32),
            ],
        ),
        out_shape=[
            jax.ShapeDtypeStruct((seqs, block, width), BF16),
            jax.ShapeDtypeStruct((seqs, length, 2 * width), BF16),
        ],
        compiler_params=pltpu.CompilerParams(vmem_limit_bytes=VMEM_LIMIT),
        cost_estimate=pl.CostEstimate(
            flops=40 << 30, bytes_accessed=28 << 20, transcendentals=8 << 20
        ),
        name="attend_back",
    )(low, first, query, keyvalues, starts, mixed, grad, logs)


def slab_copies(slab_ref, merge_ref, up_ref, down_ref, sems):
    owners = slab_ref.shape[0]
    width = slab_ref.shape[2]
    rows = width // owners
    chunks = up_ref.shape[1] // width
    groups = [[], [], []]
    for owner in range(owners):
        here = pl.ds(owner * rows, rows)
        groups[0].append((slab_ref.at[owner, pl.ds(0, rows), :], merge_ref.at[here, :]))
        for c in range(chunks):
            groups[1].append(
                (
                    slab_ref.at[owner, pl.ds((1 + c) * rows, rows), :],
                    up_ref.at[here, pl.ds(c * width, width)],
                )
            )
        groups[2].append(
            (
                slab_ref.at[owner, pl.ds((1 + chunks) * rows, chunks * rows), :],
                down_ref.at[pl.ds(owner * chunks * rows, chunks * rows), :],
            )
        )
    return [
        [pltpu.make_async_copy(*pair, sems.at[k, n]) for n, pair in enumerate(group)]
        for k, group in enumerate(groups)
    ]


def mlp_kernel(
    factor_ref,
    mixed_ref,
    token_ref,
    teacher_ref,
    weight_ref,
    outbias_ref,
    gain_ref,
    shift_ref,
    upbias_ref,
    downbias_ref,
    slab_ref,
    layer_ref,
    gresid_ref,
    gmixed_ref,
    sums_ref,
    upsums_ref,
    gslab_ref,
    merge_ref,
    up_ref,
    down_ref,
    slope_ref,
    normed_ref,
    active_ref,
    ghidden_ref,
    gmlp_ref,
    gbranch_ref,
    split_ref,
    block_ref,
    sems,
    split_sems,
    block_sems,
):
    width = token_ref.shape[-1]
    hidden = up_ref.shape[1]
    step = pl.program_id(0)
    here = pl.ds(pl.multiple_of(step * MLP_TILE, MLP_TILE), MLP_TILE)
    copies = slab_copies(slab_ref, merge_ref, up_ref, down_ref, sems)

    def arrive(k):
        @pl.when(step == 0)
        def _():
            for copy in copies[k]:
                copy.wait()

    @pl.when(step == 0)
    def _():
        for group in copies:
            for copy in group:
                copy.start()
        sums_ref[...] = jnp.zeros_like(sums_ref)
        upsums_ref[...] = jnp.zeros_like(upsums_ref)

    arrive(0)
    resid = (
        token_ref[...].astype(F32) + dot(mixed_ref[here, :], merge_ref[...]) + outbias_ref[...]
    )
    unit, scale = norm_parts(resid)
    normed = (unit * gain_ref[...] + shift_ref[...]).astype(BF16)
    normed_ref[here, :] = normed
    arrive(1)
    cuts = [slice(c, c + MLP_CHUNK) for c in range(0, hidden, MLP_CHUNK)]
    result = resid + downbias_ref[...]
    for n, cols in enumerate(cuts):
        inner = dot(normed, up_ref[:, cols]) + upbias_ref[:, cols]
        square = inner * inner
        curve = jnp.tanh(0.7978845608028654 * (inner + 0.044715 * square * inner))
        half = 0.5 * (1.0 + curve)
        active = (half * inner).astype(BF16)
        active_ref[here, cols] = active
        slope_ref[:, cols] = half + 0.5 * inner * (1.0 - curve * curve) * (
            0.7978845608028654 * (1.0 + 3.0 * 0.044715 * square)
        )
        if n == 0:
            arrive(2)
        result += dot(active_ref[here, cols], down_ref[cols, :])
    layer_ref[...] = result.astype(BF16)
    error = result - teacher_ref[...].astype(F32)
    weight = weight_ref[...]
    sums_ref[4:5, :] += jnp.sum(weight * (error * error), 0, keepdims=True)
    gresult = error * (weight * factor_ref[0])
    gmlp = gresult.astype(BF16)
    gmlp_ref[here, :] = gmlp
    sums_ref[3:4, :] += jnp.sum(gmlp.astype(F32), 0, keepdims=True)
    gnormed = jnp.zeros_like(result)
    for cols in cuts:
        gactive = dot(gmlp, down_ref[cols, :], NT)
        ghidden = (gactive * slope_ref[:, cols]).astype(BF16)
        ghidden_ref[here, cols] = ghidden
        upsums_ref[0:1, cols] += jnp.sum(ghidden.astype(F32), 0, keepdims=True)
        gnormed += dot(ghidden_ref[here, cols], up_ref[:, cols], NT)
    sums_ref[1:2, :] += jnp.sum(gnormed * unit, 0, keepdims=True)
    sums_ref[2:3, :] += jnp.sum(gnormed, 0, keepdims=True)
    gresid = gresult + norm_back(gnormed, gain_ref[...], unit, scale)
    gresid_ref[...] = gresid
    gbranch = gresid.astype(BF16)
    gbranch_ref[here, :] = gbranch
    sums_ref[0:1, :] += jnp.sum(gbranch.astype(F32), 0, keepdims=True)
    gmixed_ref[...] = dot(gbranch, merge_ref[...], NT).astype(BF16)

    owners, rows, _ = split_ref.shape[1:]
    chunks = hidden // width
    share = owners // chunks

    def split_copy(index):
        return pltpu.make_async_copy(
            split_ref.at[index % 2],
            gslab_ref.at[:, pl.ds(pl.multiple_of(index * rows, 16), rows), :],
            split_sems.at[index % 2],
        )

    def block_copy(index):
        return pltpu.make_async_copy(
            block_ref.at[index % 2],
            gslab_ref.at[
                pl.ds(index * share, share), pl.ds((1 + chunks) * rows, chunks * rows), :
            ],
            block_sems.at[index % 2],
        )

    @pl.when(step == pl.num_programs(0) - 1)
    def _():
        out = dot(mixed_ref[...], gbranch_ref[...], TN).astype(BF16)
        split_ref[0] = out.reshape(owners, rows, width)
        split_copy(0).start()

        def ups(index, nothing):
            @pl.when(index >= 2)
            def _():
                split_copy(index - 2).wait()

            cols = pl.ds(pl.multiple_of((index - 1) * width, 128), width)
            out = dot(normed_ref[...], ghidden_ref[:, cols], TN).astype(BF16)
            split_ref[index % 2] = out.reshape(owners, rows, width)
            split_copy(index).start()
            return nothing

        lax.fori_loop(1, chunks + 1, ups, 0)

        def downs(index, nothing):
            @pl.when(index >= 2)
            def _():
                block_copy(index - 2).wait()

            cols = pl.ds(pl.multiple_of(index * width, 128), width)
            out = dot(active_ref[:, cols], gmlp_ref[...], TN).astype(BF16)
            block_ref[index % 2] = out.reshape(share, chunks * rows, width)
            block_copy(index).start()
            return nothing

        lax.fori_loop(0, chunks, downs, 0)
        split_copy(chunks - 1).wait()
        split_copy(chunks).wait()
        block_copy(chunks - 2).wait()
        block_copy(chunks - 1).wait()


def mlp(factor, mixed, tokens, teacher, weight, vectors, slab):
    rows, width = tokens.shape
    outbias, gain, shift, upbias, downbias = vectors
    hidden = upbias.shape[1]
    chunks = hidden // width
    owners = slab.shape[0]
    few = width // owners
    tile = lambda n: pl.BlockSpec((MLP_TILE, n), lambda i: (i, 0))
    fixed = lambda m, n: pl.BlockSpec((m, n), lambda i: (0, 0))
    anywhere = pl.BlockSpec(memory_space=pl.ANY)
    shape = jax.ShapeDtypeStruct
    return pl.pallas_call(
        mlp_kernel,
        grid=(rows // MLP_TILE,),
        in_specs=[
            pl.BlockSpec(memory_space=pltpu.SMEM),
            fixed(rows, width),
            tile(width),
            tile(width),
            tile(1),
            fixed(1, width),
            fixed(1, width),
            fixed(1, width),
            fixed(1, hidden),
            fixed(1, width),
            anywhere,
        ],
        out_specs=[
            tile(width),
            tile(width),
            tile(width),
            fixed(8, width),
            fixed(8, hidden),
            anywhere,
        ],
        out_shape=[
            shape((rows, width), BF16),
            shape((rows, width), F32),
            shape((rows, width), BF16),
            shape((8, width), F32),
            shape((8, hidden), F32),
            shape((owners, (1 + 2 * chunks) * few, width), BF16),
        ],
        scratch_shapes=[
            pltpu.VMEM((width, width), BF16),
            pltpu.VMEM((width, hidden), BF16),
            pltpu.VMEM((hidden, width), BF16),
            pltpu.VMEM((MLP_TILE, hidden), F32),
            pltpu.VMEM((rows, width), BF16),
            pltpu.VMEM((rows, hidden), BF16),
            pltpu.VMEM((rows, hidden), BF16),
            pltpu.VMEM((rows, width), BF16),
            pltpu.VMEM((rows, width), BF16),
            pltpu.VMEM((2, owners, few, width), BF16),
            pltpu.VMEM((2, owners // chunks, chunks * few, width), BF16),
            pltpu.SemaphoreType.DMA((3, owners * chunks)),
            pltpu.SemaphoreType.DMA((2,)),
            pltpu.SemaphoreType.DMA((2,)),
        ],
        compiler_params=pltpu.CompilerParams(vmem_limit_bytes=VMEM_LIMIT),
        cost_estimate=pl.CostEstimate(
            flops=6 * rows * width * (width + 2 * hidden),
            bytes_accessed=40 << 20,
            transcendentals=rows * hidden,
        ),
        name="mlp",
    )(factor, mixed, tokens, teacher, weight, outbias, gain, shift, upbias, downbias, slab)


def halo_back_kernel(
    low_ref,
    halo_any,
    grad_any,
    whole_any,
    out_any,
    sums_ref,
    halo_ref,
    grad_ref,
    out_ref,
    weight_ref,
    halo_sems,
    grad_sems,
    out_sems,
    sem,
):
    seqs, rows, width = halo_ref.shape
    tiles = rows // ROW_TILE
    weight = pltpu.make_async_copy(whole_any.at[:, pl.ds(width, 2 * width)], weight_ref, sem)
    weight.start()

    def arrive(seq, tile, at):
        return (
            pltpu.make_async_copy(
                halo_any.at[seq, at], halo_ref.at[seq, at], halo_sems.at[seq, tile]
            ),
            pltpu.make_async_copy(
                grad_any.at[seq, at], grad_ref.at[seq, at], grad_sems.at[seq, tile]
            ),
        )

    def leave(seq, tile, at):
        return pltpu.make_async_copy(
            out_ref.at[seq, at], out_any.at[seq, at], out_sems.at[seq, tile]
        )

    def begin(seq, tile, at):
        @pl.when(tile >= low_ref[seq])
        def _():
            for copy in arrive(seq, tile, at):
                copy.start()

        @pl.when(tile < low_ref[seq])
        def _():
            out_ref[seq, at, :] = jnp.zeros((ROW_TILE, width), BF16)
            leave(seq, tile, at).start()

    def work(seq, tile, at):
        for copy in arrive(seq, tile, at):
            copy.wait()
        grad = dot(grad_ref[seq, at, :], weight_ref[...], NT)
        unit, _ = norm_parts(halo_ref[seq, at, :].astype(F32))
        out_ref[seq, at, :] = grad.astype(BF16)
        leave(seq, tile, at).start()
        sums_ref[0:1, :] += jnp.sum(grad * unit, 0, keepdims=True)
        sums_ref[1:2, :] += jnp.sum(grad, 0, keepdims=True)

    def end(seq, tile, at):
        leave(seq, tile, at).wait()

    every_tile(low_ref, seqs, tiles, begin, every=True)
    sums_ref[...] = jnp.zeros_like(sums_ref)
    weight.wait()
    every_tile(low_ref, seqs, tiles, work)
    every_tile(low_ref, seqs, tiles, end, every=True)


def halo_back(low, halo, gkeyvalues, whole):
    seqs, rows, width = halo.shape
    tiles = rows // ROW_TILE
    anywhere = pl.BlockSpec(memory_space=pl.ANY)
    return pl.pallas_call(
        halo_back_kernel,
        grid_spec=pltpu.PrefetchScalarGridSpec(
            num_scalar_prefetch=1,
            grid=(1,),
            in_specs=[anywhere, anywhere, anywhere],
            out_specs=[anywhere, pl.BlockSpec((8, width), lambda i, low: (0, 0))],
            scratch_shapes=[
                pltpu.VMEM((seqs, rows, width), BF16),
                pltpu.VMEM((seqs, rows, 2 * width), BF16),
                pltpu.VMEM((seqs, rows, width), BF16),
                pltpu.VMEM((width, 2 * width), BF16),
                pltpu.SemaphoreType.DMA((seqs, tiles)),
                pltpu.SemaphoreType.DMA((seqs, tiles)),
                pltpu.SemaphoreType.DMA((seqs, tiles)),
                pltpu.SemaphoreType.DMA,
            ],
        ),
        out_shape=[
            jax.ShapeDtypeStruct((seqs, rows, width), BF16),
            jax.ShapeDtypeStruct((8, width), F32),
        ],
        compiler_params=pltpu.CompilerParams(vmem_limit_bytes=VMEM_LIMIT),
        cost_estimate=pl.CostEstimate(
            flops=4 << 30, bytes_accessed=16 << 20, transcendentals=0
        ),
        name="halo_back",
    )(low, halo, gkeyvalues, whole)


def own_back_kernel(
    low_ref,
    order_ref,
    own_any,
    normed_any,
    gquery_any,
    gkeyvalue_any,
    whole_any,
    gnormed_any,
    keep_any,
    give_any,
    sums_ref,
    own_ref,
    normed_ref,
    gquery_ref,
    gkeyvalue_ref,
    weight_ref,
    total_ref,
    gnormed_ref,
    gweight_ref,
    sems,
    out_sems,
):
    seqs, block, width = own_ref.shape
    halo = normed_ref.shape[1] - block
    tiles = halo // ROW_TILE
    here = pl.ds(halo, block)
    before = pl.ds(0, halo)
    first = [
        pltpu.make_async_copy(normed_any.at[:, here], normed_ref.at[:, here], sems.at[0]),
        pltpu.make_async_copy(gkeyvalue_any.at[:, here], gkeyvalue_ref.at[:, here], sems.at[1]),
        pltpu.make_async_copy(gquery_any, gquery_ref, sems.at[2]),
    ]
    later = [
        pltpu.make_async_copy(normed_any.at[:, before], normed_ref.at[:, before], sems.at[3]),
        pltpu.make_async_copy(gkeyvalue_any.at[:, before], gkeyvalue_ref.at[:, before], sems.at[4]),
    ]
    last = [
        pltpu.make_async_copy(whole_any, weight_ref, sems.at[5]),
        pltpu.make_async_copy(own_any, own_ref, sems.at[6]),
    ]
    for copy in first + later + last:
        copy.start()
    for copy in first:
        copy.wait()
    rows = seqs * block
    gweight_ref[:, :width] = dot(
        normed_ref[:, halo:, :].reshape(rows, width), gquery_ref[...].reshape(rows, width), TN
    ).astype(BF16)

    def whole(k, nothing):
        cols = pl.ds(pl.multiple_of(k * width, 128), width)
        total_ref[:, cols] = dot(
            normed_ref[:, halo:, :].reshape(rows, width),
            gkeyvalue_ref[:, halo:, cols].reshape(rows, width),
            TN,
        )
        return nothing

    lax.fori_loop(0, 2, whole, 0)
    sums_ref[...] = jnp.zeros_like(sums_ref)
    sums_ref[2:3, :] = jnp.sum(
        gquery_ref[...].reshape(rows, width).astype(F32), 0, keepdims=True
    )
    sums_ref[3:4, :] = jnp.sum(
        gkeyvalue_ref[:, halo:, width:].reshape(rows, width).astype(F32), 0, keepdims=True
    )
    for copy in later:
        copy.wait()

    def add(seq, tile, at):
        total_ref[...] += dot(normed_ref[seq, at, :], gkeyvalue_ref[seq, at, :], TN)
        sums_ref[3:4, :] += jnp.sum(gkeyvalue_ref[seq, at, width:].astype(F32), 0, keepdims=True)

    every_tile(low_ref, seqs, tiles, add)
    gweight_ref[:, width:] = total_ref[...].astype(BF16)
    slots = keep_any.shape[0]
    share = width // (2 * slots)
    sends = [
        pltpu.make_async_copy(
            gweight_ref.at[pl.ds(pl.multiple_of(order_ref[k] * share, 16), share), :],
            (keep_any, give_any)[k // slots].at[k % slots, pl.ds(0, share), :],
            out_sems.at[1 + k],
        )
        for k in range(2 * slots)
    ]
    for copy in sends:
        copy.start()
    for copy in last:
        copy.wait()

    def lead(seq, nothing):
        grad = dot(gquery_ref[seq], weight_ref[:, :width], NT)
        grad += dot(gkeyvalue_ref[seq, halo:, :], weight_ref[:, width:], NT)
        gnormed_ref[seq] = grad
        unit, _ = norm_parts(own_ref[seq].astype(F32))
        sums_ref[0:1, :] += jnp.sum(grad * unit, 0, keepdims=True)
        sums_ref[1:2, :] += jnp.sum(grad, 0, keepdims=True)
        return nothing

    lax.fori_loop(0, seqs, lead, 0)
    back = pltpu.make_async_copy(gnormed_ref, gnormed_any, out_sems.at[0])
    back.start()
    for copy in sends:
        copy.wait()
    back.wait()


def own_back(low, order, own, normed, gquery, gkeyvalues, whole):
    seqs, block, width = own.shape
    length = normed.shape[1]
    anywhere = pl.BlockSpec(memory_space=pl.ANY)
    return pl.pallas_call(
        own_back_kernel,
        grid_spec=pltpu.PrefetchScalarGridSpec(
            num_scalar_prefetch=2,
            grid=(1,),
            in_specs=[anywhere] * 5,
            out_specs=[
                anywhere,
                anywhere,
                anywhere,
                pl.BlockSpec((8, width), lambda i, low, order: (0, 0)),
            ],
            scratch_shapes=[
                pltpu.VMEM((seqs, block, width), BF16),
                pltpu.VMEM((seqs, length, width), BF16),
                pltpu.VMEM((seqs, block, width), BF16),
                pltpu.VMEM((seqs, length, 2 * width), BF16),
                pltpu.VMEM((width, 3 * width), BF16),
                pltpu.VMEM((width, 2 * width), F32),
                pltpu.VMEM((seqs, block, width), F32),
                pltpu.VMEM((width, 3 * width), BF16),
                pltpu.SemaphoreType.DMA((7,)),
                pltpu.SemaphoreType.DMA((1 + SHARES,)),
            ],
        ),
        out_shape=[
            jax.ShapeDtypeStruct((seqs, block, width), F32),
            jax.ShapeDtypeStruct((SHARES // 2, width // SHARES + SMALL_ROWS, 3 * width), BF16),
            jax.ShapeDtypeStruct((SHARES // 2, width // SHARES + SMALL_ROWS, 3 * width), BF16),
            jax.ShapeDtypeStruct((8, width), F32),
        ],
        compiler_params=pltpu.CompilerParams(vmem_limit_bytes=VMEM_LIMIT),
        cost_estimate=pl.CostEstimate(
            flops=16 << 30, bytes_accessed=24 << 20, transcendentals=0
        ),
        name="own_back",
    )(low, order, own, normed, gquery, gkeyvalues, whole)


def finish_kernel(own_ref, gnormed_ref, gresid_ref, gain_ref, *rest):
    more_refs, (out_ref, total_ref) = rest[:-2], rest[-2:]
    start = 0
    for more_ref in more_refs:
        end = start + more_ref.shape[1]
        total_ref[start:end, :] = gnormed_ref[0, start:end, :] + more_ref[0].astype(F32)
        start = end

    def one(t, nothing):
        at = pl.ds(pl.multiple_of(t * HALO_CHUNK, HALO_CHUNK), HALO_CHUNK)
        unit, scale = norm_parts(own_ref[0, at, :].astype(F32))
        out_ref[0, at, :] = (
            gresid_ref[0, at, :] + norm_back(total_ref[at, :], gain_ref[...], unit, scale)
        ).astype(BF16)
        return nothing

    lax.fori_loop(0, own_ref.shape[1] // HALO_CHUNK, one, 0)


def finish(own, gnormed, more, gresid, gain):
    seqs, block, width = own.shape
    whole = lambda rows: pl.BlockSpec((1, rows, width), lambda s: (s, 0, 0))
    tile = whole(block)
    return pl.pallas_call(
        finish_kernel,
        grid=(seqs,),
        in_specs=[tile, tile, tile, pl.BlockSpec((1, width), lambda s: (0, 0))]
        + [whole(part.shape[1]) for part in more],
        out_specs=tile,
        out_shape=jax.ShapeDtypeStruct(own.shape, BF16),
        scratch_shapes=[pltpu.VMEM((block, width), F32)],
        cost_estimate=pl.CostEstimate(
            flops=20 * seqs * block * width,
            bytes_accessed=14 * seqs * block * width,
            transcendentals=0,
        ),
        name="finish",
    )(own, gnormed, gresid, gain, *more)


def swap(x, axis, bit):
    size = lax.axis_size(axis)
    return lax.ppermute(x, axis, [(i, i ^ bit) for i in range(size)])


def shift(x, axis, step):
    size = lax.axis_size(axis)
    return lax.ppermute(
        x, axis, [(i, i + step) for i in range(size) if 0 <= i + step < size]
    )


def sum_over(x, axis):
    bit = 1
    while bit < lax.axis_size(axis):
        x = x + swap(x, axis, bit)
        bit *= 2
    return x


def max_over(x, axis):
    bit = 1
    while bit < lax.axis_size(axis):
        x = jnp.maximum(x, swap(x, axis, bit))
        bit *= 2
    return x


def gather_near(shard):
    size = lax.axis_size("fsdp")
    if size != 8:
        return [lax.all_gather(shard, "fsdp", axis=0, tiled=True)]
    return [shard] + [swap(shard, "fsdp", 2 * d) for d in range(1, size // 2)]


def gather_rest(near):
    if lax.axis_size("fsdp") != 8:
        return near
    return near + [swap(piece, "fsdp", 1) for piece in near]


def piece_order():
    size = lax.axis_size("fsdp")
    me = lax.axis_index("fsdp").astype(jnp.int32)
    if size != 8:
        return jnp.zeros((1,), jnp.int32)
    return jnp.stack(
        [me ^ (2 * d) for d in range(size // 2)] + [me ^ (2 * d) ^ 1 for d in range(size // 2)]
    )


def sum_seq(total):
    if lax.axis_size("seq") != 4:
        return lax.psum(total, "seq")
    return sum_seq_rest(sum_seq_second(sum_seq_first(total)))


def sum_seq_first(total):
    rows, columns = total.shape
    odd = lax.axis_index("seq") % 2
    halves = total.reshape(2, rows // 2, columns)
    pick = lambda k: lax.dynamic_index_in_dim(halves, k, 0, keepdims=False)
    return (pick(odd).astype(F32) + swap(pick(1 - odd), "seq", 1).astype(F32)).astype(BF16)


def sum_seq_second(half):
    return (half.astype(F32) + swap(half, "seq", 2).astype(F32)).astype(BF16)


def sum_seq_rest(half):
    odd = lax.axis_index("seq") % 2
    back = swap(half, "seq", 1)
    return jnp.where(
        odd == 0, jnp.concatenate([half, back], 0), jnp.concatenate([back, half], 0)
    )


def reduce_rows(keep, give, half, *first):
    other = swap(give, "fsdp", 1)
    staged = lax.axis_size("seq") == 4
    if staged:
        half = sum_seq_first(half)
    mine = [
        (keep[d].astype(F32) + other[d].astype(F32)).astype(BF16) for d in range(keep.shape[0])
    ]
    arrived = [swap(part, "fsdp", 2 * d) for d, part in enumerate(mine) if d > 0]
    arrived, half, *first = lax.optimization_barrier((arrived, half, *first))
    total = mine[0].astype(F32)
    for part in arrived:
        total = total + part.astype(F32)
    total = total.astype(BF16)
    if not staged:
        return lax.psum(total, "seq"), half, *first
    total, half = sum_seq_first(total), sum_seq_second(half)
    total, half = lax.optimization_barrier((total, half))
    return sum_seq_rest(sum_seq_second(total)), sum_seq_rest(half), *first


def gather_slab(outweight, fcweight, projweight, *first):
    width = outweight.shape[1]
    cuts = fcweight.shape[1] // width

    def join(out, up, down, axis):
        ups = [lax.slice_in_dim(up, c * width, (c + 1) * width, axis=-1) for c in range(cuts)]
        return jnp.concatenate([out, *ups, down], axis)

    if lax.axis_size("fsdp") == SHARES:
        slab = join(outweight, fcweight, projweight, 0)
        slab, *first = lax.optimization_barrier((slab, *first))
        return lax.all_gather(slab, "fsdp", axis=0, tiled=False), *first
    whole = [
        lax.all_gather(w, "fsdp", axis=0, tiled=True) for w in (outweight, fcweight, projweight)
    ]
    return join(*(w.reshape(SHARES, -1, w.shape[1]) for w in whole), 1), *first


def reduce_slab(slab, width, hidden):
    owners = lax.axis_size("fsdp")
    cuts = hidden // width
    rows = width // SHARES

    def part(array, axis):
        at = lambda a, b: lax.slice_in_dim(array, a * rows, b * rows, axis=axis)
        ups = [at(1 + c, 2 + c) for c in range(cuts)]
        return at(0, 1), jnp.concatenate(ups, -1), at(1 + cuts, 1 + 2 * cuts)

    if owners == SHARES:
        return part(slab.astype(F32), 0)
    return [
        lax.psum(
            lax.psum_scatter(
                g.reshape(-1, g.shape[-1]), "fsdp", scatter_dimension=0, tiled=True
            ),
            "seq",
        ).astype(F32)
        for g in part(slab, 1)
    ]


def local(
    tokens,
    teacher,
    segment_ids,
    latent_flags,
    valid_mask,
    attngain,
    attnshift,
    qkvweight,
    qvbias,
    outweight,
    outbias,
    mlpgain,
    mlpshift,
    fcweight,
    fcbias,
    projweight,
    projbias,
):
    seqs, block, width = tokens.shape
    groups = lax.axis_size("seq")
    owners = lax.axis_size("fsdp")
    rows = seqs * block
    halo_rows = (groups - 1) * block
    far_rows = halo_rows - block
    me = lax.axis_index("fsdp")
    place = lax.axis_index("seq").astype(jnp.int32)
    hidden = fcweight.shape[1]

    order = piece_order()
    qkv_pieces = gather_near(qkvweight)

    weight = (valid_mask * (1 - latent_flags)).astype(F32)
    below = jnp.sum(
        (segment_ids[:, :, None] < jnp.arange(1, 4, dtype=jnp.int32)).astype(jnp.int32), 1
    )
    facts = jnp.concatenate([below.reshape(-1), jnp.sum(weight).astype(jnp.int32)[None]])

    shards = [attngain, attnshift, qvbias, outbias, mlpgain, mlpshift, fcbias, projbias]
    sent = [tokens[k] for k in range(seqs)] + [tokens[:, block - HALO_CHUNK :]]
    bit = 1
    while bit < groups:
        facts = facts + swap(facts, "seq", bit)
        if bit == 1:
            facts, shards = lax.optimization_barrier((facts, shards))
        bit *= 2

    sent, facts = lax.optimization_barrier((sent, facts))
    near = [shift(sent[k], "seq", 1) for k in range(seqs)]
    far = shift(sent[seqs], "seq", 2) if far_rows > 0 else None
    bounds = facts[:-1].reshape(seqs, 3)

    def start_of(positions):
        found = jnp.zeros((seqs,) + positions.shape, jnp.int32)
        for d in range(3):
            bound = bounds[:, d].reshape((seqs,) + (1,) * positions.ndim)
            found = jnp.maximum(found, jnp.where(bound <= positions[None], bound, 0))
        return found

    firsts = jnp.arange(groups, dtype=jnp.int32) * block
    reach = jnp.max(firsts[None] - start_of(firsts)) - block
    chunks = jnp.maximum(reach + HALO_CHUNK - 1, 0) // HALO_CHUNK

    facts = jnp.stack([facts[-1], chunks])
    bit = 1
    while bit < owners:
        other = swap(facts, "fsdp", bit)
        facts = jnp.where(jnp.arange(2) == 1, jnp.maximum(facts, other), facts + other)
        bit *= 2

    packed = jnp.concatenate(
        [jnp.pad(v[None], ((0, 0), (0, -v.shape[0] % 128))) for v in shards], 1
    )
    table = jnp.where(
        lax.broadcasted_iota(jnp.int32, (owners, packed.shape[1]), 0) == me,
        packed,
        jnp.zeros((), BF16),
    )
    table = sum_over(table, "fsdp")

    qkv_pieces = gather_rest(qkv_pieces)
    slab, qkv_pieces, table, facts, near[0] = gather_slab(
        outweight, fcweight, projweight, qkv_pieces, table, facts, near[0]
    )
    count = facts[0].astype(F32)
    chunks = facts[1]

    vectors = []
    at = 0
    for shard in shards:
        size = shard.shape[0]
        vectors.append(table[:, at : at + size].reshape(1, size * owners).astype(F32))
        at += size + -size % 128
    gain1, shift1, bias1, outbias_v, gain2, shift2, upbias, downbias = vectors


    base = (place - (groups - 1)) * block
    starts = start_of(place * block + jnp.arange(block, dtype=jnp.int32)) - base
    low_rows = starts[:, ::QUERY_TILE]
    low = (low_rows // KEY_TILE).reshape(-1)
    low_tile = starts[:, 0] // ROW_TILE
    first = low_tile * (ROW_TILE // KEY_TILE)
    starts = starts[:, None, :]

    bias1 = jnp.concatenate([bias1[:, :width], jnp.zeros((1, width), F32), bias1[:, width:]], 1)
    normed, query, keyvalues, qkv = project_own(
        order, tokens, gain1, shift1, bias1, qkv_pieces, halo_rows + block
    )
    near[-1], query = lax.optimization_barrier((near[-1], query))
    halo = jnp.stack(near)
    if far_rows > 0:
        blank = jnp.zeros((seqs, far_rows - HALO_CHUNK, width), BF16)
        halo = jnp.concatenate([blank, far, halo], 1)

    def fetch(state):
        j, halo = state
        sent = lax.dynamic_slice_in_dim(halo, halo_rows - HALO_CHUNK * (j + 1), HALO_CHUNK, 1)
        came = shift(sent, "seq", 1)
        return j + 1, lax.dynamic_update_slice_in_dim(
            halo, came, far_rows - HALO_CHUNK * (j + 1), 1
        )

    if far_rows > 0:
        _, halo = lax.while_loop(lambda state: state[0] < chunks, fetch, (jnp.int32(1), halo))

    normed, keyvalues = project_halo(
        low_tile, halo, gain1, shift1, bias1, qkv, normed, keyvalues
    )
    mixed, logs = attend(low, query, keyvalues, starts)

    factor = (rows * owners * groups) / count
    layer_out, gresid, gmixed, sums, upsums, outer = mlp(
        factor.reshape(1),
        mixed.reshape(rows, width),
        tokens.reshape(rows, width),
        teacher.reshape(rows, width),
        weight.reshape(rows, 1),
        (outbias_v, gain2, shift2, upbias, downbias),
        slab,
    )

    small = jnp.concatenate(
        [upsums[0].reshape(SHARES, -1)] + [sums[k].reshape(SHARES, -1) for k in range(4)], 1
    )
    outer, gmixed = lax.optimization_barrier((outer, gmixed))
    staged = owners == SHARES and groups == 4
    if owners == SHARES:
        outer = lax.psum_scatter(outer, "fsdp", scatter_dimension=0, tiled=False)
        outer = outer if staged else sum_seq(outer)

    gquery, gkeyvalues = attend_back(
        low, first, query, keyvalues, starts, mixed, gmixed.reshape(seqs, block, width), logs
    )
    ghalo, halo_sums = halo_back(low_tile, halo, gkeyvalues, qkv)

    def give(state):
        j, ghalo = state
        j = j - 1
        sent = lax.dynamic_slice_in_dim(ghalo, far_rows - HALO_CHUNK * (j + 1), HALO_CHUNK, 1)
        came = shift(sent, "seq", -1)
        spot = halo_rows - HALO_CHUNK * (j + 1)
        held = lax.dynamic_slice_in_dim(ghalo, spot, HALO_CHUNK, 1)
        total = (held.astype(F32) + came.astype(F32)).astype(BF16)
        return j, lax.dynamic_update_slice_in_dim(ghalo, total, spot, 1)

    if far_rows > 0:
        _, ghalo = lax.while_loop(lambda state: state[0] > 1, give, (chunks, ghalo))

    ghalo, gquery = lax.optimization_barrier((ghalo, gquery))
    ends = far_rows + block - HALO_CHUNK
    cut = far_rows + (block - HALO_CHUNK) // 2
    closing = ghalo[:, ends:]
    came = shift(ghalo[:, far_rows - HALO_CHUNK : far_rows], "seq", -1) if far_rows > 0 else closing
    near = [shift(ghalo[:, far_rows:cut], "seq", -1), shift(ghalo[:, cut:ends], "seq", -1)]
    sort = order if owners == SHARES else jnp.arange(SHARES, dtype=jnp.int32)
    gnormed, keep, give, own_sums = own_back(
        low_tile, sort, tokens, normed, gquery, gkeyvalues, qkv
    )
    keep, give, own_sums, halo_sums, near[0], came = lax.optimization_barrier(
        (keep, give, own_sums, halo_sums, near[0], came)
    )
    if far_rows > 0:
        closing = (closing.astype(F32) + came.astype(F32)).astype(BF16)
    near.append(shift(closing, "seq", -1))
    late = jnp.concatenate(
        [(own_sums[k] + halo_sums[k]).reshape(SHARES, -1) for k in range(2)]
        + [own_sums[2:4].reshape(SHARES, -1)],
        1,
    ).astype(BF16)
    late = jnp.pad(late, ((0, 0), (0, width - late.shape[1])))
    loss_row = jnp.broadcast_to(sums[4:5].astype(BF16), (SHARES, width))
    late = jnp.concatenate([late, small.astype(BF16), loss_row], 1)
    slots = SHARES // 2
    late = jnp.stack([lax.dynamic_index_in_dim(late, sort[k], 0) for k in range(SHARES)])
    late = jnp.pad(late, ((0, 0), (0, SMALL_ROWS - 1), (0, 0)))
    share = width // SHARES
    keep = lax.dynamic_update_slice_in_dim(keep, late[:slots], share, 1)
    give = lax.dynamic_update_slice_in_dim(give, late[slots:], share, 1)

    grad_tokens = finish(
        tokens,
        gnormed,
        near,
        gresid.reshape(tokens.shape),
        gain1,
    )

    if owners == SHARES:
        joint, outer, grad_tokens = reduce_rows(keep, give, outer, grad_tokens)
    else:
        joint = jnp.concatenate([keep, give])
        small_late = lax.psum(joint[:, share].astype(F32), ("fsdp", "seq"))
        joint = joint[:, :share].reshape(width, 3 * width)
        joint = lax.psum_scatter(joint, "fsdp", scatter_dimension=0, tiled=True)
        joint = lax.psum(joint, "seq")
    joint = joint.astype(F32)
    grad_merge, grad_up, grad_down = reduce_slab(outer, width, hidden)

    share = width // owners
    at = hidden // SHARES
    wide = width // SHARES
    spots = [(0, wide), (wide, wide), (2 * wide, 2 * wide), (width, at)]
    spots += [(width + at + k * wide, wide) for k in range(4)]
    if owners == SHARES:
        cuts = [joint[share, start : start + size] for start, size in spots]
        loss_row = joint[share, 2 * width :]
    else:
        full = [small_late[:, start : start + size].reshape(-1) for start, size in spots]
        cuts = [
            lax.dynamic_slice_in_dim(v, me * (v.shape[0] // owners), v.shape[0] // owners)
            for v in full
        ]
        loss_row = small_late[0, 2 * width :]
    loss = jnp.sum(loss_row) / (width * count)
    return (
        loss,
        layer_out.reshape(tokens.shape),
        grad_tokens,
        cuts[0],
        cuts[1],
        joint[:share],
        cuts[2],
        grad_merge,
        cuts[4],
        cuts[5],
        cuts[6],
        grad_up,
        cuts[3],
        grad_down,
        cuts[7],
    )


def solution(mesh):
    placed = (
        P("fsdp", "seq", None),
        P("fsdp", "seq", None),
        P("fsdp", "seq"),
        P("fsdp", "seq"),
        P("fsdp", "seq"),
        P("fsdp"),
        P("fsdp"),
        P("fsdp", None),
        P("fsdp"),
        P("fsdp", None),
        P("fsdp"),
        P("fsdp"),
        P("fsdp"),
        P("fsdp", None),
        P("fsdp"),
        P("fsdp", None),
        P("fsdp"),
    )
    return jax.shard_map(
        local,
        mesh=mesh,
        in_specs=placed,
        out_specs=(
            P(),
            P("fsdp", "seq", None),
            P("fsdp", "seq", None),
            P("fsdp"),
            P("fsdp"),
            P("fsdp", None),
            P("fsdp"),
            P("fsdp", None),
            P("fsdp"),
            P("fsdp"),
            P("fsdp"),
            P("fsdp", None),
            P("fsdp"),
            P("fsdp", None),
            P("fsdp"),
        ),
        check_vma=False,
    )
```

```python
import functools

import jax
import jax.numpy as jnp
from jax import lax
from jax.experimental import pallas as pl
from jax.experimental.pallas import tpu as pltpu
from jax.sharding import PartitionSpec as P

H = 12
HD = 64
PAIR = 2 * HD
EPSILON = 1e-05
KEY_TILE = 128
QUERY_TILE = 128
ROW_TILE = 256
MLP_TILE = 256
MLP_CHUNK = 1536
HALO_CHUNK = 128
SHARES = 8
SMALL_ROWS = 16
VMEM_LIMIT = 62 * 1024 * 1024

NT = (((1,), (1,)), ((), ()))
NN = (((1,), (0,)), ((), ()))
TN = (((0,), (0,)), ((), ()))
F32 = jnp.float32
BF16 = jnp.bfloat16


def dot(left, right, dims=NN):
    return lax.dot_general(left, right, dims, preferred_element_type=F32)


def norm_parts(values):
    center = values - jnp.mean(values, -1, keepdims=True)
    spread = jnp.mean(center * center, -1, keepdims=True)
    scale = lax.rsqrt(spread + EPSILON)
    return center * scale, scale


def norm_back(grad, gain, unit, scale):
    weighted = grad * gain
    first = jnp.mean(weighted, -1, keepdims=True)
    second = jnp.mean(weighted * unit, -1, keepdims=True)
    return scale * (weighted - first - unit * second)


def piece_copies(order_ref, pieces, whole_ref, sems):
    copies = []
    for place, piece in enumerate(pieces):
        rows = piece.shape[0]
        if len(pieces) == 1:
            target = whole_ref
        else:
            target = whole_ref.at[pl.ds(pl.multiple_of(order_ref[place] * rows, 16), rows), :]
        copies.append(pltpu.make_async_copy(piece, target, sems.at[place]))
    return copies


def project_own_kernel(count, order_ref, own_ref, gain_ref, shift_ref, bias_ref, *rest):
    pieces = rest[:count]
    normed_ref, query_ref, keyvalue_ref, whole_ref, weight_ref, sems, whole_sem = rest[count:]
    width = own_ref.shape[-1]
    seq = pl.program_id(0)
    whole = pltpu.make_async_copy(weight_ref, whole_ref, whole_sem)

    @pl.when(seq == 0)
    def _():
        copies = piece_copies(order_ref, pieces, weight_ref, sems)
        for copy in copies:
            copy.start()
        for copy in copies:
            copy.wait()
        whole.start()

    unit, _ = norm_parts(own_ref[0].astype(F32))
    normed = (unit * gain_ref[...] + shift_ref[...]).astype(BF16)
    normed_ref[0] = normed
    joint = (dot(normed, weight_ref[...]) + bias_ref[...]).astype(BF16)
    query_ref[0] = joint[:, :width]
    keyvalue_ref[0] = joint[:, width:]

    @pl.when(seq == pl.num_programs(0) - 1)
    def _():
        whole.wait()


def project_own(order, own, gain, shift, bias, pieces, length):
    seqs, block, width = own.shape
    last = length // block - 1
    fixed = lambda s, order: (0, 0)
    spot = lambda s, order: (s, 0, 0)
    end = lambda s, order: (s, last, 0)
    return pl.pallas_call(
        functools.partial(project_own_kernel, len(pieces)),
        grid_spec=pltpu.PrefetchScalarGridSpec(
            num_scalar_prefetch=1,
            grid=(seqs,),
            in_specs=[
                pl.BlockSpec((1, block, width), spot),
                pl.BlockSpec((1, width), fixed),
                pl.BlockSpec((1, width), fixed),
                pl.BlockSpec((1, 3 * width), fixed),
            ]
            + [pl.BlockSpec(memory_space=pl.ANY)] * len(pieces),
            out_specs=[
                pl.BlockSpec((1, block, width), end),
                pl.BlockSpec((1, block, width), spot),
                pl.BlockSpec((1, block, 2 * width), end),
                pl.BlockSpec(memory_space=pl.ANY),
            ],
            scratch_shapes=[
                pltpu.VMEM((width, 3 * width), BF16),
                pltpu.SemaphoreType.DMA((len(pieces),)),
                pltpu.SemaphoreType.DMA,
            ],
        ),
        out_shape=[
            jax.ShapeDtypeStruct((seqs, length, width), BF16),
            jax.ShapeDtypeStruct((seqs, block, width), BF16),
            jax.ShapeDtypeStruct((seqs, length, 2 * width), BF16),
            jax.ShapeDtypeStruct((width, 3 * width), BF16),
        ],
        compiler_params=pltpu.CompilerParams(vmem_limit_bytes=VMEM_LIMIT),
        cost_estimate=pl.CostEstimate(
            flops=6 * seqs * block * width * width, bytes_accessed=16 << 20, transcendentals=0
        ),
        name="project_own",
    )(order, own, gain, shift, bias, *pieces)


def every_tile(low_ref, seqs, tiles, work, every=False):
    for seq in range(seqs):

        def one(tile, nothing):
            work(seq, tile, pl.ds(pl.multiple_of(tile * ROW_TILE, ROW_TILE), ROW_TILE))
            return nothing

        lax.fori_loop(0 if every else low_ref[seq], tiles, one, 0)


def project_halo_kernel(
    low_ref, gain_ref, shift_ref, bias_ref, halo_any, whole_any, *rest
):
    (
        normed_any,
        keyvalue_any,
        halo_ref,
        normed_ref,
        keyvalue_ref,
        weight_ref,
        in_sems,
        normed_sems,
        keyvalue_sems,
        sem,
    ) = rest[2:]
    seqs, rows, width = halo_ref.shape
    tiles = rows // ROW_TILE
    weight = pltpu.make_async_copy(whole_any.at[:, pl.ds(width, 2 * width)], weight_ref, sem)
    weight.start()

    def arrive(seq, tile, at):
        return pltpu.make_async_copy(
            halo_any.at[seq, at], halo_ref.at[seq, at], in_sems.at[seq, tile]
        )

    def leave(seq, tile, at):
        return (
            pltpu.make_async_copy(
                normed_ref.at[seq, at], normed_any.at[seq, at], normed_sems.at[seq, tile]
            ),
            pltpu.make_async_copy(
                keyvalue_ref.at[seq, at], keyvalue_any.at[seq, at], keyvalue_sems.at[seq, tile]
            ),
        )

    def begin(seq, tile, at):
        arrive(seq, tile, at).start()

    def work(seq, tile, at):
        arrive(seq, tile, at).wait()
        unit, _ = norm_parts(halo_ref[seq, at, :].astype(F32))
        normed = (unit * gain_ref[...] + shift_ref[...]).astype(BF16)
        normed_ref[seq, at, :] = normed
        keyvalue_ref[seq, at, :] = (
            dot(normed, weight_ref[...]) + bias_ref[:, width:]
        ).astype(BF16)
        for copy in leave(seq, tile, at):
            copy.start()

    def end(seq, tile, at):
        for copy in leave(seq, tile, at):
            copy.wait()

    every_tile(low_ref, seqs, tiles, begin)
    weight.wait()
    every_tile(low_ref, seqs, tiles, work)
    every_tile(low_ref, seqs, tiles, end)


def project_halo(low, halo, gain, shift, bias, whole, normed, keyvalues):
    seqs, rows, width = halo.shape
    tiles = rows // ROW_TILE
    fixed = lambda i, low: (0, 0)
    anywhere = pl.BlockSpec(memory_space=pl.ANY)
    return pl.pallas_call(
        project_halo_kernel,
        grid_spec=pltpu.PrefetchScalarGridSpec(
            num_scalar_prefetch=1,
            grid=(1,),
            in_specs=[
                pl.BlockSpec((1, width), fixed),
                pl.BlockSpec((1, width), fixed),
                pl.BlockSpec((1, 3 * width), fixed),
                anywhere,
                anywhere,
                anywhere,
                anywhere,
            ],
            out_specs=[anywhere, anywhere],
            scratch_shapes=[
                pltpu.VMEM((seqs, rows, width), BF16),
                pltpu.VMEM((seqs, rows, width), BF16),
                pltpu.VMEM((seqs, rows, 2 * width), BF16),
                pltpu.VMEM((width, 2 * width), BF16),
                pltpu.SemaphoreType.DMA((seqs, tiles)),
                pltpu.SemaphoreType.DMA((seqs, tiles)),
                pltpu.SemaphoreType.DMA((seqs, tiles)),
                pltpu.SemaphoreType.DMA,
            ],
        ),
        out_shape=[
            jax.ShapeDtypeStruct(normed.shape, BF16),
            jax.ShapeDtypeStruct(keyvalues.shape, BF16),
        ],
        input_output_aliases={6: 0, 7: 1},
        compiler_params=pltpu.CompilerParams(vmem_limit_bytes=VMEM_LIMIT),
        cost_estimate=pl.CostEstimate(
            flops=2 * seqs * rows * width * width, bytes_accessed=16 << 20, transcendentals=0
        ),
        name="project_halo",
    )(low, gain, shift, bias, halo, whole, normed, keyvalues)


def two_heads(tile):
    left = lax.broadcasted_iota(jnp.int32, tile.shape, 1) < HD
    zero = jnp.zeros_like(tile)
    return jnp.concatenate([jnp.where(left, tile, zero), jnp.where(left, zero, tile)], 0)


def visible(first_key, starts, first_query):
    shape = (KEY_TILE, starts.shape[1])
    keys = first_key + lax.broadcasted_iota(jnp.int32, shape, 0)
    queries = first_query + lax.broadcasted_iota(jnp.int32, shape, 1)
    return (keys >= starts) & (keys <= queries)


def head_rows(first, second):
    shape = (HD, first.shape[1])
    return jnp.concatenate(
        [jnp.broadcast_to(first, shape), jnp.broadcast_to(second, shape)], 0
    )


def attend_kernel(halo, low_ref, query_ref, keyvalue_ref, start_ref, out_ref, log_ref):
    seq = pl.program_id(0)
    block = query_ref.shape[1]
    width = query_ref.shape[2]
    pairs = width // PAIR
    after = lambda c: slice(width + c.start, width + c.stop)
    tiles = block // QUERY_TILE
    def rows(tile, nothing):
        here = pl.ds(pl.multiple_of(tile * QUERY_TILE, QUERY_TILE), QUERY_TILE)
        starts = start_ref[0, :, here]
        cols = [slice(p * PAIR, (p + 1) * PAIR) for p in range(pairs)]

        def step(j, carry):
            place = pl.ds(pl.multiple_of(j * KEY_TILE, KEY_TILE), KEY_TILE)
            ok = visible(j * KEY_TILE, starts, halo + tile * QUERY_TILE)
            scores = [
                dot(two_heads(keyvalue_ref[0, place, c]), query_ref[0, here, c] * 0.125, NT)
                for c in cols
            ]
            left = []
            for p in range(pairs):
                highs, totals, mixed = carry[3 * p : 3 * p + 3]
                powers, fades, sums, nexts = [], [], [], []
                for h in range(2):
                    part = jnp.where(ok, scores[p][h * KEY_TILE : (h + 1) * KEY_TILE], -1e30)
                    high = highs[h : h + 1]
                    later = jnp.maximum(high, jnp.max(part, 0, keepdims=True))
                    power = jnp.exp(part - later)
                    fade = jnp.exp(high - later)
                    sums.append(totals[h : h + 1] * fade + jnp.sum(power, 0, keepdims=True))
                    powers.append(power.astype(BF16))
                    fades.append(fade)
                    nexts.append(later)
                added = dot(
                    two_heads(keyvalue_ref[0, place, after(cols[p])]), jnp.concatenate(powers, 0), TN
                )
                left += [
                    jnp.concatenate(nexts, 0),
                    jnp.concatenate(sums, 0),
                    mixed * head_rows(*fades) + added,
                ]
            return tuple(left)

        row = jnp.zeros((2, QUERY_TILE), F32)
        done = lax.fori_loop(
            low_ref[seq * tiles + tile],
            (halo + (tile + 1) * QUERY_TILE) // KEY_TILE,
            step,
            (row - 1e30, row, jnp.zeros((PAIR, QUERY_TILE), F32)) * pairs,
        )
        for p in range(pairs):
            highs, totals, mixed = done[3 * p : 3 * p + 3]
            total = head_rows(totals[0:1], totals[1:2])
            out_ref[0, here, cols[p]] = jnp.transpose(mixed / total).astype(BF16)
            log_ref[0, p, :, here] = highs + jnp.log(totals)
        return nothing

    lax.fori_loop(0, tiles, rows, 0)


def attend(low, query, keyvalues, starts):
    seqs, block, width = query.shape
    length = keyvalues.shape[1]
    pairs = width // PAIR
    rows = pl.BlockSpec((1, block, width), lambda s, low: (s, 0, 0))
    full = pl.BlockSpec((1, length, 2 * width), lambda s, low: (s, 0, 0))
    return pl.pallas_call(
        functools.partial(attend_kernel, length - block),
        grid_spec=pltpu.PrefetchScalarGridSpec(
            num_scalar_prefetch=1,
            grid=(seqs,),
            in_specs=[rows, full, pl.BlockSpec((1, 1, block), lambda s, low: (s, 0, 0))],
            out_specs=[rows, pl.BlockSpec((1, pairs, 2, block), lambda s, low: (s, 0, 0, 0))],
        ),
        out_shape=[
            jax.ShapeDtypeStruct((seqs, block, width), BF16),
            jax.ShapeDtypeStruct((seqs, pairs, 2, block), F32),
        ],
        compiler_params=pltpu.CompilerParams(vmem_limit_bytes=VMEM_LIMIT),
        cost_estimate=pl.CostEstimate(
            flops=16 << 30, bytes_accessed=16 << 20, transcendentals=8 << 20
        ),
        name="attend",
    )(low, query, keyvalues, starts)


def attend_back_kernel(
    halo,
    low_ref,
    first_ref,
    query_ref,
    keyvalue_ref,
    start_ref,
    out_ref,
    grad_ref,
    log_ref,
    gquery_ref,
    gkeyvalue_ref,
    turned_ref,
    center_ref,
    sumk_ref,
    sumv_ref,
):
    seq = pl.program_id(0)
    block = query_ref.shape[1]
    width = query_ref.shape[2]
    pairs = width // PAIR
    after = lambda c: slice(width + c.start, width + c.stop)
    tiles = block // QUERY_TILE
    cols = [slice(p * PAIR, (p + 1) * PAIR) for p in range(pairs)]
    turned_ref[...] = jnp.zeros_like(turned_ref)
    for p in range(pairs):
        products = jnp.transpose(grad_ref[0, :, cols[p]].astype(F32) * out_ref[0, :, cols[p]].astype(F32))
        center_ref[p, 0:1, :] = jnp.sum(products[:HD], 0, keepdims=True)
        center_ref[p, 1:2, :] = jnp.sum(products[HD:], 0, keepdims=True)
    left = lax.broadcasted_iota(jnp.int32, (KEY_TILE, PAIR), 1) < HD

    def step(j, nothing):
        place = pl.ds(pl.multiple_of(j * KEY_TILE, KEY_TILE), KEY_TILE)
        sumk_ref[...] = jnp.zeros_like(sumk_ref)
        sumv_ref[...] = jnp.zeros_like(sumv_ref)
        def rows(tile, nothing):
            here = pl.ds(pl.multiple_of(tile * QUERY_TILE, QUERY_TILE), QUERY_TILE)
            last = (halo + (tile + 1) * QUERY_TILE) // KEY_TILE

            @pl.when((j >= low_ref[seq * tiles + tile]) & (j < last))
            def _():
                ok = visible(j * KEY_TILE, start_ref[0, :, here], halo + tile * QUERY_TILE)
                keys = [two_heads(keyvalue_ref[0, place, c]) for c in cols]
                queries = [query_ref[0, here, c] * 0.125 for c in cols]
                grads = [grad_ref[0, here, c] for c in cols]
                scores = [dot(k, q, NT) for k, q in zip(keys, queries)]
                gprobs = [
                    dot(two_heads(keyvalue_ref[0, place, after(c)]), g, NT) for c, g in zip(cols, grads)
                ]
                for p in range(pairs):
                    probs, gscores = [], []
                    for head in range(2):
                        part = slice(head * KEY_TILE, (head + 1) * KEY_TILE)
                        row = slice(head, head + 1)
                        prob = jnp.exp(
                            jnp.where(ok, scores[p][part] - log_ref[0, p, row, here], -1e30)
                        )
                        gscore = prob * (gprobs[p][part] - center_ref[p, row, here])
                        probs.append(prob.astype(BF16))
                        gscores.append(gscore.astype(BF16))
                    probs = jnp.concatenate(probs, 0)
                    gscores = jnp.concatenate(gscores, 0)
                    sumv_ref[p] += dot(probs, grads[p])
                    sumk_ref[p] += dot(gscores, queries[p])
                    turned_ref[p, :, here] += dot(keys[p], gscores, TN)

            return nothing

        lax.fori_loop(0, tiles, rows, 0)

        for p in range(pairs):
            gkeyvalue_ref[0, place, cols[p]] = jnp.where(
                left, sumk_ref[p, :KEY_TILE], sumk_ref[p, KEY_TILE:]
            ).astype(BF16)
            gkeyvalue_ref[0, place, after(cols[p])] = jnp.where(
                left, sumv_ref[p, :KEY_TILE], sumv_ref[p, KEY_TILE:]
            ).astype(BF16)
        return nothing

    lax.fori_loop(first_ref[seq], (halo + block) // KEY_TILE, step, 0)
    for p in range(pairs):
        gquery_ref[0, :, cols[p]] = (jnp.transpose(turned_ref[p]) * 0.125).astype(BF16)


def attend_back(low, first, query, keyvalues, starts, mixed, grad, logs):
    seqs, block, width = query.shape
    length = keyvalues.shape[1]
    pairs = width // PAIR
    rows = pl.BlockSpec((1, block, width), lambda s, low, first: (s, 0, 0))
    full = pl.BlockSpec((1, length, 2 * width), lambda s, low, first: (s, 0, 0))
    return pl.pallas_call(
        functools.partial(attend_back_kernel, length - block),
        grid_spec=pltpu.PrefetchScalarGridSpec(
            num_scalar_prefetch=2,
            grid=(seqs,),
            in_specs=[
                rows,
                full,
                pl.BlockSpec((1, 1, block), lambda s, low, first: (s, 0, 0)),
                rows,
                rows,
                pl.BlockSpec((1, pairs, 2, block), lambda s, low, first: (s, 0, 0, 0)),
            ],
            out_specs=[rows, full],
            scratch_shapes=[
                pltpu.VMEM((pairs, PAIR, block), F32),
                pltpu.VMEM((pairs, 8, block), F32),
                pltpu.VMEM((pairs, 2 * KEY_TILE, PAIR), F32),
                pltpu.VMEM((pairs, 2 * KEY_TILE, PAIR), F32),
            ],
        ),
        out_shape=[
            jax.ShapeDtypeStruct((seqs, block, width), BF16),
            jax.ShapeDtypeStruct((seqs, length, 2 * width), BF16),
        ],
        compiler_params=pltpu.CompilerParams(vmem_limit_bytes=VMEM_LIMIT),
        cost_estimate=pl.CostEstimate(
            flops=40 << 30, bytes_accessed=28 << 20, transcendentals=8 << 20
        ),
        name="attend_back",
    )(low, first, query, keyvalues, starts, mixed, grad, logs)


def slab_copies(slab_ref, merge_ref, up_ref, down_ref, sems):
    owners = slab_ref.shape[0]
    width = slab_ref.shape[2]
    rows = width // owners
    chunks = up_ref.shape[1] // width
    groups = [[], [], []]
    for owner in range(owners):
        here = pl.ds(owner * rows, rows)
        groups[0].append((slab_ref.at[owner, pl.ds(0, rows), :], merge_ref.at[here, :]))
        for c in range(chunks):
            groups[1].append(
                (
                    slab_ref.at[owner, pl.ds((1 + c) * rows, rows), :],
                    up_ref.at[here, pl.ds(c * width, width)],
                )
            )
        groups[2].append(
            (
                slab_ref.at[owner, pl.ds((1 + chunks) * rows, chunks * rows), :],
                down_ref.at[pl.ds(owner * chunks * rows, chunks * rows), :],
            )
        )
    return [
        [pltpu.make_async_copy(*pair, sems.at[k, n]) for n, pair in enumerate(group)]
        for k, group in enumerate(groups)
    ]


def mlp_kernel(
    factor_ref,
    mixed_ref,
    token_ref,
    teacher_ref,
    weight_ref,
    outbias_ref,
    gain_ref,
    shift_ref,
    upbias_ref,
    downbias_ref,
    slab_ref,
    layer_ref,
    gresid_ref,
    gmixed_ref,
    sums_ref,
    upsums_ref,
    gslab_ref,
    merge_ref,
    up_ref,
    down_ref,
    slope_ref,
    normed_ref,
    active_ref,
    ghidden_ref,
    gmlp_ref,
    gbranch_ref,
    split_ref,
    block_ref,
    sems,
    split_sems,
    block_sems,
):
    width = token_ref.shape[-1]
    hidden = up_ref.shape[1]
    step = pl.program_id(0)
    here = pl.ds(pl.multiple_of(step * MLP_TILE, MLP_TILE), MLP_TILE)
    copies = slab_copies(slab_ref, merge_ref, up_ref, down_ref, sems)

    def arrive(k):
        @pl.when(step == 0)
        def _():
            for copy in copies[k]:
                copy.wait()

    @pl.when(step == 0)
    def _():
        for group in copies:
            for copy in group:
                copy.start()
        sums_ref[...] = jnp.zeros_like(sums_ref)
        upsums_ref[...] = jnp.zeros_like(upsums_ref)

    arrive(0)
    resid = (
        token_ref[...].astype(F32) + dot(mixed_ref[here, :], merge_ref[...]) + outbias_ref[...]
    )
    unit, scale = norm_parts(resid)
    normed = (unit * gain_ref[...] + shift_ref[...]).astype(BF16)
    normed_ref[here, :] = normed
    arrive(1)
    cuts = [slice(c, c + MLP_CHUNK) for c in range(0, hidden, MLP_CHUNK)]
    result = resid + downbias_ref[...]
    for n, cols in enumerate(cuts):
        inner = dot(normed, up_ref[:, cols]) + upbias_ref[:, cols]
        square = inner * inner
        curve = jnp.tanh(0.7978845608028654 * (inner + 0.044715 * square * inner))
        half = 0.5 * (1.0 + curve)
        active = (half * inner).astype(BF16)
        active_ref[here, cols] = active
        slope_ref[:, cols] = half + 0.5 * inner * (1.0 - curve * curve) * (
            0.7978845608028654 * (1.0 + 3.0 * 0.044715 * square)
        )
        if n == 0:
            arrive(2)
        result += dot(active_ref[here, cols], down_ref[cols, :])
    layer_ref[...] = result.astype(BF16)
    error = result - teacher_ref[...].astype(F32)
    weight = weight_ref[...]
    sums_ref[4:5, :] += jnp.sum(weight * (error * error), 0, keepdims=True)
    gresult = error * (weight * factor_ref[0])
    gmlp = gresult.astype(BF16)
    gmlp_ref[here, :] = gmlp
    sums_ref[3:4, :] += jnp.sum(gmlp.astype(F32), 0, keepdims=True)
    gnormed = jnp.zeros_like(result)
    for cols in cuts:
        gactive = dot(gmlp, down_ref[cols, :], NT)
        ghidden = (gactive * slope_ref[:, cols]).astype(BF16)
        ghidden_ref[here, cols] = ghidden
        upsums_ref[0:1, cols] += jnp.sum(ghidden.astype(F32), 0, keepdims=True)
        gnormed += dot(ghidden_ref[here, cols], up_ref[:, cols], NT)
    sums_ref[1:2, :] += jnp.sum(gnormed * unit, 0, keepdims=True)
    sums_ref[2:3, :] += jnp.sum(gnormed, 0, keepdims=True)
    gresid = gresult + norm_back(gnormed, gain_ref[...], unit, scale)
    gresid_ref[...] = gresid
    gbranch = gresid.astype(BF16)
    gbranch_ref[here, :] = gbranch
    sums_ref[0:1, :] += jnp.sum(gbranch.astype(F32), 0, keepdims=True)
    gmixed_ref[...] = dot(gbranch, merge_ref[...], NT).astype(BF16)

    owners, rows, _ = split_ref.shape[1:]
    chunks = hidden // width
    share = owners // chunks

    def split_copy(index):
        return pltpu.make_async_copy(
            split_ref.at[index % 2],
            gslab_ref.at[:, pl.ds(pl.multiple_of(index * rows, 16), rows), :],
            split_sems.at[index % 2],
        )

    def block_copy(index):
        return pltpu.make_async_copy(
            block_ref.at[index % 2],
            gslab_ref.at[
                pl.ds(index * share, share), pl.ds((1 + chunks) * rows, chunks * rows), :
            ],
            block_sems.at[index % 2],
        )

    @pl.when(step == pl.num_programs(0) - 1)
    def _():
        out = dot(mixed_ref[...], gbranch_ref[...], TN).astype(BF16)
        split_ref[0] = out.reshape(owners, rows, width)
        split_copy(0).start()

        def ups(index, nothing):
            @pl.when(index >= 2)
            def _():
                split_copy(index - 2).wait()

            cols = pl.ds(pl.multiple_of((index - 1) * width, 128), width)
            out = dot(normed_ref[...], ghidden_ref[:, cols], TN).astype(BF16)
            split_ref[index % 2] = out.reshape(owners, rows, width)
            split_copy(index).start()
            return nothing

        lax.fori_loop(1, chunks + 1, ups, 0)

        def downs(index, nothing):
            @pl.when(index >= 2)
            def _():
                block_copy(index - 2).wait()

            cols = pl.ds(pl.multiple_of(index * width, 128), width)
            out = dot(active_ref[:, cols], gmlp_ref[...], TN).astype(BF16)
            block_ref[index % 2] = out.reshape(share, chunks * rows, width)
            block_copy(index).start()
            return nothing

        lax.fori_loop(0, chunks, downs, 0)
        split_copy(chunks - 1).wait()
        split_copy(chunks).wait()
        block_copy(chunks - 2).wait()
        block_copy(chunks - 1).wait()


def mlp(factor, mixed, tokens, teacher, weight, vectors, slab):
    rows, width = tokens.shape
    outbias, gain, shift, upbias, downbias = vectors
    hidden = upbias.shape[1]
    chunks = hidden // width
    owners = slab.shape[0]
    few = width // owners
    tile = lambda n: pl.BlockSpec((MLP_TILE, n), lambda i: (i, 0))
    fixed = lambda m, n: pl.BlockSpec((m, n), lambda i: (0, 0))
    anywhere = pl.BlockSpec(memory_space=pl.ANY)
    shape = jax.ShapeDtypeStruct
    return pl.pallas_call(
        mlp_kernel,
        grid=(rows // MLP_TILE,),
        in_specs=[
            pl.BlockSpec(memory_space=pltpu.SMEM),
            fixed(rows, width),
            tile(width),
            tile(width),
            tile(1),
            fixed(1, width),
            fixed(1, width),
            fixed(1, width),
            fixed(1, hidden),
            fixed(1, width),
            anywhere,
        ],
        out_specs=[
            tile(width),
            tile(width),
            tile(width),
            fixed(8, width),
            fixed(8, hidden),
            anywhere,
        ],
        out_shape=[
            shape((rows, width), BF16),
            shape((rows, width), F32),
            shape((rows, width), BF16),
            shape((8, width), F32),
            shape((8, hidden), F32),
            shape((owners, (1 + 2 * chunks) * few, width), BF16),
        ],
        scratch_shapes=[
            pltpu.VMEM((width, width), BF16),
            pltpu.VMEM((width, hidden), BF16),
            pltpu.VMEM((hidden, width), BF16),
            pltpu.VMEM((MLP_TILE, hidden), F32),
            pltpu.VMEM((rows, width), BF16),
            pltpu.VMEM((rows, hidden), BF16),
            pltpu.VMEM((rows, hidden), BF16),
            pltpu.VMEM((rows, width), BF16),
            pltpu.VMEM((rows, width), BF16),
            pltpu.VMEM((2, owners, few, width), BF16),
            pltpu.VMEM((2, owners // chunks, chunks * few, width), BF16),
            pltpu.SemaphoreType.DMA((3, owners * chunks)),
            pltpu.SemaphoreType.DMA((2,)),
            pltpu.SemaphoreType.DMA((2,)),
        ],
        compiler_params=pltpu.CompilerParams(vmem_limit_bytes=VMEM_LIMIT),
        cost_estimate=pl.CostEstimate(
            flops=6 * rows * width * (width + 2 * hidden),
            bytes_accessed=40 << 20,
            transcendentals=rows * hidden,
        ),
        name="mlp",
    )(factor, mixed, tokens, teacher, weight, outbias, gain, shift, upbias, downbias, slab)


def halo_back_kernel(
    low_ref,
    halo_any,
    grad_any,
    whole_any,
    out_any,
    sums_ref,
    halo_ref,
    grad_ref,
    out_ref,
    weight_ref,
    halo_sems,
    grad_sems,
    out_sems,
    sem,
):
    seqs, rows, width = halo_ref.shape
    tiles = rows // ROW_TILE
    weight = pltpu.make_async_copy(whole_any.at[:, pl.ds(width, 2 * width)], weight_ref, sem)
    weight.start()

    def arrive(seq, tile, at):
        return (
            pltpu.make_async_copy(
                halo_any.at[seq, at], halo_ref.at[seq, at], halo_sems.at[seq, tile]
            ),
            pltpu.make_async_copy(
                grad_any.at[seq, at], grad_ref.at[seq, at], grad_sems.at[seq, tile]
            ),
        )

    def leave(seq, tile, at):
        return pltpu.make_async_copy(
            out_ref.at[seq, at], out_any.at[seq, at], out_sems.at[seq, tile]
        )

    def begin(seq, tile, at):
        @pl.when(tile >= low_ref[seq])
        def _():
            for copy in arrive(seq, tile, at):
                copy.start()

        @pl.when(tile < low_ref[seq])
        def _():
            out_ref[seq, at, :] = jnp.zeros((ROW_TILE, width), BF16)
            leave(seq, tile, at).start()

    def work(seq, tile, at):
        for copy in arrive(seq, tile, at):
            copy.wait()
        grad = dot(grad_ref[seq, at, :], weight_ref[...], NT)
        unit, _ = norm_parts(halo_ref[seq, at, :].astype(F32))
        out_ref[seq, at, :] = grad.astype(BF16)
        leave(seq, tile, at).start()
        sums_ref[0:1, :] += jnp.sum(grad * unit, 0, keepdims=True)
        sums_ref[1:2, :] += jnp.sum(grad, 0, keepdims=True)

    def end(seq, tile, at):
        leave(seq, tile, at).wait()

    every_tile(low_ref, seqs, tiles, begin, every=True)
    sums_ref[...] = jnp.zeros_like(sums_ref)
    weight.wait()
    every_tile(low_ref, seqs, tiles, work)
    every_tile(low_ref, seqs, tiles, end, every=True)


def halo_back(low, halo, gkeyvalues, whole):
    seqs, rows, width = halo.shape
    tiles = rows // ROW_TILE
    anywhere = pl.BlockSpec(memory_space=pl.ANY)
    return pl.pallas_call(
        halo_back_kernel,
        grid_spec=pltpu.PrefetchScalarGridSpec(
            num_scalar_prefetch=1,
            grid=(1,),
            in_specs=[anywhere, anywhere, anywhere],
            out_specs=[anywhere, pl.BlockSpec((8, width), lambda i, low: (0, 0))],
            scratch_shapes=[
                pltpu.VMEM((seqs, rows, width), BF16),
                pltpu.VMEM((seqs, rows, 2 * width), BF16),
                pltpu.VMEM((seqs, rows, width), BF16),
                pltpu.VMEM((width, 2 * width), BF16),
                pltpu.SemaphoreType.DMA((seqs, tiles)),
                pltpu.SemaphoreType.DMA((seqs, tiles)),
                pltpu.SemaphoreType.DMA((seqs, tiles)),
                pltpu.SemaphoreType.DMA,
            ],
        ),
        out_shape=[
            jax.ShapeDtypeStruct((seqs, rows, width), BF16),
            jax.ShapeDtypeStruct((8, width), F32),
        ],
        compiler_params=pltpu.CompilerParams(vmem_limit_bytes=VMEM_LIMIT),
        cost_estimate=pl.CostEstimate(
            flops=4 << 30, bytes_accessed=16 << 20, transcendentals=0
        ),
        name="halo_back",
    )(low, halo, gkeyvalues, whole)


def own_back_kernel(
    low_ref,
    order_ref,
    own_any,
    normed_any,
    gquery_any,
    gkeyvalue_any,
    whole_any,
    gnormed_any,
    keep_any,
    give_any,
    sums_ref,
    own_ref,
    normed_ref,
    gquery_ref,
    gkeyvalue_ref,
    weight_ref,
    total_ref,
    gnormed_ref,
    gweight_ref,
    sems,
    out_sems,
):
    seqs, block, width = own_ref.shape
    halo = normed_ref.shape[1] - block
    tiles = halo // ROW_TILE
    here = pl.ds(halo, block)
    before = pl.ds(0, halo)
    first = [
        pltpu.make_async_copy(normed_any.at[:, here], normed_ref.at[:, here], sems.at[0]),
        pltpu.make_async_copy(gkeyvalue_any.at[:, here], gkeyvalue_ref.at[:, here], sems.at[1]),
        pltpu.make_async_copy(gquery_any, gquery_ref, sems.at[2]),
    ]
    later = [
        pltpu.make_async_copy(normed_any.at[:, before], normed_ref.at[:, before], sems.at[3]),
        pltpu.make_async_copy(gkeyvalue_any.at[:, before], gkeyvalue_ref.at[:, before], sems.at[4]),
    ]
    last = [
        pltpu.make_async_copy(whole_any, weight_ref, sems.at[5]),
        pltpu.make_async_copy(own_any, own_ref, sems.at[6]),
    ]
    for copy in first + later + last:
        copy.start()
    for copy in first:
        copy.wait()
    rows = seqs * block
    gweight_ref[:, :width] = dot(
        normed_ref[:, halo:, :].reshape(rows, width), gquery_ref[...].reshape(rows, width), TN
    ).astype(BF16)

    def whole(k, nothing):
        cols = pl.ds(pl.multiple_of(k * width, 128), width)
        total_ref[:, cols] = dot(
            normed_ref[:, halo:, :].reshape(rows, width),
            gkeyvalue_ref[:, halo:, cols].reshape(rows, width),
            TN,
        )
        return nothing

    lax.fori_loop(0, 2, whole, 0)
    sums_ref[...] = jnp.zeros_like(sums_ref)
    sums_ref[2:3, :] = jnp.sum(
        gquery_ref[...].reshape(rows, width).astype(F32), 0, keepdims=True
    )
    sums_ref[3:4, :] = jnp.sum(
        gkeyvalue_ref[:, halo:, width:].reshape(rows, width).astype(F32), 0, keepdims=True
    )
    for copy in later:
        copy.wait()

    def add(seq, tile, at):
        total_ref[...] += dot(normed_ref[seq, at, :], gkeyvalue_ref[seq, at, :], TN)
        sums_ref[3:4, :] += jnp.sum(gkeyvalue_ref[seq, at, width:].astype(F32), 0, keepdims=True)

    every_tile(low_ref, seqs, tiles, add)
    gweight_ref[:, width:] = total_ref[...].astype(BF16)
    slots = keep_any.shape[0]
    share = width // (2 * slots)
    sends = [
        pltpu.make_async_copy(
            gweight_ref.at[pl.ds(pl.multiple_of(order_ref[k] * share, 16), share), :],
            (keep_any, give_any)[k // slots].at[k % slots, pl.ds(0, share), :],
            out_sems.at[1 + k],
        )
        for k in range(2 * slots)
    ]
    for copy in sends:
        copy.start()
    for copy in last:
        copy.wait()

    def lead(seq, nothing):
        grad = dot(gquery_ref[seq], weight_ref[:, :width], NT)
        grad += dot(gkeyvalue_ref[seq, halo:, :], weight_ref[:, width:], NT)
        gnormed_ref[seq] = grad
        unit, _ = norm_parts(own_ref[seq].astype(F32))
        sums_ref[0:1, :] += jnp.sum(grad * unit, 0, keepdims=True)
        sums_ref[1:2, :] += jnp.sum(grad, 0, keepdims=True)
        return nothing

    lax.fori_loop(0, seqs, lead, 0)
    back = pltpu.make_async_copy(gnormed_ref, gnormed_any, out_sems.at[0])
    back.start()
    for copy in sends:
        copy.wait()
    back.wait()


def own_back(low, order, own, normed, gquery, gkeyvalues, whole):
    seqs, block, width = own.shape
    length = normed.shape[1]
    anywhere = pl.BlockSpec(memory_space=pl.ANY)
    return pl.pallas_call(
        own_back_kernel,
        grid_spec=pltpu.PrefetchScalarGridSpec(
            num_scalar_prefetch=2,
            grid=(1,),
            in_specs=[anywhere] * 5,
            out_specs=[
                anywhere,
                anywhere,
                anywhere,
                pl.BlockSpec((8, width), lambda i, low, order: (0, 0)),
            ],
            scratch_shapes=[
                pltpu.VMEM((seqs, block, width), BF16),
                pltpu.VMEM((seqs, length, width), BF16),
                pltpu.VMEM((seqs, block, width), BF16),
                pltpu.VMEM((seqs, length, 2 * width), BF16),
                pltpu.VMEM((width, 3 * width), BF16),
                pltpu.VMEM((width, 2 * width), F32),
                pltpu.VMEM((seqs, block, width), F32),
                pltpu.VMEM((width, 3 * width), BF16),
                pltpu.SemaphoreType.DMA((7,)),
                pltpu.SemaphoreType.DMA((1 + SHARES,)),
            ],
        ),
        out_shape=[
            jax.ShapeDtypeStruct((seqs, block, width), F32),
            jax.ShapeDtypeStruct((SHARES // 2, width // SHARES + SMALL_ROWS, 3 * width), BF16),
            jax.ShapeDtypeStruct((SHARES // 2, width // SHARES + SMALL_ROWS, 3 * width), BF16),
            jax.ShapeDtypeStruct((8, width), F32),
        ],
        compiler_params=pltpu.CompilerParams(vmem_limit_bytes=VMEM_LIMIT),
        cost_estimate=pl.CostEstimate(
            flops=16 << 30, bytes_accessed=24 << 20, transcendentals=0
        ),
        name="own_back",
    )(low, order, own, normed, gquery, gkeyvalues, whole)


def finish_kernel(own_ref, gnormed_ref, gresid_ref, gain_ref, *rest):
    more_refs, (out_ref, total_ref) = rest[:-2], rest[-2:]
    start = 0
    for more_ref in more_refs:
        end = start + more_ref.shape[1]
        total_ref[start:end, :] = gnormed_ref[0, start:end, :] + more_ref[0].astype(F32)
        start = end

    def one(t, nothing):
        at = pl.ds(pl.multiple_of(t * HALO_CHUNK, HALO_CHUNK), HALO_CHUNK)
        unit, scale = norm_parts(own_ref[0, at, :].astype(F32))
        out_ref[0, at, :] = (
            gresid_ref[0, at, :] + norm_back(total_ref[at, :], gain_ref[...], unit, scale)
        ).astype(BF16)
        return nothing

    lax.fori_loop(0, own_ref.shape[1] // HALO_CHUNK, one, 0)


def finish(own, gnormed, more, gresid, gain):
    seqs, block, width = own.shape
    whole = lambda rows: pl.BlockSpec((1, rows, width), lambda s: (s, 0, 0))
    tile = whole(block)
    return pl.pallas_call(
        finish_kernel,
        grid=(seqs,),
        in_specs=[tile, tile, tile, pl.BlockSpec((1, width), lambda s: (0, 0))]
        + [whole(part.shape[1]) for part in more],
        out_specs=tile,
        out_shape=jax.ShapeDtypeStruct(own.shape, BF16),
        scratch_shapes=[pltpu.VMEM((block, width), F32)],
        cost_estimate=pl.CostEstimate(
            flops=20 * seqs * block * width,
            bytes_accessed=14 * seqs * block * width,
            transcendentals=0,
        ),
        name="finish",
    )(own, gnormed, gresid, gain, *more)


def swap(x, axis, bit):
    size = lax.axis_size(axis)
    return lax.ppermute(x, axis, [(i, i ^ bit) for i in range(size)])


def shift(x, axis, step):
    size = lax.axis_size(axis)
    return lax.ppermute(
        x, axis, [(i, i + step) for i in range(size) if 0 <= i + step < size]
    )


def sum_over(x, axis):
    bit = 1
    while bit < lax.axis_size(axis):
        x = x + swap(x, axis, bit)
        bit *= 2
    return x


def max_over(x, axis):
    bit = 1
    while bit < lax.axis_size(axis):
        x = jnp.maximum(x, swap(x, axis, bit))
        bit *= 2
    return x


def gather_near(shard):
    size = lax.axis_size("fsdp")
    if size != 8:
        return [lax.all_gather(shard, "fsdp", axis=0, tiled=True)]
    return [shard] + [swap(shard, "fsdp", 2 * d) for d in range(1, size // 2)]


def gather_rest(near):
    if lax.axis_size("fsdp") != 8:
        return near
    return near + [swap(piece, "fsdp", 1) for piece in near]


def piece_order():
    size = lax.axis_size("fsdp")
    me = lax.axis_index("fsdp").astype(jnp.int32)
    if size != 8:
        return jnp.zeros((1,), jnp.int32)
    return jnp.stack(
        [me ^ (2 * d) for d in range(size // 2)] + [me ^ (2 * d) ^ 1 for d in range(size // 2)]
    )


def sum_seq(total):
    if lax.axis_size("seq") != 4:
        return lax.psum(total, "seq")
    return sum_seq_rest(sum_seq_second(sum_seq_first(total)))


def sum_seq_first(total):
    rows, columns = total.shape
    odd = lax.axis_index("seq") % 2
    halves = total.reshape(2, rows // 2, columns)
    pick = lambda k: lax.dynamic_index_in_dim(halves, k, 0, keepdims=False)
    return (pick(odd).astype(F32) + swap(pick(1 - odd), "seq", 1).astype(F32)).astype(BF16)


def sum_seq_second(half):
    return (half.astype(F32) + swap(half, "seq", 2).astype(F32)).astype(BF16)


def sum_seq_rest(half):
    odd = lax.axis_index("seq") % 2
    back = swap(half, "seq", 1)
    return jnp.where(
        odd == 0, jnp.concatenate([half, back], 0), jnp.concatenate([back, half], 0)
    )


def reduce_rows(keep, give, half, *first):
    other = swap(give, "fsdp", 1)
    staged = lax.axis_size("seq") == 4
    if staged:
        half = sum_seq_first(half)
    mine = [
        (keep[d].astype(F32) + other[d].astype(F32)).astype(BF16) for d in range(keep.shape[0])
    ]
    arrived = [swap(part, "fsdp", 2 * d) for d, part in enumerate(mine) if d > 0]
    arrived, half, *first = lax.optimization_barrier((arrived, half, *first))
    total = mine[0].astype(F32)
    for part in arrived:
        total = total + part.astype(F32)
    total = total.astype(BF16)
    if not staged:
        return lax.psum(total, "seq"), half, *first
    total, half = sum_seq_first(total), sum_seq_second(half)
    total, half = lax.optimization_barrier((total, half))
    return sum_seq_rest(sum_seq_second(total)), sum_seq_rest(half), *first


def gather_slab(outweight, fcweight, projweight, *first):
    width = outweight.shape[1]
    cuts = fcweight.shape[1] // width

    def join(out, up, down, axis):
        ups = [lax.slice_in_dim(up, c * width, (c + 1) * width, axis=-1) for c in range(cuts)]
        return jnp.concatenate([out, *ups, down], axis)

    if lax.axis_size("fsdp") == SHARES:
        slab = join(outweight, fcweight, projweight, 0)
        slab, *first = lax.optimization_barrier((slab, *first))
        return lax.all_gather(slab, "fsdp", axis=0, tiled=False), *first
    whole = [
        lax.all_gather(w, "fsdp", axis=0, tiled=True) for w in (outweight, fcweight, projweight)
    ]
    return join(*(w.reshape(SHARES, -1, w.shape[1]) for w in whole), 1), *first


def reduce_slab(slab, width, hidden):
    owners = lax.axis_size("fsdp")
    cuts = hidden // width
    rows = width // SHARES

    def part(array, axis):
        at = lambda a, b: lax.slice_in_dim(array, a * rows, b * rows, axis=axis)
        ups = [at(1 + c, 2 + c) for c in range(cuts)]
        return at(0, 1), jnp.concatenate(ups, -1), at(1 + cuts, 1 + 2 * cuts)

    if owners == SHARES:
        return [g.astype(F32) for g in part(slab, 0)]
    return [
        lax.psum(
            lax.psum_scatter(
                g.reshape(-1, g.shape[-1]), "fsdp", scatter_dimension=0, tiled=True
            ),
            "seq",
        ).astype(F32)
        for g in part(slab, 1)
    ]


def local(
    tokens,
    teacher,
    segment_ids,
    latent_flags,
    valid_mask,
    attngain,
    attnshift,
    qkvweight,
    qvbias,
    outweight,
    outbias,
    mlpgain,
    mlpshift,
    fcweight,
    fcbias,
    projweight,
    projbias,
):
    seqs, block, width = tokens.shape
    groups = lax.axis_size("seq")
    owners = lax.axis_size("fsdp")
    rows = seqs * block
    halo_rows = (groups - 1) * block
    far_rows = halo_rows - block
    me = lax.axis_index("fsdp")
    place = lax.axis_index("seq").astype(jnp.int32)
    hidden = fcweight.shape[1]

    order = piece_order()
    qkv_pieces = gather_near(qkvweight)

    weight = (valid_mask * (1 - latent_flags)).astype(F32)
    below = jnp.sum(
        (segment_ids[:, :, None] < jnp.arange(1, 4, dtype=jnp.int32)).astype(jnp.int32), 1
    )
    facts = jnp.concatenate([below.reshape(-1), jnp.sum(weight).astype(jnp.int32)[None]])

    shards = [attngain, attnshift, qvbias, outbias, mlpgain, mlpshift, fcbias, projbias]
    sent = [tokens[k] for k in range(seqs)] + [tokens[:, block - HALO_CHUNK :]]
    bit = 1
    while bit < groups:
        facts = facts + swap(facts, "seq", bit)
        if bit == 1:
            facts, shards = lax.optimization_barrier((facts, shards))
        bit *= 2

    sent, facts = lax.optimization_barrier((sent, facts))
    near = [shift(sent[k], "seq", 1) for k in range(seqs)]
    far = shift(sent[seqs], "seq", 2) if far_rows > 0 else None
    bounds = facts[:-1].reshape(seqs, 3)

    def start_of(positions):
        found = jnp.zeros((seqs,) + positions.shape, jnp.int32)
        for d in range(3):
            bound = bounds[:, d].reshape((seqs,) + (1,) * positions.ndim)
            found = jnp.maximum(found, jnp.where(bound <= positions[None], bound, 0))
        return found

    firsts = jnp.arange(groups, dtype=jnp.int32) * block
    reach = jnp.max(firsts[None] - start_of(firsts)) - block
    chunks = jnp.maximum(reach + HALO_CHUNK - 1, 0) // HALO_CHUNK

    facts = jnp.stack([facts[-1], chunks])
    bit = 1
    while bit < owners:
        other = swap(facts, "fsdp", bit)
        facts = jnp.where(jnp.arange(2) == 1, jnp.maximum(facts, other), facts + other)
        bit *= 2

    packed = jnp.concatenate(
        [jnp.pad(v[None], ((0, 0), (0, -v.shape[0] % 128))) for v in shards], 1
    )
    table = jnp.where(
        lax.broadcasted_iota(jnp.int32, (owners, packed.shape[1]), 0) == me,
        packed,
        jnp.zeros((), BF16),
    )
    table = sum_over(table, "fsdp")

    qkv_pieces, near[0] = lax.optimization_barrier((qkv_pieces, near[0]))
    qkv_pieces = gather_rest(qkv_pieces)
    slab, qkv_pieces, table, facts, near[0] = gather_slab(
        outweight, fcweight, projweight, qkv_pieces, table, facts, near[0]
    )
    count = facts[0].astype(F32)
    chunks = facts[1]

    vectors = []
    at = 0
    for shard in shards:
        size = shard.shape[0]
        vectors.append(table[:, at : at + size].reshape(1, size * owners).astype(F32))
        at += size + -size % 128
    vectors, held = lax.optimization_barrier((vectors, order))
    gain1, shift1, bias1, outbias_v, gain2, shift2, upbias, downbias = vectors


    base = (place - (groups - 1)) * block
    starts = start_of(place * block + jnp.arange(block, dtype=jnp.int32)) - base
    low_rows = starts[:, ::QUERY_TILE]
    low = (low_rows // KEY_TILE).reshape(-1)
    low_tile = starts[:, 0] // ROW_TILE
    first = low_tile * (ROW_TILE // KEY_TILE)
    starts = starts[:, None, :]

    bias1 = jnp.concatenate([bias1[:, :width], jnp.zeros((1, width), F32), bias1[:, width:]], 1)
    normed, query, keyvalues, qkv = project_own(
        held, tokens, gain1, shift1, bias1, qkv_pieces, halo_rows + block
    )
    halo = jnp.zeros((seqs, halo_rows, width), BF16)
    for k in range(seqs):
        if k == seqs - 1:
            halo, near[k], query = lax.optimization_barrier((halo, near[k], query))
        halo = lax.dynamic_update_slice(halo, near[k][None], (k, far_rows, 0))
    if far_rows > 0:
        halo = lax.dynamic_update_slice(halo, far, (0, far_rows - HALO_CHUNK, 0))

    def fetch(state):
        j, halo = state
        sent = lax.dynamic_slice_in_dim(halo, halo_rows - HALO_CHUNK * (j + 1), HALO_CHUNK, 1)
        came = shift(sent, "seq", 1)
        return j + 1, lax.dynamic_update_slice_in_dim(
            halo, came, far_rows - HALO_CHUNK * (j + 1), 1
        )

    if far_rows > 0:
        _, halo = lax.while_loop(lambda state: state[0] < chunks, fetch, (jnp.int32(1), halo))

    normed, keyvalues = project_halo(
        low_tile, halo, gain1, shift1, bias1, qkv, normed, keyvalues
    )
    mixed, logs = attend(low, query, keyvalues, starts)

    factor = (rows * owners * groups) / count
    layer_out, gresid, gmixed, sums, upsums, outer = mlp(
        factor.reshape(1),
        mixed.reshape(rows, width),
        tokens.reshape(rows, width),
        teacher.reshape(rows, width),
        weight.reshape(rows, 1),
        (outbias_v, gain2, shift2, upbias, downbias),
        slab,
    )

    small = jnp.concatenate(
        [upsums[0].reshape(SHARES, -1)] + [sums[k].reshape(SHARES, -1) for k in range(4)], 1
    )
    outer, gmixed = lax.optimization_barrier((outer, gmixed))
    staged = owners == SHARES and groups == 4
    if owners == SHARES:
        outer = lax.psum_scatter(outer, "fsdp", scatter_dimension=0, tiled=False)
        outer = outer if staged else sum_seq(outer)

    gquery, gkeyvalues = attend_back(
        low, first, query, keyvalues, starts, mixed, gmixed.reshape(seqs, block, width), logs
    )
    ghalo, halo_sums = halo_back(low_tile, halo, gkeyvalues, qkv)

    def give(state):
        j, ghalo = state
        j = j - 1
        sent = lax.dynamic_slice_in_dim(ghalo, far_rows - HALO_CHUNK * (j + 1), HALO_CHUNK, 1)
        came = shift(sent, "seq", -1)
        spot = halo_rows - HALO_CHUNK * (j + 1)
        held = lax.dynamic_slice_in_dim(ghalo, spot, HALO_CHUNK, 1)
        total = (held.astype(F32) + came.astype(F32)).astype(BF16)
        return j, lax.dynamic_update_slice_in_dim(ghalo, total, spot, 1)

    if far_rows > 0:
        _, ghalo = lax.while_loop(lambda state: state[0] > 1, give, (chunks, ghalo))

    ghalo, gquery = lax.optimization_barrier((ghalo, gquery))
    ends = far_rows + block - HALO_CHUNK
    cut = far_rows + (block - HALO_CHUNK) // 2
    closing = ghalo[:, ends:]
    came = shift(ghalo[:, far_rows - HALO_CHUNK : far_rows], "seq", -1) if far_rows > 0 else closing
    near = [shift(ghalo[:, far_rows:cut], "seq", -1), shift(ghalo[:, cut:ends], "seq", -1)]
    sort = order if owners == SHARES else jnp.arange(SHARES, dtype=jnp.int32)
    gnormed, keep, give, own_sums = own_back(
        low_tile, sort, tokens, normed, gquery, gkeyvalues, qkv
    )
    keep, give, own_sums, halo_sums, near[0], came = lax.optimization_barrier(
        (keep, give, own_sums, halo_sums, near[0], came)
    )
    if far_rows > 0:
        closing = (closing.astype(F32) + came.astype(F32)).astype(BF16)
    near.append(shift(closing, "seq", -1))
    late = jnp.concatenate(
        [(own_sums[k] + halo_sums[k]).reshape(SHARES, -1) for k in range(2)]
        + [own_sums[2:4].reshape(SHARES, -1)],
        1,
    ).astype(BF16)
    late = jnp.pad(late, ((0, 0), (0, width - late.shape[1])))
    loss_row = jnp.broadcast_to(sums[4:5].astype(BF16), (SHARES, width))
    late = jnp.concatenate([late, small.astype(BF16), loss_row], 1)
    slots = SHARES // 2
    late = jnp.stack([lax.dynamic_index_in_dim(late, sort[k], 0) for k in range(SHARES)])
    late = jnp.pad(late, ((0, 0), (0, SMALL_ROWS - 1), (0, 0)))
    share = width // SHARES
    keep = lax.dynamic_update_slice_in_dim(keep, late[:slots], share, 1)
    give = lax.dynamic_update_slice_in_dim(give, late[slots:], share, 1)

    grad_tokens = finish(
        tokens,
        gnormed,
        near,
        gresid.reshape(tokens.shape),
        gain1,
    )

    if owners == SHARES:
        joint, outer, grad_tokens = reduce_rows(keep, give, outer, grad_tokens)
    else:
        joint = jnp.concatenate([keep, give])
        small_late = lax.psum(joint[:, share].astype(F32), ("fsdp", "seq"))
        joint = joint[:, :share].reshape(width, 3 * width)
        joint = lax.psum_scatter(joint, "fsdp", scatter_dimension=0, tiled=True)
        joint = lax.psum(joint, "seq")
    grad_merge, grad_up, grad_down = reduce_slab(outer, width, hidden)

    share = width // owners
    at = hidden // SHARES
    wide = width // SHARES
    spots = [(0, wide), (wide, wide), (2 * wide, 2 * wide), (width, at)]
    spots += [(width + at + k * wide, wide) for k in range(4)]
    if owners == SHARES:
        tail = joint[share].astype(F32)
        cuts = [tail[start : start + size] for start, size in spots]
        loss_row = tail[2 * width :]
    else:
        full = [small_late[:, start : start + size].reshape(-1) for start, size in spots]
        cuts = [
            lax.dynamic_slice_in_dim(v, me * (v.shape[0] // owners), v.shape[0] // owners)
            for v in full
        ]
        loss_row = small_late[0, 2 * width :]
    loss = jnp.sum(loss_row) / (width * count)
    return (
        loss,
        layer_out.reshape(tokens.shape),
        grad_tokens,
        cuts[0],
        cuts[1],
        joint[:share].astype(F32),
        cuts[2],
        grad_merge,
        cuts[4],
        cuts[5],
        cuts[6],
        grad_up,
        cuts[3],
        grad_down,
        cuts[7],
    )


def solution(mesh):
    placed = (
        P("fsdp", "seq", None),
        P("fsdp", "seq", None),
        P("fsdp", "seq"),
        P("fsdp", "seq"),
        P("fsdp", "seq"),
        P("fsdp"),
        P("fsdp"),
        P("fsdp", None),
        P("fsdp"),
        P("fsdp", None),
        P("fsdp"),
        P("fsdp"),
        P("fsdp"),
        P("fsdp", None),
        P("fsdp"),
        P("fsdp", None),
        P("fsdp"),
    )
    return jax.shard_map(
        local,
        mesh=mesh,
        in_specs=placed,
        out_specs=(
            P(),
            P("fsdp", "seq", None),
            P("fsdp", "seq", None),
            P("fsdp"),
            P("fsdp"),
            P("fsdp", None),
            P("fsdp"),
            P("fsdp", None),
            P("fsdp"),
            P("fsdp"),
            P("fsdp"),
            P("fsdp", None),
            P("fsdp"),
            P("fsdp", None),
            P("fsdp"),
        ),
        check_vma=False,
    )
```
